32 devices in a mesh: grp: 2 (over x), res: 16 (over z, y, core).
Axes of the slice: x: 2, y: 2, z: 4, core: 2. Of those that a mesh axis runs over, the one named last changes fastest.
Arguments:
- alignment_embedding: bfloat16 [256, 128, 256], P('grp', 'res'), parts along dimension 0, may hold values from -6 to 6
- coupling_embedding: bfloat16 [128, 256, 128], P('res', 'grp'), parts along dimension 1, may hold values from -6 to 6
- query_key_matrix: bfloat16 [256, 1024], replicated, may hold values from -0.375 to 0.375
- coupling_logit_matrix: bfloat16 [128, 8], replicated, may hold values from -8 to 8
- focus_final_matrix: bfloat16 [256, 256], replicated, may hold values from -3 to 3
- tensor_average_matrix: bfloat16 [256, 64], replicated, may hold values from -0.375 to 0.375
- tensor_average_final: bfloat16 [1024, 128], replicated, may hold values from -2 to 2
- trilateral_entry_matrix: bfloat16 [2, 128, 640], replicated, may hold values from -0.5 to 0.5
- trilateral_exit_matrix: bfloat16 [2, 128, 128], replicated, may hold values from -0.5 to 0.5
Outputs:
- alignment_mixed: bfloat16 [256, 128, 256], P('grp', 'res'), parts along dimension 0
- coupling_refreshed: bfloat16 [128, 256, 128], P('res', 'grp'), parts along dimension 1
The draws below stay inside these ranges and needn't reach their ends.
There are 2 independent parts, one for each index of `grp`. The reference program is written for one: setup_inputs(seed, part) draws one part's arguments, and reference() takes and returns one part's arrays. A program takes and returns all parts, laid end to end along the dimension named above; an argument that names none is the same for every part. Nothing has to cross between parts.
All inputs are finite; a program needn't handle non-finite values.
Results may differ from the reference program's by a relative error of at most 0.018.
The reference program's roundings to bfloat16 on the way count: a program that leaves them out, or rounds other values in their place, can miss the bound.
Values may be sent and summed in bfloat16 or wider, within the bound.
No kernel may reach another device: no remote copies, remote signals or barrier semaphores. Data moves between devices by JAX's collectives and lax.ppermute only.
A program may use at most 128 MiB of HBM per device.

```python
import math
import jax
import jax.numpy as jnp
from jax import lax

ALIGN_DEPTH = 256
COUPLING_DEPTH = 128
FOCUS_GROUPS = 8
SUBSPACE_WIDTH = 32
TENSOR_DEPTH = 32
ALIGNED_CHAINS = 128
AMINO_ACIDS = 128


def draw_coupling_embedding(key, part):
    return jnp.clip(jax.random.normal(key, (AMINO_ACIDS, AMINO_ACIDS, COUPLING_DEPTH), jnp.float32), -6.0, 6.0).astype(jnp.bfloat16)


def draw_coupling_logit_matrix(key, part):
    return jnp.clip(jax.random.normal(key, (COUPLING_DEPTH, FOCUS_GROUPS), jnp.float32) * (2.0 / math.sqrt(COUPLING_DEPTH)), -8.0, 8.0).astype(jnp.bfloat16)


def shard_levels(key, shape, cuts, low, largest):
    def one(position, shards_of):
        draws = jax.random.uniform(jax.random.fold_in(jax.random.fold_in(key, 6), position), (shards_of,), jnp.float32, low / len(cuts), largest / len(cuts))
        return jnp.repeat(jnp.exp(draws), shape[position] // shards_of).reshape((-1,) + (1,) * (len(shape) - position - 1))

    gain = one(*cuts[0])
    for cut in cuts[1:]:
        gain = gain * one(*cut)
    return gain


def normal_values(stream_key, extent, width, bound, cuts=(), held_as=jnp.bfloat16):
    factor_of = shard_levels(stream_key, extent, cuts, -0.22, 0.18) if cuts else 1.0
    drawn = jax.random.normal(stream_key, extent, jnp.float32) * width * factor_of
    return jnp.minimum(jnp.maximum(drawn, -bound), bound).astype(held_as)


def setup_inputs(seed: int = 0, part: int = 0) -> dict:
    keys = jax.random.split(jax.random.key(seed), 10)
    part_splits = jax.random.split(jax.random.fold_in(keys[9], part), 10)
    alignment_embedding = normal_values(part_splits[0], (ALIGNED_CHAINS, AMINO_ACIDS, ALIGN_DEPTH), 1.0, 6.0, ((1, 16),))
    coupling_embedding = draw_coupling_embedding(jax.random.fold_in(jax.random.fold_in(keys[9], part), 71), part)
    query_key_matrix = normal_values(keys[2], (ALIGN_DEPTH, 4 * FOCUS_GROUPS * SUBSPACE_WIDTH), ALIGN_DEPTH ** -0.5, 0.375)
    coupling_logit_matrix = draw_coupling_logit_matrix(jax.random.fold_in(keys[9], 71), part)
    focus_final_matrix = normal_values(keys[4], (FOCUS_GROUPS * SUBSPACE_WIDTH, ALIGN_DEPTH), (max(1, FOCUS_GROUPS * SUBSPACE_WIDTH // 64)) ** -0.5, 3.0)
    tensor_average_matrix = normal_values(keys[5], (ALIGN_DEPTH, 2 * TENSOR_DEPTH), ALIGN_DEPTH ** -0.5, 0.375)
    tensor_average_final = normal_values(keys[6], (TENSOR_DEPTH * TENSOR_DEPTH, COUPLING_DEPTH), (max(1, TENSOR_DEPTH * TENSOR_DEPTH // ALIGNED_CHAINS)) ** -0.5, 2.0)
    trilateral_entry_matrix = normal_values(keys[7], (2, COUPLING_DEPTH, 5 * COUPLING_DEPTH), COUPLING_DEPTH ** -0.5, 0.5)
    trilateral_exit_matrix = normal_values(keys[8], (2, COUPLING_DEPTH, COUPLING_DEPTH), COUPLING_DEPTH ** -0.5, 0.5)
    return dict(alignment_embedding=alignment_embedding, coupling_embedding=coupling_embedding, query_key_matrix=query_key_matrix, coupling_logit_matrix=coupling_logit_matrix, focus_final_matrix=focus_final_matrix, tensor_average_matrix=tensor_average_matrix, tensor_average_final=tensor_average_final, trilateral_entry_matrix=trilateral_entry_matrix, trilateral_exit_matrix=trilateral_exit_matrix)


def standardise_entries(values_in, axis_num):
    values_in = values_in.astype(jnp.float32)
    centred = values_in - lax.optimization_barrier(jnp.mean(values_in, axis=axis_num, keepdims=True))
    spread = lax.optimization_barrier(jnp.mean(centred * centred, axis=axis_num, keepdims=True))
    return centred * lax.rsqrt(spread + 1e-05)

def normalise_scores(scores):
    row_max = lax.optimization_barrier(jnp.max(scores, axis=-1, keepdims=True))
    weights = jnp.exp(scores - row_max)
    return (weights / lax.optimization_barrier(jnp.sum(weights, axis=-1, keepdims=True))).astype(jnp.bfloat16)

def triangle(pair_prev, weight_in, weight_out, contraction):
    normed = standardise_entries(pair_prev, -1).astype(jnp.bfloat16)
    mapped_strands = jnp.dot(normed.reshape(AMINO_ACIDS * AMINO_ACIDS, COUPLING_DEPTH), weight_in, preferred_element_type=jnp.float32).reshape(AMINO_ACIDS, AMINO_ACIDS, 5, COUPLING_DEPTH)
    left_edge = (jax.nn.sigmoid(mapped_strands[:, :, 0]) * mapped_strands[:, :, 1]).astype(jnp.bfloat16)
    right_edge = (jax.nn.sigmoid(mapped_strands[:, :, 2]) * mapped_strands[:, :, 3]).astype(jnp.bfloat16)
    gate_pair = jax.nn.sigmoid(mapped_strands[:, :, 4])
    edge_sums = jnp.einsum(contraction, left_edge.astype(jnp.float32), right_edge.astype(jnp.float32)).astype(jnp.bfloat16)
    edge_norm = standardise_entries(edge_sums, -1).astype(jnp.bfloat16)
    update = jnp.dot(edge_norm.reshape(AMINO_ACIDS * AMINO_ACIDS, COUPLING_DEPTH), weight_out, preferred_element_type=jnp.float32).reshape(AMINO_ACIDS, AMINO_ACIDS, COUPLING_DEPTH)
    return (pair_prev.astype(jnp.float32) + gate_pair * update).astype(jnp.bfloat16)

def reference(alignment_embedding, coupling_embedding, query_key_matrix, coupling_logit_matrix, focus_final_matrix, tensor_average_matrix, tensor_average_final, trilateral_entry_matrix, trilateral_exit_matrix):
    alignment_standardised = standardise_entries(alignment_embedding, -1).astype(jnp.bfloat16)
    mapped_strands = jnp.dot(alignment_standardised.reshape(ALIGNED_CHAINS * AMINO_ACIDS, ALIGN_DEPTH), query_key_matrix, preferred_element_type=jnp.float32).reshape(ALIGNED_CHAINS, AMINO_ACIDS, 4, FOCUS_GROUPS, SUBSPACE_WIDTH)
    queries = mapped_strands[:, :, 0].astype(jnp.bfloat16)
    key_rows = mapped_strands[:, :, 1].astype(jnp.bfloat16)
    value_rows = mapped_strands[:, :, 2].astype(jnp.bfloat16)
    alignment_sigmoid_factors = jax.nn.sigmoid(mapped_strands[:, :, 3])
    pair_norm = standardise_entries(coupling_embedding, -1).astype(jnp.bfloat16)
    bias_terms = jnp.dot(pair_norm.reshape(AMINO_ACIDS * AMINO_ACIDS, COUPLING_DEPTH), coupling_logit_matrix, preferred_element_type=jnp.float32).reshape(AMINO_ACIDS, AMINO_ACIDS, FOCUS_GROUPS)
    bias_heads = jnp.transpose(bias_terms, (2, 0, 1))
    score_scale = SUBSPACE_WIDTH ** (-0.5)

    def one_sequence(operands):
        seq_query, seq_key, seq_value = operands
        scores = jnp.einsum('ihd,jhd->hij', seq_query.astype(jnp.float32), seq_key.astype(jnp.float32)) * score_scale + bias_heads
        weights = normalise_scores(scores)
        return jnp.einsum('hij,jhd->ihd', weights.astype(jnp.float32), seq_value.astype(jnp.float32)).astype(jnp.bfloat16)
    mixed_signals = lax.map(one_sequence, (queries, key_rows, value_rows))
    sigmoid_scaled_result = (mixed_signals.astype(jnp.float32) * alignment_sigmoid_factors).astype(jnp.bfloat16)
    alignment_increment = jnp.dot(sigmoid_scaled_result.reshape(ALIGNED_CHAINS * AMINO_ACIDS, FOCUS_GROUPS * SUBSPACE_WIDTH), focus_final_matrix, preferred_element_type=jnp.float32).reshape(ALIGNED_CHAINS, AMINO_ACIDS, ALIGN_DEPTH)
    alignment_mixed = (alignment_embedding.astype(jnp.float32) + alignment_increment).astype(jnp.bfloat16)
    tensor_average_scaled = standardise_entries(alignment_mixed, -1).astype(jnp.bfloat16)
    flank_mapping = jnp.dot(tensor_average_scaled.reshape(ALIGNED_CHAINS * AMINO_ACIDS, ALIGN_DEPTH), tensor_average_matrix, preferred_element_type=jnp.float32).reshape(ALIGNED_CHAINS, AMINO_ACIDS, 2, TENSOR_DEPTH).astype(jnp.bfloat16)
    left_side = flank_mapping[:, :, 0]
    target_real_entries = flank_mapping[:, :, 1].astype(jnp.float32)

    def one_row(source_embedding_line):
        tensor_accumulated = jnp.einsum('ig,irb->rgb', source_embedding_line.astype(jnp.float32), target_real_entries) * (1.0 / ALIGNED_CHAINS)
        tensor_accumulated = tensor_accumulated.astype(jnp.bfloat16).reshape(AMINO_ACIDS, TENSOR_DEPTH * TENSOR_DEPTH)
        return jnp.dot(tensor_accumulated, tensor_average_final, preferred_element_type=jnp.float32)
    opm_update = lax.map(one_row, jnp.transpose(left_side, (1, 0, 2)))
    pair_mid = (coupling_embedding.astype(jnp.float32) + opm_update).astype(jnp.bfloat16)
    pair_tri = triangle(pair_mid, trilateral_entry_matrix[0], trilateral_exit_matrix[0], 'ikc,jkc->ijc')
    coupling_refreshed = triangle(pair_tri, trilateral_entry_matrix[1], trilateral_exit_matrix[1], 'kic,kjc->ijc')
    return (alignment_mixed, coupling_refreshed)
```

```python
import jax
import jax.numpy as jnp
from jax import lax
from jax.sharding import PartitionSpec as P


def standardise_entries(values_in, axis_num):
    values_in = values_in.astype(jnp.float32)
    centred = values_in - jnp.mean(values_in, axis=axis_num, keepdims=True)
    spread = jnp.mean(centred * centred, axis=axis_num, keepdims=True)
    return centred * lax.rsqrt(spread + 1e-05)


def exchange(blocks):
    return lax.all_to_all(blocks, "res", split_axis=0, concat_axis=0, tiled=True)


def with_partner(values):
    count = lax.axis_size("res")
    return lax.ppermute(values, "res", [(k, k ^ 1) for k in range(count)])


def triangle(pair_prev, weight_in, weight_out, contraction):
    local_strands, total_res, pair_width = pair_prev.shape
    count = lax.axis_size("res")
    share = pair_width // count
    normed = standardise_entries(pair_prev, -1).astype(jnp.bfloat16)
    five = weight_in.reshape(pair_width, 5, pair_width)
    paired = five[:, :4].reshape(pair_width, 2, 2, count, share).transpose(0, 2, 3, 1, 4)
    mapped = jnp.einsum(
        "rnc,ctwsk->twskrn", normed, paired, preferred_element_type=jnp.float32
    )
    edges = (jax.nn.sigmoid(mapped[0]) * mapped[1]).astype(jnp.bfloat16)
    arrived = exchange(edges)
    gate_pair = jax.nn.sigmoid(
        jnp.einsum("rnc,cf->rnf", normed, five[:, 4], preferred_element_type=jnp.float32)
    )
    product = jnp.einsum(
        contraction, arrived[:, 0], arrived[:, 1], preferred_element_type=jnp.float32
    ).astype(jnp.bfloat16)
    product = product.reshape(share, count, local_strands, total_res).transpose(1, 0, 2, 3)
    gathered = exchange(product).reshape(pair_width, local_strands, total_res)
    edge_norm = standardise_entries(gathered, 0).astype(jnp.bfloat16)
    update = jnp.einsum("crn,cf->rnf", edge_norm, weight_out, preferred_element_type=jnp.float32)
    return (pair_prev.astype(jnp.float32) + gate_pair * update).astype(jnp.bfloat16)


def body(
    alignment_embedding,
    coupling_embedding,
    query_key_matrix,
    coupling_logit_matrix,
    focus_final_matrix,
    tensor_average_matrix,
    tensor_average_final,
    trilateral_entry_matrix,
    trilateral_exit_matrix,
):
    chain_tally, local_strands, depth = alignment_embedding.shape
    total_res, pair_width = coupling_embedding.shape[1:]
    count = lax.axis_size("res")
    core = lax.axis_index("res") % 2
    heads = coupling_logit_matrix.shape[1]
    width = query_key_matrix.shape[1] // (4 * heads)
    per_device = chain_tally // count
    tensor_depth = tensor_average_matrix.shape[1] // 2
    half = total_res // 2

    rows = exchange(alignment_embedding).reshape(count, per_device, local_strands, depth)
    rows = rows.transpose(1, 0, 2, 3).reshape(per_device, total_res, depth)

    pair_norm = standardise_entries(coupling_embedding, -1).astype(jnp.bfloat16)
    bias_rows = jnp.einsum(
        "rnc,ch->hrn", pair_norm, coupling_logit_matrix, preferred_element_type=jnp.float32
    )
    upper = lax.reduce_precision(bias_rows, 8, 7)
    terms = jnp.stack([upper, bias_rows - upper]).astype(jnp.bfloat16)
    term = exchange(jnp.tile(terms, (count // 2, 1, 1, 1)))
    bias = term.astype(jnp.float32) + with_partner(term).astype(jnp.float32)
    bias = bias.transpose(1, 0, 2, 3).reshape(heads, total_res, total_res)

    standard = standardise_entries(rows, -1).astype(jnp.bfloat16)
    projection = query_key_matrix.reshape(depth, 4, heads, width)
    mapped = jnp.einsum(
        "snc,cthd->tshnd", standard, projection[:, :3], preferred_element_type=jnp.float32
    ).astype(jnp.bfloat16)
    gate = jax.nn.sigmoid(
        jnp.einsum("snc,chd->shnd", standard, projection[:, 3], preferred_element_type=jnp.float32)
    )
    scores = (
        jnp.einsum("shid,shjd->shij", mapped[0], mapped[1], preferred_element_type=jnp.float32)
        * width ** (-0.5)
        + bias
    )
    weights = jnp.exp(scores - jnp.max(scores, axis=-1, keepdims=True))
    weights = (weights / jnp.sum(weights, axis=-1, keepdims=True)).astype(jnp.bfloat16)
    attended = jnp.einsum(
        "shij,shjd->shid", weights, mapped[2], preferred_element_type=jnp.float32
    ).astype(jnp.bfloat16)
    gated = (attended.astype(jnp.float32) * gate).astype(jnp.bfloat16)
    increment = jnp.einsum(
        "shnd,hdc->snc",
        gated,
        focus_final_matrix.reshape(heads, width, depth),
        preferred_element_type=jnp.float32,
    )
    mixed = (rows.astype(jnp.float32) + increment).astype(jnp.bfloat16)

    tensor_scaled = standardise_entries(mixed, -1).astype(jnp.bfloat16)
    flank = jnp.einsum(
        "snc,ctk->tsnk",
        tensor_scaled,
        tensor_average_matrix.reshape(depth, 2, tensor_depth),
        preferred_element_type=jnp.float32,
    ).astype(jnp.bfloat16)
    left = flank[0].reshape(per_device, count // 2, 2, local_strands * tensor_depth)
    left = left.transpose(1, 2, 0, 3)
    right = flank[1].reshape(per_device, 2, half, tensor_depth).transpose(1, 0, 3, 2)
    right = right.reshape(2, per_device, tensor_depth * half)
    right = jnp.broadcast_to(right, (count // 2,) + right.shape)
    flanks = jnp.concatenate([left, right], axis=-1).reshape(count, per_device, -1)
    flanks = exchange(flanks)
    mixed_out = exchange(
        mixed.reshape(per_device, count, local_strands, depth).transpose(1, 0, 2, 3)
    ).reshape(chain_tally, local_strands, depth)

    flanks = flanks.reshape(chain_tally, -1)
    left_all = flanks[:, : local_strands * tensor_depth]
    mine = flanks[:, local_strands * tensor_depth :]
    other = with_partner(mine)
    both = jnp.stack([mine, other])
    both = jnp.where(core == 0, both, both[::-1]).reshape(2, chain_tally, tensor_depth, half)
    group = 4 if local_strands % 4 == 0 else 1
    final = tensor_average_final.reshape(tensor_depth, tensor_depth, pair_width)
    final = jnp.einsum(
        "ab,cef->eacbf", jnp.eye(group, dtype=final.dtype), final
    ).reshape(tensor_depth, group * tensor_depth, group * pair_width)
    outer = jnp.einsum(
        "xsej,sgm->exjgm",
        both,
        left_all.reshape(chain_tally, local_strands // group, group * tensor_depth),
        preferred_element_type=jnp.float32,
    ) * (1.0 / chain_tally)
    opm = jnp.einsum(
        "exjgm,emn->gxjn", outer.astype(jnp.bfloat16), final, preferred_element_type=jnp.float32
    )
    opm = opm.reshape(local_strands // group, total_res, group, pair_width)
    opm = opm.transpose(0, 2, 1, 3).reshape(local_strands, total_res, pair_width)
    pair_mid = (coupling_embedding.astype(jnp.float32) + opm).astype(jnp.bfloat16)

    pair_tri = triangle(
        pair_mid, trilateral_entry_matrix[0], trilateral_exit_matrix[0], "xcik,ycjk->cxiyj"
    )
    coupling_refreshed = triangle(
        pair_tri, trilateral_entry_matrix[1], trilateral_exit_matrix[1], "xcki,xckj->cij"
    )
    return (mixed_out, coupling_refreshed)


def solution(mesh):
    return jax.shard_map(
        body,
        mesh=mesh,
        in_specs=(P("grp", "res", None), P("res", "grp", None), P(), P(), P(), P(), P(), P(), P()),
        out_specs=(P("grp", "res", None), P("res", "grp", None)),
        check_vma=False,
    )
```

```python
import math

import jax
import jax.numpy as jnp
from jax import lax
from jax.experimental import pallas as pl
from jax.experimental.pallas import tpu as pltpu
from jax.sharding import PartitionSpec as P


def standardise_entries(values_in, axis_num):
    values_in = values_in.astype(jnp.float32)
    centred = values_in - jnp.mean(values_in, axis=axis_num, keepdims=True)
    spread = jnp.mean(centred * centred, axis=axis_num, keepdims=True)
    return centred * lax.rsqrt(spread + 1e-05)


def exchange(blocks):
    return lax.all_to_all(blocks, "res", split_axis=0, concat_axis=0, tiled=True)


def across(values, bit):
    count = lax.axis_size("res")
    return lax.ppermute(values, "res", [(k, k ^ bit) for k in range(count)])


def params(megabytes=16):
    return pltpu.CompilerParams(vmem_limit_bytes=megabytes << 20)


def whole(count):
    return [pl.BlockSpec(memory_space=pltpu.VMEM)] * count


def lanes_norm(values):
    centred = values - jnp.mean(values, axis=-1, keepdims=True)
    spread = jnp.mean(centred * centred, axis=-1, keepdims=True)
    return centred * lax.rsqrt(spread + 1e-05)


def row_edges(pair_row, entry, edges_ref, r):
    count, _, _, share, lanes = edges_ref.shape
    width = count * share
    normed = lanes_norm(pair_row).astype(jnp.bfloat16)
    mapped = lax.dot_general(
        entry, normed, (((1,), (1,)), ((), ())), preferred_element_type=jnp.float32
    )
    for side in range(2):
        base = 2 * side * width
        edge = jax.nn.sigmoid(mapped[base : base + width]) * mapped[base + width : base + 2 * width]
        edges_ref[:, side, r] = edge.reshape(count, share, lanes).astype(jnp.bfloat16)


def product_kernel(incoming, arrived_ref, product_ref, left_ref, right_ref):
    count, _, strands, share, lanes = arrived_ref.shape
    rows = count * strands
    for side, ref in enumerate((left_ref, right_ref)):
        ref[...] = arrived_ref[:, side].astype(jnp.float32).reshape(rows * share, lanes)
    dims = (((0,), (0,)), ((), ())) if incoming else (((1,), (1,)), ((), ()))
    for ch in range(share):
        left = left_ref[pl.ds(ch, rows, stride=share), :].astype(jnp.bfloat16)
        right = right_ref[pl.ds(ch, rows, stride=share), :].astype(jnp.bfloat16)
        out = lax.dot_general(left, right, dims, preferred_element_type=jnp.float32)
        product_ref[:, ch] = out.reshape(count, strands, lanes).astype(jnp.bfloat16)


def product_call(arrived, incoming):
    count, _, strands, share, lanes = arrived.shape
    scratch = pltpu.VMEM((count * strands * share, lanes), jnp.float32)
    return pl.pallas_call(
        lambda *refs: product_kernel(incoming, *refs),
        out_shape=jax.ShapeDtypeStruct((count, share, strands, lanes), jnp.bfloat16),
        in_specs=whole(1),
        out_specs=pl.BlockSpec(memory_space=pltpu.VMEM),
        scratch_shapes=[scratch, scratch],
        compiler_params=params(),
        name="edge_product",
    )(arrived)


def exit_rows(gathered_ref, exit_ref, pair_ref, gate_ref, out_ref, spread_ref, each):
    count, share, strands, lanes = gathered_ref.shape
    width = count * share
    spread_ref[...] = gathered_ref[...].astype(jnp.float32).reshape(width * strands, lanes)
    for r in range(strands):
        edges = spread_ref[pl.ds(r, width, stride=strands), :]
        centred = edges - jnp.mean(edges, axis=0, keepdims=True)
        spread = jnp.mean(centred * centred, axis=0, keepdims=True)
        normed = (centred * lax.rsqrt(spread + 1e-05)).astype(jnp.bfloat16)
        update = lax.dot_general(
            normed, exit_ref[...], (((0,), (0,)), ((), ())), preferred_element_type=jnp.float32
        )
        new = (pair_ref[r].astype(jnp.float32) + gate_ref[r] * update).astype(jnp.bfloat16)
        out_ref[r] = new
        each(r, new)


def exit_entry_kernel(gathered_ref, exit_ref, pair_ref, gate_ref, entry_ref, out_ref, edges_ref, spread_ref):
    entry = entry_ref[...]

    def each(r, new):
        row_edges(new.astype(jnp.float32), entry, edges_ref, r)

    exit_rows(gathered_ref, exit_ref, pair_ref, gate_ref, out_ref, spread_ref, each)


def exit_kernel(gathered_ref, exit_ref, pair_ref, gate_ref, out_ref, spread_ref):
    exit_rows(gathered_ref, exit_ref, pair_ref, gate_ref, out_ref, spread_ref, lambda r, new: None)


def exit_call(gathered, weight, pair_prev, gate, entry=None):
    count, share, strands, lanes = gathered.shape
    pair = jax.ShapeDtypeStruct(pair_prev.shape, jnp.bfloat16)
    scratch = [pltpu.VMEM((count * share * strands, lanes), jnp.float32)]
    if entry is None:
        return pl.pallas_call(
            exit_kernel,
            out_shape=pair,
            in_specs=whole(4),
            out_specs=pl.BlockSpec(memory_space=pltpu.VMEM),
            scratch_shapes=scratch,
            compiler_params=params(),
            name="triangle_exit",
        )(gathered, weight, pair_prev, gate)
    edges = jax.ShapeDtypeStruct((count, 2, strands, share, lanes), jnp.bfloat16)
    return pl.pallas_call(
        exit_entry_kernel,
        out_shape=(pair, edges),
        in_specs=whole(5),
        out_specs=tuple(whole(2)),
        scratch_shapes=scratch,
        compiler_params=params(),
        name="triangle_exit_entry",
    )(gathered, weight, pair_prev, gate, entry)


def opm_kernel(
    core_ref, flanks_ref, other_ref, coupling_ref, final_ref, entry_ref, pair_ref, edges_ref, outer_ref
):
    chains = flanks_ref.shape[0]
    strands, total_res, width = coupling_ref.shape
    depth = final_ref.shape[0] // 128
    groups = final_ref.shape[1] // width
    half = total_res // 2
    flat = strands * depth
    span = 8 * depth
    blocks = flat // 128
    left = flanks_ref[:, :flat]
    for which in range(2):
        for pair in range(half // 16):
            parts = []
            for jg in (2 * pair, 2 * pair + 1):
                source = other_ref if which else flanks_ref
                right = source[:, flat + jg * span : flat + (jg + 1) * span]
                part = lax.dot_general(
                    right, left, (((0,), (0,)), ((), ())), preferred_element_type=jnp.float32
                ) * (1.0 / chains)
                parts.append(part.reshape(depth, 8, flat))
            both = jnp.concatenate(parts, axis=1).astype(jnp.bfloat16)
            for ig in range(blocks):
                at = ig * total_res + which * half + pair * 16
                for e in range(depth):
                    outer_ref[at : at + 16, e * 128 : (e + 1) * 128] = both[e, :, ig * 128 : (ig + 1) * 128]
    core = core_ref[0]
    for ig in range(blocks):
        update = jnp.dot(
            outer_ref[ig * total_res : (ig + 1) * total_res, :],
            final_ref[...],
            preferred_element_type=jnp.float32,
        )
        for which in range(2):
            at = pl.multiple_of(half * (core if which == 0 else 1 - core), half)
            for i4 in range(groups):
                i = ig * groups + i4
                piece = update[which * half : (which + 1) * half, i4 * width : (i4 + 1) * width]
                prev = coupling_ref[i, pl.ds(at, half), :].astype(jnp.float32)
                pair_ref[i, pl.ds(at, half), :] = (prev + piece).astype(jnp.bfloat16)
    entry = entry_ref[...]
    for r in range(strands):
        row_edges(pair_ref[r].astype(jnp.float32), entry, edges_ref, r)


def opm_call(core, flanks, other, coupling, final, entry, count):
    strands, total_res, width = coupling.shape
    share = width // count
    rows = strands * 128 // (128 * final.shape[1] // width) * total_res
    return pl.pallas_call(
        opm_kernel,
        out_shape=(
            jax.ShapeDtypeStruct(coupling.shape, jnp.bfloat16),
            jax.ShapeDtypeStruct((count, 2, strands, share, total_res), jnp.bfloat16),
        ),
        in_specs=[pl.BlockSpec(memory_space=pltpu.SMEM)] + whole(5),
        out_specs=tuple(whole(2)),
        scratch_shapes=[pltpu.VMEM((rows, final.shape[0]), jnp.bfloat16)],
        compiler_params=params(24),
        name="outer_product_entry",
    )(core, flanks, other, coupling, final, entry)


def gate_kernel(pair_ref, weight_ref, gate_ref):
    for r in range(pair_ref.shape[0]):
        normed = lanes_norm(pair_ref[r].astype(jnp.float32)).astype(jnp.bfloat16)
        gate_ref[r] = jax.nn.sigmoid(
            jnp.dot(normed, weight_ref[...], preferred_element_type=jnp.float32)
        )


def gate_call(pair, weight):
    return pl.pallas_call(
        gate_kernel,
        out_shape=jax.ShapeDtypeStruct(pair.shape, jnp.float32),
        in_specs=whole(2),
        out_specs=pl.BlockSpec(memory_space=pltpu.VMEM),
        compiler_params=params(),
        name="pair_gate",
    )(pair, weight)


def prepare_kernel(
    final_ref,
    entry_ref,
    average_ref,
    project_ref,
    block_ref,
    sides_ref,
    gates_ref,
    left_ref,
    right_ref,
    turned_ref,
    wide_ref,
):
    turned_ref[...] = project_ref[...].astype(jnp.float32).T.astype(jnp.bfloat16)
    channels = average_ref.shape[1] // 2
    for ref, first, lane_of in (
        (left_ref, 0, lambda ch, g, size: g * channels + ch),
        (right_ref, channels, lambda ch, g, size: ch * size + g),
    ):
        size, _, lanes = ref.shape
        for g in range(size):
            ch = lax.broadcasted_iota(jnp.int32, (2 * channels, lanes), 0) - first
            lane = lax.broadcasted_iota(jnp.int32, (2 * channels, lanes), 1)
            chosen = (lane_of(ch, g, size) == lane) & (ch >= 0) & (ch < channels)
            placed = jnp.dot(
                average_ref[...],
                jnp.where(chosen, 1.0, 0.0).astype(jnp.bfloat16),
                preferred_element_type=jnp.float32,
            )
            ref[g] = placed.astype(jnp.bfloat16)
    width = final_ref.shape[1]
    depth = block_ref.shape[0] // 128
    groups = 128 // depth
    wide_ref[...] = final_ref[...].astype(jnp.float32)
    block_ref[...] = jnp.zeros(block_ref.shape, block_ref.dtype)
    for e in range(depth):
        piece = wide_ref[pl.ds(e, depth, stride=depth), :].astype(jnp.bfloat16)
        for g in range(groups):
            at = e * 128 + g * depth
            block_ref[at : at + depth, g * width : (g + 1) * width] = piece
    for d in range(2):
        sides = entry_ref[d, :, : 4 * width].astype(jnp.float32)
        sides_ref[d] = sides.T.astype(jnp.bfloat16)
        gates_ref[d] = entry_ref[d, :, 4 * width :]


def prepare_call(final, entries, average, project):
    depth = math.isqrt(final.shape[0])
    width = final.shape[1]
    groups = 128 // depth
    return pl.pallas_call(
        prepare_kernel,
        out_shape=(
            jax.ShapeDtypeStruct((depth * 128, groups * width), jnp.bfloat16),
            jax.ShapeDtypeStruct((2, 4 * width, width), jnp.bfloat16),
            jax.ShapeDtypeStruct((2, width, width), jnp.bfloat16),
            jax.ShapeDtypeStruct((groups, average.shape[0], 128), jnp.bfloat16),
            jax.ShapeDtypeStruct((8, average.shape[0], 8 * depth), jnp.bfloat16),
            jax.ShapeDtypeStruct(project.shape[::-1], jnp.bfloat16),
        ),
        in_specs=whole(4),
        out_specs=tuple(whole(6)),
        scratch_shapes=[pltpu.VMEM(final.shape, jnp.float32)],
        compiler_params=params(24),
        name="prepare_weights",
    )(final, entries, average, project)


def pack_kernel(msa_ref, pair_ref, weight_ref, out_ref):
    count, chains, parts = out_ref.shape[:3]
    for d in range(count):
        for k in range(parts - 1):
            out_ref[d, :, k] = msa_ref[d * chains : (d + 1) * chains, :, k * 128 : (k + 1) * 128]
    for r in range(pair_ref.shape[0]):
        normed = lanes_norm(pair_ref[r].astype(jnp.float32)).astype(jnp.bfloat16)
        bias = lax.dot_general(
            weight_ref[...], normed, (((1,), (1,)), ((), ())), preferred_element_type=jnp.float32
        )
        upper = bias.astype(jnp.bfloat16)
        lower = (bias - upper.astype(jnp.float32)).astype(jnp.bfloat16)
        for d in range(count):
            out_ref[d, r, parts - 1] = lower if d % 2 else upper


def pack_call(msa, pair, weight, count):
    chains, strands, depth = msa.shape
    return pl.pallas_call(
        pack_kernel,
        out_shape=jax.ShapeDtypeStruct(
            (count, chains // count, depth // 128 + 1, strands, 128), jnp.bfloat16
        ),
        in_specs=whole(3),
        out_specs=pl.BlockSpec(memory_space=pltpu.VMEM),
        compiler_params=params(),
        name="pack_rows",
    )(msa, pair, weight.T)


def arrived_rows(arrived_ref, s):
    count, _, parts, strands, lanes = arrived_ref.shape
    pieces = [
        arrived_ref[:, s, k].astype(jnp.float32).reshape(count * strands, lanes)
        for k in range(parts - 1)
    ]
    return jnp.concatenate(pieces, axis=-1)


def project_kernel(arrived_ref, weight_ref, query_ref, key_ref, value_ref, gate_ref):
    inner = query_ref.shape[1]
    for s in range(query_ref.shape[0]):
        normed = lanes_norm(arrived_rows(arrived_ref, s)).astype(jnp.bfloat16)
        mapped = lax.dot_general(
            weight_ref[...], normed, (((1,), (1,)), ((), ())), preferred_element_type=jnp.float32
        )
        for k, ref in enumerate((query_ref, key_ref, value_ref)):
            ref[s] = mapped[k * inner : (k + 1) * inner].astype(jnp.bfloat16)
        gate_ref[s] = jax.nn.sigmoid(mapped[3 * inner :])


def project_call(arrived, weight):
    count, chains, _, strands, _ = arrived.shape
    turned = (chains, weight.shape[0] // 4, count * strands)
    half = jax.ShapeDtypeStruct(turned, jnp.bfloat16)
    return pl.pallas_call(
        project_kernel,
        out_shape=(half, half, half, jax.ShapeDtypeStruct(turned, jnp.float32)),
        in_specs=whole(2),
        out_specs=tuple(whole(4)),
        compiler_params=params(),
        name="project_rows",
    )(arrived, weight)


def attend_kernel(
    width,
    arrived_ref,
    other_ref,
    query_ref,
    key_ref,
    value_ref,
    gate_ref,
    final_ref,
    left_ref,
    right_ref,
    mixed_ref,
    flanks_ref,
    bias_ref,
    turned_ref,
    scaled_ref,
):
    count, chains, strands, depth = mixed_ref.shape
    inner, total_res = query_ref.shape[1:]
    heads = inner // width
    mine = arrived_ref[:, :, arrived_ref.shape[2] - 1].astype(jnp.float32)
    bias = mine + other_ref[...].astype(jnp.float32)
    bias_ref[...] = bias.reshape(total_res * heads, total_res)
    for h in range(heads):
        turned_ref[h] = bias_ref[pl.ds(h, total_res, stride=heads), :].T
    scale = width ** (-0.5)
    for s in range(chains):
        attended = []
        for h in range(heads):
            at = slice(h * width, (h + 1) * width)
            scores = lax.dot_general(
                key_ref[s, at],
                query_ref[s, at],
                (((0,), (0,)), ((), ())),
                preferred_element_type=jnp.float32,
            )
            scores = scores * scale + turned_ref[h]
            weights = jnp.exp(scores - jnp.max(scores, axis=0, keepdims=True))
            weights = weights * (1.0 / jnp.sum(weights, axis=0, keepdims=True))
            attended.append(
                jnp.dot(
                    value_ref[s, at],
                    weights.astype(jnp.bfloat16),
                    preferred_element_type=jnp.float32,
                )
            )
        attended = jnp.concatenate(attended).astype(jnp.bfloat16).astype(jnp.float32)
        gated = (attended * gate_ref[s]).astype(jnp.bfloat16)
        increment = lax.dot_general(
            gated, final_ref[...], (((0,), (0,)), ((), ())), preferred_element_type=jnp.float32
        )
        mixed = (arrived_rows(arrived_ref, s) + increment).astype(jnp.bfloat16)
        mixed = mixed.astype(jnp.float32)
        normed = lanes_norm(mixed)
        for k in range(depth // 128):
            scaled_ref[k, pl.ds(s, total_res, stride=chains), :] = normed[:, k * 128 : (k + 1) * 128]
        mixed_ref[:, s] = mixed.reshape(count, strands, depth).astype(jnp.bfloat16)

    scaled = jnp.concatenate([scaled_ref[k] for k in range(depth // 128)], axis=-1)
    scaled = scaled.reshape(total_res, chains, depth)

    def side(weights_ref):
        group, _, lanes = weights_ref.shape
        total = None
        grouped = scaled.reshape(total_res // group, group, chains, depth)
        for g in range(group):
            part = grouped[:, g].reshape(total_res // group * chains, depth).astype(jnp.bfloat16)
            out = jnp.dot(part, weights_ref[g], preferred_element_type=jnp.float32)
            total = out if total is None else total + out
        return total.reshape(total_res // group, chains, lanes).astype(jnp.bfloat16)

    left, right = side(left_ref), side(right_ref)
    lefts, rights = left.shape[0] // count, right.shape[0] // 2
    for d in range(count):
        at = 0
        for k in range(lefts):
            flanks_ref[d, :, at : at + left.shape[2]] = left[d * lefts + k]
            at += left.shape[2]
        for k in range(rights):
            flanks_ref[d, :, at : at + right.shape[2]] = right[(d % 2) * rights + k]
            at += right.shape[2]


def attend_call(arrived, other, projected, width, final, left, right):
    count, chains, parts, strands, _ = arrived.shape
    inner, total_res = projected[0].shape[1:]
    depth, heads = (parts - 1) * 128, inner // width
    lanes = strands // left.shape[0] * left.shape[2] + total_res // 2 // right.shape[0] * right.shape[2]
    return pl.pallas_call(
        lambda *refs: attend_kernel(width, *refs),
        out_shape=(
            jax.ShapeDtypeStruct((count, chains, strands, depth), jnp.bfloat16),
            jax.ShapeDtypeStruct((count, chains, lanes), jnp.bfloat16),
        ),
        in_specs=whole(9),
        out_specs=tuple(whole(2)),
        scratch_shapes=[
            pltpu.VMEM((total_res * heads, total_res), jnp.float32),
            pltpu.VMEM((heads, total_res, total_res), jnp.float32),
            pltpu.VMEM((depth // 128, total_res * chains, 128), jnp.float32),
        ],
        compiler_params=params(),
        name="attend_rows",
    )(arrived, other, *projected, final, left, right)


def pair_track(core, flanks, other, coupling, prepared, exits):
    final, sides, gates = prepared[:3]
    count = lax.axis_size("res")
    pair, edges = opm_call(core, flanks, other, coupling, final, sides[0], count)
    for d in range(2):
        arrived = exchange(edges)
        gate = gate_call(pair, gates[d])
        product = product_call(arrived, d == 1)
        gathered = exchange(product)
        if d == 0:
            pair, edges = exit_call(gathered, exits[0], pair, gate, sides[1])
        else:
            pair = exit_call(gathered, exits[1], pair, gate)
    return pair


def triangle(pair_prev, weight_in, weight_out, contraction):
    local_strands, total_res, pair_width = pair_prev.shape
    count = lax.axis_size("res")
    share = pair_width // count
    normed = standardise_entries(pair_prev, -1).astype(jnp.bfloat16)
    five = weight_in.reshape(pair_width, 5, pair_width)
    paired = five[:, :4].reshape(pair_width, 2, 2, count, share).transpose(0, 2, 3, 1, 4)
    mapped = jnp.einsum(
        "rnc,ctwsk->twskrn", normed, paired, preferred_element_type=jnp.float32
    )
    edges = (jax.nn.sigmoid(mapped[0]) * mapped[1]).astype(jnp.bfloat16)
    arrived = exchange(edges)
    gate_pair = jax.nn.sigmoid(
        jnp.einsum("rnc,cf->rnf", normed, five[:, 4], preferred_element_type=jnp.float32)
    )
    product = jnp.einsum(
        contraction, arrived[:, 0], arrived[:, 1], preferred_element_type=jnp.float32
    ).astype(jnp.bfloat16)
    product = product.reshape(share, count, local_strands, total_res).transpose(1, 0, 2, 3)
    gathered = exchange(product).reshape(pair_width, local_strands, total_res)
    edge_norm = standardise_entries(gathered, 0).astype(jnp.bfloat16)
    update = jnp.einsum("crn,cf->rnf", edge_norm, weight_out, preferred_element_type=jnp.float32)
    return (pair_prev.astype(jnp.float32) + gate_pair * update).astype(jnp.bfloat16)


def body(
    alignment_embedding,
    coupling_embedding,
    query_key_matrix,
    coupling_logit_matrix,
    focus_final_matrix,
    tensor_average_matrix,
    tensor_average_final,
    trilateral_entry_matrix,
    trilateral_exit_matrix,
):
    chain_tally, local_strands, depth = alignment_embedding.shape
    total_res, pair_width = coupling_embedding.shape[1:]
    count = lax.axis_size("res")
    core = lax.axis_index("res") % 2
    heads = coupling_logit_matrix.shape[1]
    width = query_key_matrix.shape[1] // (4 * heads)
    per_device = chain_tally // count
    tensor_depth = tensor_average_matrix.shape[1] // 2
    half = total_res // 2

    fits = (
        pair_width == 128
        and pair_width % (8 * count) == 0
        and count & (count - 1) == 0
        and total_res == 128
        and local_strands == 8
        and per_device == 8
        and heads == 8
        and heads * width == depth
        and depth % 128 == 0
        and tensor_depth == 32
    )
    if fits:
        prepared = prepare_call(
            tensor_average_final,
            trilateral_entry_matrix,
            tensor_average_matrix,
            query_key_matrix,
        )
        packed = pack_call(alignment_embedding, coupling_embedding, coupling_logit_matrix, count)
        arrived = exchange(packed)
        other = across(arrived[:, :, -1], 1)
        projected = project_call(arrived, prepared[5])
        mixed, flanks = attend_call(
            arrived, other, projected, width, focus_final_matrix, *prepared[3:5]
        )
        flanks = exchange(flanks)
        flanks = flanks.reshape(chain_tally, -1)
        other = across(flanks, 1)
        mixed_out = exchange(mixed).reshape(chain_tally, local_strands, depth)
        refreshed = pair_track(
            core.reshape(1), flanks, other, coupling_embedding, prepared, trilateral_exit_matrix
        )
        return (mixed_out, refreshed)

    rows = exchange(alignment_embedding).reshape(count, per_device, local_strands, depth)
    rows = rows.transpose(1, 0, 2, 3).reshape(per_device, total_res, depth)
    pair_norm = standardise_entries(coupling_embedding, -1).astype(jnp.bfloat16)
    bias_rows = jnp.einsum(
        "rnc,ch->hrn", pair_norm, coupling_logit_matrix, preferred_element_type=jnp.float32
    )
    bias = lax.all_gather(bias_rows, "res", axis=1, tiled=True)

    standard = standardise_entries(rows, -1).astype(jnp.bfloat16)
    projection = query_key_matrix.reshape(depth, 4, heads, width)
    mapped = jnp.einsum(
        "snc,cthd->tshnd", standard, projection[:, :3], preferred_element_type=jnp.float32
    ).astype(jnp.bfloat16)
    gate = jax.nn.sigmoid(
        jnp.einsum("snc,chd->shnd", standard, projection[:, 3], preferred_element_type=jnp.float32)
    )
    scores = (
        jnp.einsum("shid,shjd->shij", mapped[0], mapped[1], preferred_element_type=jnp.float32)
        * width ** (-0.5)
        + bias
    )
    weights = jnp.exp(scores - jnp.max(scores, axis=-1, keepdims=True))
    weights = (weights / jnp.sum(weights, axis=-1, keepdims=True)).astype(jnp.bfloat16)
    attended = jnp.einsum(
        "shij,shjd->shid", weights, mapped[2], preferred_element_type=jnp.float32
    ).astype(jnp.bfloat16)
    gated = (attended.astype(jnp.float32) * gate).astype(jnp.bfloat16)
    increment = jnp.einsum(
        "shnd,hdc->snc",
        gated,
        focus_final_matrix.reshape(heads, width, depth),
        preferred_element_type=jnp.float32,
    )
    mixed = (rows.astype(jnp.float32) + increment).astype(jnp.bfloat16)

    tensor_scaled = standardise_entries(mixed, -1).astype(jnp.bfloat16)
    flank = jnp.einsum(
        "snc,ctk->tsnk",
        tensor_scaled,
        tensor_average_matrix.reshape(depth, 2, tensor_depth),
        preferred_element_type=jnp.float32,
    ).astype(jnp.bfloat16)
    left = flank[0].reshape(per_device, count // 2, 2, local_strands * tensor_depth)
    left = left.transpose(1, 2, 0, 3)
    right = flank[1].reshape(per_device, 2, half // 8, 8, tensor_depth).transpose(1, 0, 2, 4, 3)
    right = right.reshape(2, per_device, tensor_depth * half)
    right = jnp.broadcast_to(right, (count // 2,) + right.shape)
    flanks = jnp.concatenate([left, right], axis=-1).reshape(count, per_device, -1)
    flanks = exchange(flanks)
    mixed_out = exchange(
        mixed.reshape(per_device, count, local_strands, depth).transpose(1, 0, 2, 3)
    ).reshape(chain_tally, local_strands, depth)

    flanks = flanks.reshape(chain_tally, -1)
    mine = flanks[:, local_strands * tensor_depth :]
    other = across(mine, 1)
    group = max(1, 128 // tensor_depth)
    final = tensor_average_final.reshape(tensor_depth, tensor_depth, pair_width)
    final = jnp.einsum("ab,cef->eacbf", jnp.eye(group, dtype=final.dtype), final)
    final = final.reshape(tensor_depth * group * tensor_depth, group * pair_width)
    left_all = flanks[:, : local_strands * tensor_depth]
    both = jnp.stack([mine, other])
    both = jnp.where(core == 0, both, both[::-1])
    both = both.reshape(2, chain_tally, half // 8, tensor_depth, 8)
    outer = jnp.einsum(
        "xsaej,sgm->gxajem",
        both,
        left_all.reshape(chain_tally, local_strands // group, group * tensor_depth),
        preferred_element_type=jnp.float32,
    ) * (1.0 / chain_tally)
    outer = outer.astype(jnp.bfloat16).reshape(local_strands // group, total_res, -1)
    opm = jnp.einsum("gjk,kn->gjn", outer, final, preferred_element_type=jnp.float32)
    opm = opm.reshape(local_strands // group, total_res, group, pair_width)
    opm = opm.transpose(0, 2, 1, 3).reshape(local_strands, total_res, pair_width)
    pair_mid = (coupling_embedding.astype(jnp.float32) + opm).astype(jnp.bfloat16)

    pair_tri = triangle(
        pair_mid, trilateral_entry_matrix[0], trilateral_exit_matrix[0], "xcik,ycjk->cxiyj"
    )
    coupling_refreshed = triangle(
        pair_tri, trilateral_entry_matrix[1], trilateral_exit_matrix[1], "xcki,xckj->cij"
    )
    return (mixed_out, coupling_refreshed)


def solution(mesh):
    return jax.shard_map(
        body,
        mesh=mesh,
        in_specs=(P("grp", "res", None), P("res", "grp", None), P(), P(), P(), P(), P(), P(), P()),
        out_specs=(P("grp", "res", None), P("res", "grp", None)),
        check_vma=False,
    )
```

```python
import math

import jax
import jax.numpy as jnp
from jax import lax
from jax.experimental import pallas as pl
from jax.experimental.pallas import tpu as pltpu
from jax.sharding import PartitionSpec as P


LOG2E = math.log2(math.e)


def standardise_entries(values_in, axis_num):
    values_in = values_in.astype(jnp.float32)
    centred = values_in - jnp.mean(values_in, axis=axis_num, keepdims=True)
    spread = jnp.mean(centred * centred, axis=axis_num, keepdims=True)
    return centred * lax.rsqrt(spread + 1e-05)


def exchange(blocks):
    return lax.all_to_all(blocks, "res", split_axis=0, concat_axis=0, tiled=True)


def across(values, bit):
    count = lax.axis_size("res")
    return lax.ppermute(values, "res", [(k, k ^ bit) for k in range(count)])


def params(megabytes=16):
    return pltpu.CompilerParams(vmem_limit_bytes=megabytes << 20)


def whole(count):
    return [pl.BlockSpec(memory_space=pltpu.VMEM)] * count


def lanes_norm(values):
    centred = values - jnp.mean(values, axis=-1, keepdims=True)
    spread = jnp.mean(centred * centred, axis=-1, keepdims=True)
    return centred * lax.rsqrt(spread + 1e-05)


def edges_in_turn(new_row, entry_ref, edges_ref, gate_ref):
    count, _, strands, share, lanes = edges_ref.shape
    width = count * share
    mapped, gates = {}, {}
    for n in range(strands // 2 + 1):
        if n < strands // 2:
            normed = [lanes_norm(new_row(2 * n + k)).astype(jnp.bfloat16) for k in range(2)]
            normed = jnp.concatenate(normed)
            mapped[n] = [
                lax.dot_general(
                    entry_ref[2 * side * width : 2 * (side + 1) * width],
                    normed,
                    (((1,), (1,)), ((), ())),
                    preferred_element_type=jnp.float32,
                )
                for side in range(2)
            ]
            gates[n] = lax.dot_general(
                normed,
                entry_ref[4 * width :],
                (((1,), (1,)), ((), ())),
                preferred_element_type=jnp.float32,
            )
        if n:
            gate = jax.nn.sigmoid(gates.pop(n - 1))
            for k in range(2):
                gate_ref[2 * n - 2 + k] = gate[k * lanes : (k + 1) * lanes]
            for side, both in enumerate(mapped.pop(n - 1)):
                edge = jax.nn.sigmoid(both[:width]) * both[width:]
                for k in range(2):
                    part = edge[:, k * lanes : (k + 1) * lanes].reshape(count, share, lanes)
                    edges_ref[:, side, 2 * n - 2 + k] = part.astype(jnp.bfloat16)


def product_kernel(incoming, arrived_ref, product_ref, left_ref, right_ref):
    count, _, strands, share, lanes = arrived_ref.shape
    rows = count * strands
    for side, ref in enumerate((left_ref, right_ref)):
        ref[...] = arrived_ref[:, side].astype(jnp.float32).reshape(rows * share, lanes)
    dims = (((0,), (0,)), ((), ())) if incoming else (((1,), (1,)), ((), ()))
    for ch in range(share):
        left = left_ref[pl.ds(ch, rows, stride=share), :].astype(jnp.bfloat16)
        right = right_ref[pl.ds(ch, rows, stride=share), :].astype(jnp.bfloat16)
        out = lax.dot_general(left, right, dims, preferred_element_type=jnp.float32)
        product_ref[:, ch] = out.reshape(count, strands, lanes).astype(jnp.bfloat16)


def product_call(arrived, incoming):
    count, _, strands, share, lanes = arrived.shape
    scratch = pltpu.VMEM((count * strands * share, lanes), jnp.float32)
    return pl.pallas_call(
        lambda *refs: product_kernel(incoming, *refs),
        out_shape=jax.ShapeDtypeStruct((count, share, strands, lanes), jnp.bfloat16),
        in_specs=whole(1),
        out_specs=pl.BlockSpec(memory_space=pltpu.VMEM),
        scratch_shapes=[scratch, scratch],
        compiler_params=params(),
        name="edge_product",
    )(arrived)


def exit_rows(which, gathered_ref, exit_ref, pair_ref, gate_ref, out_ref, spread_ref):
    count, share, strands, lanes = gathered_ref.shape
    width = count * share
    spread_ref[...] = gathered_ref[...].astype(jnp.float32).reshape(width * strands, lanes)

    def update(r):
        edges = spread_ref[pl.ds(r, width, stride=strands), :]
        centred = edges - jnp.mean(edges, axis=0, keepdims=True)
        spread = jnp.mean(centred * centred, axis=0, keepdims=True)
        normed = (centred * lax.rsqrt(spread + 1e-05)).astype(jnp.bfloat16)
        return lax.dot_general(
            normed, exit_ref[which], (((0,), (0,)), ((), ())), preferred_element_type=jnp.float32
        )

    updates = {0: update(0)}

    def new_row(r):
        if r + 1 < strands:
            updates[r + 1] = update(r + 1)
        new = pair_ref[r].astype(jnp.float32) + gate_ref[r] * updates.pop(r)
        new = new.astype(jnp.bfloat16)
        out_ref[r] = new
        return new.astype(jnp.float32)

    return new_row


def exit_entry_kernel(
    gathered_ref,
    exit_ref,
    pair_ref,
    gate_ref,
    entry_ref,
    arrived_ref,
    out_ref,
    edges_ref,
    next_gate_ref,
    mixed_ref,
    spread_ref,
    sems,
):
    copies = [
        pltpu.make_async_copy(
            arrived_ref.at[:, 2 + k], mixed_ref.at[:, :, :, pl.ds(k * 128, 128)], sems.at[k]
        )
        for k in range(arrived_ref.shape[1] - 2)
    ]
    for copy in copies:
        copy.start()
    new_row = exit_rows(0, gathered_ref, exit_ref, pair_ref, gate_ref, out_ref, spread_ref)
    edges_in_turn(new_row, entry_ref.at[1], edges_ref, next_gate_ref)
    for copy in copies:
        copy.wait()


def exit_entry_call(gathered, weight, pair_prev, gate, entry, arrived):
    count, share, strands, lanes = gathered.shape
    parts = arrived.shape[1] - 2
    anywhere = pl.BlockSpec(memory_space=pl.ANY)
    return pl.pallas_call(
        exit_entry_kernel,
        out_shape=(
            jax.ShapeDtypeStruct(pair_prev.shape, jnp.bfloat16),
            jax.ShapeDtypeStruct((count, 2, strands, share, lanes), jnp.bfloat16),
            jax.ShapeDtypeStruct(pair_prev.shape, jnp.float32),
            jax.ShapeDtypeStruct((count, strands, share, parts * 128), jnp.bfloat16),
        ),
        in_specs=whole(5) + [anywhere],
        out_specs=tuple(whole(3)) + (pl.BlockSpec(memory_space=pltpu.HBM),),
        scratch_shapes=[
            pltpu.VMEM((count * share * strands, lanes), jnp.float32),
            pltpu.SemaphoreType.DMA((parts,)),
        ],
        compiler_params=params(),
        name="triangle_exit_entry",
    )(gathered, weight, pair_prev, gate, entry, arrived)


def exit_kernel(gathered_ref, exit_ref, pair_ref, gate_ref, out_ref, spread_ref):
    new_row = exit_rows(1, gathered_ref, exit_ref, pair_ref, gate_ref, out_ref, spread_ref)
    for r in range(pair_ref.shape[0]):
        new_row(r)


def exit_call(gathered, weight, pair_prev, gate):
    count, share, strands, lanes = gathered.shape
    return pl.pallas_call(
        exit_kernel,
        out_shape=jax.ShapeDtypeStruct(pair_prev.shape, jnp.bfloat16),
        in_specs=whole(4),
        out_specs=pl.BlockSpec(memory_space=pltpu.VMEM),
        scratch_shapes=[pltpu.VMEM((count * share * strands, lanes), jnp.float32)],
        compiler_params=params(),
        name="triangle_exit",
    )(gathered, weight, pair_prev, gate)


def opm_kernel(
    core_ref, flanks_ref, other_ref, mixed_ref, coupling_ref, final_ref, entry_ref, pair_ref, edges_ref, gate_ref, outer_ref
):
    chains = flanks_ref.shape[0]
    strands, total_res, width = coupling_ref.shape
    depth = final_ref.shape[0] // 128
    groups = final_ref.shape[1] // width
    half = total_res // 2
    flat = strands * depth
    span = 8 * depth
    blocks = flat // 128
    left = flanks_ref[:, :flat]
    for k in range(edges_ref.shape[1] - 2):
        edges_ref[:, 2 + k] = mixed_ref[:, :, :, k * 128 : (k + 1) * 128]
    for which in range(2):
        for pair in range(half // 16):
            parts = []
            for jg in (2 * pair, 2 * pair + 1):
                source = other_ref if which else flanks_ref
                right = source[:, flat + jg * span : flat + (jg + 1) * span]
                part = lax.dot_general(
                    right, left, (((0,), (0,)), ((), ())), preferred_element_type=jnp.float32
                ) * (1.0 / chains)
                parts.append(part.reshape(depth, 8, flat))
            both = jnp.concatenate(parts, axis=1).astype(jnp.bfloat16)
            for ig in range(blocks):
                at = ig * total_res + which * half + pair * 16
                for e in range(depth):
                    outer_ref[at : at + 16, e * 128 : (e + 1) * 128] = both[e, :, ig * 128 : (ig + 1) * 128]
    first = core_ref[0] == 0

    product = jnp.dot(outer_ref[...], final_ref[...], preferred_element_type=jnp.float32)

    def new_row(r):
        ig, i4 = divmod(r, groups)
        mine, theirs = (
            product[
                ig * total_res + which * half : ig * total_res + (which + 1) * half,
                i4 * width : (i4 + 1) * width,
            ]
            for which in range(2)
        )
        piece = jnp.concatenate([jnp.where(first, mine, theirs), jnp.where(first, theirs, mine)])
        new = (coupling_ref[r].astype(jnp.float32) + piece).astype(jnp.bfloat16)
        pair_ref[r] = new
        return new.astype(jnp.float32)

    edges_in_turn(new_row, entry_ref.at[0], edges_ref, gate_ref)


def opm_call(core, flanks, other, mixed, coupling, final, entry):
    count, _, _, depth = mixed.shape
    strands, total_res, width = coupling.shape
    share = width // count
    rows = strands * 128 // (128 * final.shape[1] // width) * total_res
    return pl.pallas_call(
        opm_kernel,
        out_shape=(
            jax.ShapeDtypeStruct(coupling.shape, jnp.bfloat16),
            jax.ShapeDtypeStruct(
                (count, 2 + depth // 128, strands, share, total_res), jnp.bfloat16
            ),
            jax.ShapeDtypeStruct(coupling.shape, jnp.float32),
        ),
        in_specs=[pl.BlockSpec(memory_space=pltpu.SMEM)] + whole(6),
        out_specs=tuple(whole(3)),
        scratch_shapes=[pltpu.VMEM((rows, final.shape[0]), jnp.bfloat16)],
        compiler_params=params(24),
        name="outer_product_entry",
    )(core, flanks, other, mixed, coupling, final, entry)


def spread_kernel(final_ref, block_ref, wide_ref):
    width = final_ref.shape[1]
    depth = block_ref.shape[0] // 128
    groups = 128 // depth
    wide_ref[...] = final_ref[...].astype(jnp.float32)
    block_ref[...] = jnp.zeros(block_ref.shape, block_ref.dtype)
    for e in range(depth):
        piece = wide_ref[pl.ds(e, depth, stride=depth), :].astype(jnp.bfloat16)
        for g in range(groups):
            at = e * 128 + g * depth
            block_ref[at : at + depth, g * width : (g + 1) * width] = piece


def spread_call(final):
    depth = math.isqrt(final.shape[0])
    width = final.shape[1]
    return pl.pallas_call(
        spread_kernel,
        out_shape=jax.ShapeDtypeStruct((depth * 128, 128 // depth * width), jnp.bfloat16),
        in_specs=whole(1),
        out_specs=pl.BlockSpec(memory_space=pltpu.VMEM),
        scratch_shapes=[pltpu.VMEM(final.shape, jnp.float32)],
        compiler_params=params(),
        name="spread_weight",
    )(final)


def prepare_kernel(
    entry_ref,
    average_ref,
    project_ref,
    sides_ref,
    left_ref,
    right_ref,
    turned_ref,
):
    turned_ref[...] = project_ref[...].astype(jnp.float32).T.astype(jnp.bfloat16)
    channels = average_ref.shape[1] // 2
    for ref, first, lane_of in (
        (left_ref, 0, lambda ch, g, size: g * channels + ch),
        (right_ref, channels, lambda ch, g, size: ch * size + g),
    ):
        size, _, lanes = ref.shape
        for g in range(size):
            ch = lax.broadcasted_iota(jnp.int32, (2 * channels, lanes), 0) - first
            lane = lax.broadcasted_iota(jnp.int32, (2 * channels, lanes), 1)
            chosen = (lane_of(ch, g, size) == lane) & (ch >= 0) & (ch < channels)
            placed = jnp.dot(
                average_ref[...],
                jnp.where(chosen, 1.0, 0.0).astype(jnp.bfloat16),
                preferred_element_type=jnp.float32,
            )
            ref[g] = placed.astype(jnp.bfloat16)
    for d in range(2):
        sides_ref[d] = entry_ref[d].astype(jnp.float32).T.astype(jnp.bfloat16)


def prepare_call(entries, average, project):
    depth = average.shape[1] // 2
    width = entries.shape[1]
    return pl.pallas_call(
        prepare_kernel,
        out_shape=(
            jax.ShapeDtypeStruct((2, 5 * width, width), jnp.bfloat16),
            jax.ShapeDtypeStruct((128 // depth, average.shape[0], 128), jnp.bfloat16),
            jax.ShapeDtypeStruct((8, average.shape[0], 8 * depth), jnp.bfloat16),
            jax.ShapeDtypeStruct(project.shape[::-1], jnp.bfloat16),
        ),
        in_specs=whole(3),
        out_specs=tuple(whole(4)),
        compiler_params=params(),
        name="prepare_weights",
    )(entries, average, project)


def pack_kernel(
    msa_ref, pair_ref, weight_ref, out_ref, own_ref, rows_ref, logit_ref, term_ref, in_sems, out_sems
):
    count, parts = out_ref.shape[:2]
    loads = [
        pltpu.make_async_copy(pair_ref, rows_ref, in_sems.at[0]),
        pltpu.make_async_copy(weight_ref, logit_ref, in_sems.at[1]),
    ]
    own = pltpu.make_async_copy(msa_ref, own_ref, in_sems.at[2])
    stores = [
        pltpu.make_async_copy(
            own_ref.at[:, :, :, pl.ds(k * 128, 128)], out_ref.at[:, k], out_sems.at[count + k]
        )
        for k in range(parts - 1)
    ]
    for copy in loads + [own]:
        copy.start()
    for copy in loads:
        copy.wait()
    for r in range(rows_ref.shape[0]):
        if r == 1:
            own.wait()
            for copy in stores:
                copy.start()
        normed = lanes_norm(rows_ref[r].astype(jnp.float32)).astype(jnp.bfloat16)
        bias = lax.dot_general(
            logit_ref[...], normed, (((1,), (1,)), ((), ())), preferred_element_type=jnp.float32
        )
        upper = bias.astype(jnp.bfloat16)
        term_ref[0, r] = upper
        term_ref[1, r] = (bias - upper.astype(jnp.float32)).astype(jnp.bfloat16)
    terms = [
        pltpu.make_async_copy(term_ref.at[d % 2], out_ref.at[d, parts - 1], out_sems.at[d])
        for d in range(count)
    ]
    for copy in terms:
        copy.start()
    for copy in stores + terms:
        copy.wait()


def pack_call(msa, pair, weight, count):
    chains, strands, depth = msa.shape
    parts, heads = depth // 128, weight.shape[1]
    anywhere = pl.BlockSpec(memory_space=pltpu.HBM)
    return pl.pallas_call(
        pack_kernel,
        out_shape=jax.ShapeDtypeStruct(
            (count, parts + 1, chains // count, strands, 128), jnp.bfloat16
        ),
        in_specs=[anywhere] * 3,
        out_specs=anywhere,
        scratch_shapes=[
            pltpu.VMEM((count, chains // count, strands, depth), jnp.bfloat16),
            pltpu.VMEM(pair.shape, jnp.bfloat16),
            pltpu.VMEM((heads, pair.shape[2]), jnp.bfloat16),
            pltpu.VMEM((2, strands, heads, pair.shape[1]), jnp.bfloat16),
            pltpu.SemaphoreType.DMA((3,)),
            pltpu.SemaphoreType.DMA((count + parts,)),
        ],
        compiler_params=params(),
        name="pack_rows",
    )(
        *(
            pltpu.with_memory_space_constraint(operand, pltpu.HBM)
            for operand in (msa.reshape(count, chains // count, strands, depth), pair, weight.T)
        )
    )


def arrived_rows(arrived_ref, s):
    count, parts, _, strands, lanes = arrived_ref.shape
    pieces = [
        arrived_ref[:, k, s].astype(jnp.float32).reshape(count * strands, lanes)
        for k in range(parts - 1)
    ]
    return jnp.concatenate(pieces, axis=-1)


def project_kernel(arrived_ref, weight_ref, query_ref, key_ref, value_ref, gate_ref):
    inner = query_ref.shape[1]
    total_res = query_ref.shape[2]
    for s in range(0, query_ref.shape[0], 2):
        rows = jnp.concatenate([arrived_rows(arrived_ref, s + k) for k in range(2)])
        mapped = lax.dot_general(
            weight_ref[...],
            lanes_norm(rows).astype(jnp.bfloat16),
            (((1,), (1,)), ((), ())),
            preferred_element_type=jnp.float32,
        )
        for k in range(2):
            part = mapped[:, k * total_res : (k + 1) * total_res]
            for block, ref in enumerate((query_ref, key_ref, value_ref)):
                ref[s + k] = part[block * inner : (block + 1) * inner].astype(jnp.bfloat16)
            gate_ref[s + k] = jax.nn.sigmoid(part[3 * inner :])


def project_call(arrived, weight):
    count, _, chains, strands, _ = arrived.shape
    turned = (chains, weight.shape[0] // 4, count * strands)
    half = jax.ShapeDtypeStruct(turned, jnp.bfloat16)
    return pl.pallas_call(
        project_kernel,
        out_shape=(half, half, half, jax.ShapeDtypeStruct(turned, jnp.float32)),
        in_specs=whole(2),
        out_specs=tuple(whole(4)),
        compiler_params=params(),
        name="project_rows",
    )(arrived, weight)


def attend_kernel(
    width,
    arrived_ref,
    other_ref,
    query_ref,
    key_ref,
    value_ref,
    gate_ref,
    final_ref,
    left_ref,
    right_ref,
    mixed_ref,
    flanks_ref,
    bias_ref,
    turned_ref,
    scaled_ref,
):
    count, chains, strands, depth = mixed_ref.shape
    inner, total_res = query_ref.shape[1:]
    heads = inner // width
    mine = arrived_ref[:, arrived_ref.shape[1] - 1].astype(jnp.float32)
    bias = mine + other_ref[...].astype(jnp.float32)
    bias_ref[...] = bias.reshape(total_res * heads, total_res)
    for h in range(heads):
        turned_ref[h] = bias_ref[pl.ds(h, total_res, stride=heads), :].T * LOG2E
    scale = width ** (-0.5) * LOG2E

    def score(s, h):
        at = slice(h * width, (h + 1) * width)
        return lax.dot_general(
            key_ref[s, at],
            query_ref[s, at],
            (((0,), (0,)), ((), ())),
            preferred_element_type=jnp.float32,
        )

    def weigh(scores, h):
        scores = scores * scale + turned_ref[h]
        weights = jnp.exp2(scores - jnp.max(scores, axis=0, keepdims=True))
        total = jnp.sum(weights, axis=0, keepdims=True)
        return (weights * (1.0 / total)).astype(jnp.bfloat16)

    def finish(s, attended):
        attended = jnp.concatenate(attended).astype(jnp.bfloat16).astype(jnp.float32)
        gated = (attended * gate_ref[s]).astype(jnp.bfloat16)
        increment = lax.dot_general(
            gated, final_ref[...], (((0,), (0,)), ((), ())), preferred_element_type=jnp.float32
        )
        mixed = (arrived_rows(arrived_ref, s) + increment).astype(jnp.bfloat16)
        mixed = mixed.astype(jnp.float32)
        normed = lanes_norm(mixed)
        for k in range(depth // 128):
            scaled_ref[k, pl.ds(s, total_res, stride=chains), :] = normed[:, k * 128 : (k + 1) * 128]
        mixed_ref[:, s] = mixed.reshape(count, strands, depth).astype(jnp.bfloat16)

    steps = [(s, h) for s in range(chains) for h in range(heads)]
    ahead = 2
    scores = {n: score(*steps[n]) for n in range(ahead)}
    weighed, attended = {}, []
    for n in range(len(steps) + 1):
        if n + ahead < len(steps):
            scores[n + ahead] = score(*steps[n + ahead])
        if n < len(steps):
            weighed[n] = weigh(scores.pop(n), steps[n][1])
        if n:
            s, h = steps[n - 1]
            attended.append(
                jnp.dot(
                    value_ref[s, h * width : (h + 1) * width],
                    weighed.pop(n - 1),
                    preferred_element_type=jnp.float32,
                )
            )
            if h + 1 == heads:
                finish(s, attended)
                attended = []

    scaled = jnp.concatenate([scaled_ref[k] for k in range(depth // 128)], axis=-1)
    scaled = scaled.reshape(total_res, chains, depth)

    def side(weights_ref):
        group, _, lanes = weights_ref.shape
        total = None
        grouped = scaled.reshape(total_res // group, group, chains, depth)
        for g in range(group):
            part = grouped[:, g].reshape(total_res // group * chains, depth).astype(jnp.bfloat16)
            out = jnp.dot(part, weights_ref[g], preferred_element_type=jnp.float32)
            total = out if total is None else total + out
        return total.reshape(total_res // group, chains, lanes).astype(jnp.bfloat16)

    left, right = side(left_ref), side(right_ref)
    lefts, rights = left.shape[0] // count, right.shape[0] // 2
    for d in range(count):
        at = 0
        for k in range(lefts):
            flanks_ref[d, :, at : at + left.shape[2]] = left[d * lefts + k]
            at += left.shape[2]
        for k in range(rights):
            flanks_ref[d, :, at : at + right.shape[2]] = right[(d % 2) * rights + k]
            at += right.shape[2]


def attend_call(arrived, other, projected, width, final, left, right):
    count, parts, chains, strands, _ = arrived.shape
    inner, total_res = projected[0].shape[1:]
    depth, heads = (parts - 1) * 128, inner // width
    lanes = strands // left.shape[0] * left.shape[2] + total_res // 2 // right.shape[0] * right.shape[2]
    return pl.pallas_call(
        lambda *refs: attend_kernel(width, *refs),
        out_shape=(
            jax.ShapeDtypeStruct((count, chains, strands, depth), jnp.bfloat16),
            jax.ShapeDtypeStruct((count, chains, lanes), jnp.bfloat16),
        ),
        in_specs=whole(9),
        out_specs=tuple(whole(2)),
        scratch_shapes=[
            pltpu.VMEM((total_res * heads, total_res), jnp.float32),
            pltpu.VMEM((heads, total_res, total_res), jnp.float32),
            pltpu.VMEM((depth // 128, total_res * chains, 128), jnp.float32),
        ],
        compiler_params=params(),
        name="attend_rows",
    )(arrived, other, *projected, final, left, right)


def pair_track(core, flanks, other, mixed, coupling, final, prepared, exits):
    sides = prepared[0]
    pair, edges, gate = opm_call(core, flanks, other, mixed, coupling, final, sides)
    for d in range(2):
        arrived = exchange(edges)
        product = product_call(arrived, d == 1)
        gathered = exchange(product)
        if d == 0:
            pair, edges, gate, returned = exit_entry_call(
                gathered, exits, pair, gate, sides, arrived
            )
        else:
            pair = exit_call(gathered, exits, pair, gate)
    return returned.reshape((-1,) + mixed.shape[2:]), pair


def triangle(pair_prev, weight_in, weight_out, contraction):
    local_strands, total_res, pair_width = pair_prev.shape
    count = lax.axis_size("res")
    share = pair_width // count
    normed = standardise_entries(pair_prev, -1).astype(jnp.bfloat16)
    five = weight_in.reshape(pair_width, 5, pair_width)
    paired = five[:, :4].reshape(pair_width, 2, 2, count, share).transpose(0, 2, 3, 1, 4)
    mapped = jnp.einsum(
        "rnc,ctwsk->twskrn", normed, paired, preferred_element_type=jnp.float32
    )
    edges = (jax.nn.sigmoid(mapped[0]) * mapped[1]).astype(jnp.bfloat16)
    arrived = exchange(edges)
    gate_pair = jax.nn.sigmoid(
        jnp.einsum("rnc,cf->rnf", normed, five[:, 4], preferred_element_type=jnp.float32)
    )
    product = jnp.einsum(
        contraction, arrived[:, 0], arrived[:, 1], preferred_element_type=jnp.float32
    ).astype(jnp.bfloat16)
    product = product.reshape(share, count, local_strands, total_res).transpose(1, 0, 2, 3)
    gathered = exchange(product).reshape(pair_width, local_strands, total_res)
    edge_norm = standardise_entries(gathered, 0).astype(jnp.bfloat16)
    update = jnp.einsum("crn,cf->rnf", edge_norm, weight_out, preferred_element_type=jnp.float32)
    return (pair_prev.astype(jnp.float32) + gate_pair * update).astype(jnp.bfloat16)


def body(
    alignment_embedding,
    coupling_embedding,
    query_key_matrix,
    coupling_logit_matrix,
    focus_final_matrix,
    tensor_average_matrix,
    tensor_average_final,
    trilateral_entry_matrix,
    trilateral_exit_matrix,
):
    chain_tally, local_strands, depth = alignment_embedding.shape
    total_res, pair_width = coupling_embedding.shape[1:]
    count = lax.axis_size("res")
    core = lax.axis_index("res") % 2
    heads = coupling_logit_matrix.shape[1]
    width = query_key_matrix.shape[1] // (4 * heads)
    per_device = chain_tally // count
    tensor_depth = tensor_average_matrix.shape[1] // 2
    half = total_res // 2

    fits = (
        pair_width == 128
        and pair_width % (8 * count) == 0
        and count & (count - 1) == 0
        and total_res == 128
        and local_strands == 8
        and per_device == 8
        and heads == 8
        and heads * width == depth
        and depth % 128 == 0
        and tensor_depth == 32
    )
    if fits:
        prepared = prepare_call(trilateral_entry_matrix, tensor_average_matrix, query_key_matrix)
        packed = pack_call(alignment_embedding, coupling_embedding, coupling_logit_matrix, count)
        arrived = exchange(packed)
        other = across(arrived[:, -1], 1)
        projected = project_call(arrived, prepared[3])
        mixed, flanks = attend_call(
            arrived, other, projected, width, focus_final_matrix, *prepared[1:3]
        )
        flanks = exchange(flanks)
        flanks = flanks.reshape(chain_tally, -1)
        other = across(flanks, 1)
        final = spread_call(tensor_average_final)
        return pair_track(
            core.reshape(1),
            flanks,
            other,
            mixed,
            coupling_embedding,
            final,
            prepared,
            trilateral_exit_matrix,
        )

    rows = exchange(alignment_embedding).reshape(count, per_device, local_strands, depth)
    rows = rows.transpose(1, 0, 2, 3).reshape(per_device, total_res, depth)
    pair_norm = standardise_entries(coupling_embedding, -1).astype(jnp.bfloat16)
    bias_rows = jnp.einsum(
        "rnc,ch->hrn", pair_norm, coupling_logit_matrix, preferred_element_type=jnp.float32
    )
    bias = lax.all_gather(bias_rows, "res", axis=1, tiled=True)

    standard = standardise_entries(rows, -1).astype(jnp.bfloat16)
    projection = query_key_matrix.reshape(depth, 4, heads, width)
    mapped = jnp.einsum(
        "snc,cthd->tshnd", standard, projection[:, :3], preferred_element_type=jnp.float32
    ).astype(jnp.bfloat16)
    gate = jax.nn.sigmoid(
        jnp.einsum("snc,chd->shnd", standard, projection[:, 3], preferred_element_type=jnp.float32)
    )
    scores = (
        jnp.einsum("shid,shjd->shij", mapped[0], mapped[1], preferred_element_type=jnp.float32)
        * width ** (-0.5)
        + bias
    )
    weights = jnp.exp(scores - jnp.max(scores, axis=-1, keepdims=True))
    weights = (weights / jnp.sum(weights, axis=-1, keepdims=True)).astype(jnp.bfloat16)
    attended = jnp.einsum(
        "shij,shjd->shid", weights, mapped[2], preferred_element_type=jnp.float32
    ).astype(jnp.bfloat16)
    gated = (attended.astype(jnp.float32) * gate).astype(jnp.bfloat16)
    increment = jnp.einsum(
        "shnd,hdc->snc",
        gated,
        focus_final_matrix.reshape(heads, width, depth),
        preferred_element_type=jnp.float32,
    )
    mixed = (rows.astype(jnp.float32) + increment).astype(jnp.bfloat16)

    tensor_scaled = standardise_entries(mixed, -1).astype(jnp.bfloat16)
    flank = jnp.einsum(
        "snc,ctk->tsnk",
        tensor_scaled,
        tensor_average_matrix.reshape(depth, 2, tensor_depth),
        preferred_element_type=jnp.float32,
    ).astype(jnp.bfloat16)
    left = flank[0].reshape(per_device, count // 2, 2, local_strands * tensor_depth)
    left = left.transpose(1, 2, 0, 3)
    right = flank[1].reshape(per_device, 2, half // 8, 8, tensor_depth).transpose(1, 0, 2, 4, 3)
    right = right.reshape(2, per_device, tensor_depth * half)
    right = jnp.broadcast_to(right, (count // 2,) + right.shape)
    flanks = jnp.concatenate([left, right], axis=-1).reshape(count, per_device, -1)
    flanks = exchange(flanks)
    mixed_out = exchange(
        mixed.reshape(per_device, count, local_strands, depth).transpose(1, 0, 2, 3)
    ).reshape(chain_tally, local_strands, depth)

    flanks = flanks.reshape(chain_tally, -1)
    mine = flanks[:, local_strands * tensor_depth :]
    other = across(mine, 1)
    group = max(1, 128 // tensor_depth)
    final = tensor_average_final.reshape(tensor_depth, tensor_depth, pair_width)
    final = jnp.einsum("ab,cef->eacbf", jnp.eye(group, dtype=final.dtype), final)
    final = final.reshape(tensor_depth * group * tensor_depth, group * pair_width)
    left_all = flanks[:, : local_strands * tensor_depth]
    both = jnp.stack([mine, other])
    both = jnp.where(core == 0, both, both[::-1])
    both = both.reshape(2, chain_tally, half // 8, tensor_depth, 8)
    outer = jnp.einsum(
        "xsaej,sgm->gxajem",
        both,
        left_all.reshape(chain_tally, local_strands // group, group * tensor_depth),
        preferred_element_type=jnp.float32,
    ) * (1.0 / chain_tally)
    outer = outer.astype(jnp.bfloat16).reshape(local_strands // group, total_res, -1)
    opm = jnp.einsum("gjk,kn->gjn", outer, final, preferred_element_type=jnp.float32)
    opm = opm.reshape(local_strands // group, total_res, group, pair_width)
    opm = opm.transpose(0, 2, 1, 3).reshape(local_strands, total_res, pair_width)
    pair_mid = (coupling_embedding.astype(jnp.float32) + opm).astype(jnp.bfloat16)

    pair_tri = triangle(
        pair_mid, trilateral_entry_matrix[0], trilateral_exit_matrix[0], "xcik,ycjk->cxiyj"
    )
    coupling_refreshed = triangle(
        pair_tri, trilateral_entry_matrix[1], trilateral_exit_matrix[1], "xcki,xckj->cij"
    )
    return (mixed_out, coupling_refreshed)


def solution(mesh):
    return jax.shard_map(
        body,
        mesh=mesh,
        in_specs=(P("grp", "res", None), P("res", "grp", None), P(), P(), P(), P(), P(), P(), P()),
        out_specs=(P("grp", "res", None), P("res", "grp", None)),
        check_vma=False,
    )
```

```python
import math

import jax
import jax.numpy as jnp
from jax import lax
from jax.experimental import pallas as pl
from jax.experimental.pallas import tpu as pltpu
from jax.sharding import PartitionSpec as P


LOG2E = math.log2(math.e)


def standardise_entries(values_in, axis_num):
    values_in = values_in.astype(jnp.float32)
    centred = values_in - jnp.mean(values_in, axis=axis_num, keepdims=True)
    spread = jnp.mean(centred * centred, axis=axis_num, keepdims=True)
    return centred * lax.rsqrt(spread + 1e-05)


def exchange(blocks):
    return lax.all_to_all(blocks, "res", split_axis=0, concat_axis=0, tiled=True)


def across(values, bit):
    count = lax.axis_size("res")
    return lax.ppermute(values, "res", [(k, k ^ bit) for k in range(count)])


def params(megabytes=16):
    return pltpu.CompilerParams(vmem_limit_bytes=megabytes << 20)


def whole(count):
    return [pl.BlockSpec(memory_space=pltpu.VMEM)] * count


def lanes_norm(values):
    centred = values - jnp.mean(values, axis=-1, keepdims=True)
    spread = jnp.mean(centred * centred, axis=-1, keepdims=True)
    return centred * lax.rsqrt(spread + 1e-05)


def edges_in_turn(new_row, entry_ref, edges_ref, gate_ref):
    count, _, strands, share, lanes = edges_ref.shape
    width = count * share
    normed, mapped, gates = {}, {}, {}
    pairs = strands // 2
    for n in range(pairs + 2):
        if n < pairs:
            rows = [lanes_norm(new_row(2 * n + k)).astype(jnp.bfloat16) for k in range(2)]
            normed[n] = jnp.concatenate(rows)
        if 0 < n <= pairs:
            rows = normed.pop(n - 1)
            mapped[n - 1] = [
                lax.dot_general(
                    entry_ref[2 * side * width : 2 * (side + 1) * width],
                    rows,
                    (((1,), (1,)), ((), ())),
                    preferred_element_type=jnp.float32,
                )
                for side in range(2)
            ]
            gates[n - 1] = lax.dot_general(
                rows,
                entry_ref[4 * width :],
                (((1,), (1,)), ((), ())),
                preferred_element_type=jnp.float32,
            )
        if n > 1:
            gate = jax.nn.sigmoid(gates.pop(n - 2))
            for k in range(2):
                gate_ref[2 * n - 4 + k] = gate[k * lanes : (k + 1) * lanes]
            for side, both in enumerate(mapped.pop(n - 2)):
                edge = jax.nn.sigmoid(both[:width]) * both[width:]
                for k in range(2):
                    part = edge[:, k * lanes : (k + 1) * lanes].reshape(count, share, lanes)
                    edges_ref[:, side, 2 * n - 4 + k] = part.astype(jnp.bfloat16)


def product_kernel(incoming, arrived_ref, product_ref, left_ref, right_ref):
    count, _, strands, share, lanes = arrived_ref.shape
    rows = count * strands
    for side, ref in enumerate((left_ref, right_ref)):
        ref[...] = arrived_ref[:, side].astype(jnp.float32).reshape(rows * share, lanes)
    dims = (((0,), (0,)), ((), ())) if incoming else (((1,), (1,)), ((), ()))
    for ch in range(share):
        left = left_ref[pl.ds(ch, rows, stride=share), :].astype(jnp.bfloat16)
        right = right_ref[pl.ds(ch, rows, stride=share), :].astype(jnp.bfloat16)
        out = lax.dot_general(left, right, dims, preferred_element_type=jnp.float32)
        product_ref[:, ch] = out.reshape(count, strands, lanes).astype(jnp.bfloat16)


def product_call(arrived, incoming):
    count, _, strands, share, lanes = arrived.shape
    scratch = pltpu.VMEM((count * strands * share, lanes), jnp.float32)
    return pl.pallas_call(
        lambda *refs: product_kernel(incoming, *refs),
        out_shape=jax.ShapeDtypeStruct((count, share, strands, lanes), jnp.bfloat16),
        in_specs=whole(1),
        out_specs=pl.BlockSpec(memory_space=pltpu.VMEM),
        scratch_shapes=[scratch, scratch],
        compiler_params=params(),
        name="edge_product",
    )(arrived)


def exit_rows(which, gathered_ref, exit_ref, pair_ref, gate_ref, out_ref, spread_ref):
    count, share, strands, lanes = gathered_ref.shape
    width = count * share
    spread_ref[...] = gathered_ref[...].astype(jnp.float32).reshape(width * strands, lanes)

    def update(r):
        edges = spread_ref[pl.ds(r, width, stride=strands), :]
        centred = edges - jnp.mean(edges, axis=0, keepdims=True)
        spread = jnp.mean(centred * centred, axis=0, keepdims=True)
        normed = (centred * lax.rsqrt(spread + 1e-05)).astype(jnp.bfloat16)
        return lax.dot_general(
            normed, exit_ref[which], (((0,), (0,)), ((), ())), preferred_element_type=jnp.float32
        )

    ahead = 2
    updates = {r: update(r) for r in range(ahead)}

    def new_row(r):
        if r + ahead < strands:
            updates[r + ahead] = update(r + ahead)
        new = pair_ref[r].astype(jnp.float32) + gate_ref[r] * updates.pop(r)
        new = new.astype(jnp.bfloat16)
        out_ref[r] = new
        return new.astype(jnp.float32)

    return new_row


def exit_entry_kernel(
    gathered_ref,
    exit_ref,
    pair_ref,
    gate_ref,
    entry_ref,
    arrived_ref,
    out_ref,
    edges_ref,
    next_gate_ref,
    mixed_ref,
    spread_ref,
    sems,
):
    copies = [
        pltpu.make_async_copy(
            arrived_ref.at[:, 2 + k], mixed_ref.at[:, :, :, pl.ds(k * 128, 128)], sems.at[k]
        )
        for k in range(arrived_ref.shape[1] - 2)
    ]
    for copy in copies:
        copy.start()
    new_row = exit_rows(0, gathered_ref, exit_ref, pair_ref, gate_ref, out_ref, spread_ref)
    edges_in_turn(new_row, entry_ref.at[1], edges_ref, next_gate_ref)
    for copy in copies:
        copy.wait()


def exit_entry_call(gathered, weight, pair_prev, gate, entry, arrived):
    count, share, strands, lanes = gathered.shape
    parts = arrived.shape[1] - 2
    anywhere = pl.BlockSpec(memory_space=pl.ANY)
    return pl.pallas_call(
        exit_entry_kernel,
        out_shape=(
            jax.ShapeDtypeStruct(pair_prev.shape, jnp.bfloat16),
            jax.ShapeDtypeStruct((count, 2, strands, share, lanes), jnp.bfloat16),
            jax.ShapeDtypeStruct(pair_prev.shape, jnp.float32),
            jax.ShapeDtypeStruct((count, strands, share, parts * 128), jnp.bfloat16),
        ),
        in_specs=whole(5) + [anywhere],
        out_specs=tuple(whole(3)) + (pl.BlockSpec(memory_space=pltpu.HBM),),
        scratch_shapes=[
            pltpu.VMEM((count * share * strands, lanes), jnp.float32),
            pltpu.SemaphoreType.DMA((parts,)),
        ],
        compiler_params=params(),
        name="triangle_exit_entry",
    )(gathered, weight, pair_prev, gate, entry, arrived)


def exit_kernel(gathered_ref, exit_ref, pair_ref, gate_ref, out_ref, spread_ref):
    new_row = exit_rows(1, gathered_ref, exit_ref, pair_ref, gate_ref, out_ref, spread_ref)
    for r in range(pair_ref.shape[0]):
        new_row(r)


def exit_call(gathered, weight, pair_prev, gate):
    count, share, strands, lanes = gathered.shape
    return pl.pallas_call(
        exit_kernel,
        out_shape=jax.ShapeDtypeStruct(pair_prev.shape, jnp.bfloat16),
        in_specs=whole(4),
        out_specs=pl.BlockSpec(memory_space=pltpu.VMEM),
        scratch_shapes=[pltpu.VMEM((count * share * strands, lanes), jnp.float32)],
        compiler_params=params(),
        name="triangle_exit",
    )(gathered, weight, pair_prev, gate)


def half_product(flanks_ref, left, final_ref, outer_ref):
    chains, flat = left.shape
    depth = final_ref.shape[0] // 128
    span, blocks = 8 * depth, flat // 128
    half = (flanks_ref.shape[1] - flat) // depth
    for pair in range(half // 16):
        parts = []
        for jg in (2 * pair, 2 * pair + 1):
            part = lax.dot_general(
                flanks_ref[:, flat + jg * span : flat + (jg + 1) * span],
                left,
                (((0,), (0,)), ((), ())),
                preferred_element_type=jnp.float32,
            ) * (1.0 / chains)
            parts.append(part.reshape(depth, 8, flat))
        both = jnp.concatenate(parts, axis=1).astype(jnp.bfloat16)
        for ig in range(blocks):
            at = ig * half + pair * 16
            for e in range(depth):
                outer_ref[at : at + 16, e * 128 : (e + 1) * 128] = both[e, :, ig * 128 : (ig + 1) * 128]
    return jnp.dot(outer_ref[...], final_ref[...], preferred_element_type=jnp.float32)


def own_kernel(flat, flanks_ref, final_ref, product_ref, outer_ref):
    product_ref[...] = half_product(flanks_ref, flanks_ref[:, :flat], final_ref, outer_ref)


def own_call(flanks, final, flat, half):
    rows = flat // 128 * half
    return pl.pallas_call(
        lambda *refs: own_kernel(flat, *refs),
        out_shape=jax.ShapeDtypeStruct((rows, final.shape[1]), jnp.float32),
        in_specs=whole(2),
        out_specs=pl.BlockSpec(memory_space=pltpu.VMEM),
        scratch_shapes=[pltpu.VMEM((rows, final.shape[0]), jnp.bfloat16)],
        compiler_params=params(24),
        name="outer_product_own",
    )(flanks, final)


def opm_kernel(
    flat,
    core_ref,
    flanks_ref,
    other_ref,
    own_ref,
    mixed_ref,
    coupling_ref,
    final_ref,
    entry_ref,
    pair_ref,
    edges_ref,
    gate_ref,
    outer_ref,
):
    _, total_res, width = coupling_ref.shape
    groups = final_ref.shape[1] // width
    half = total_res // 2
    for k in range(edges_ref.shape[1] - 2):
        edges_ref[:, 2 + k] = mixed_ref[:, :, :, k * 128 : (k + 1) * 128]
    first = core_ref[0] == 0
    product = half_product(other_ref, flanks_ref[:, :flat], final_ref, outer_ref)

    def new_row(r):
        ig, i4 = divmod(r, groups)
        rows, lanes = slice(ig * half, (ig + 1) * half), slice(i4 * width, (i4 + 1) * width)
        mine, theirs = own_ref[rows, lanes], product[rows, lanes]
        piece = jnp.concatenate([jnp.where(first, mine, theirs), jnp.where(first, theirs, mine)])
        new = (coupling_ref[r].astype(jnp.float32) + piece).astype(jnp.bfloat16)
        pair_ref[r] = new
        return new.astype(jnp.float32)

    edges_in_turn(new_row, entry_ref.at[0], edges_ref, gate_ref)


def opm_call(core, flanks, other, own, mixed, coupling, final, entry, flat):
    count, _, _, depth = mixed.shape
    strands, total_res, width = coupling.shape
    share = width // count
    return pl.pallas_call(
        lambda *refs: opm_kernel(flat, *refs),
        out_shape=(
            jax.ShapeDtypeStruct(coupling.shape, jnp.bfloat16),
            jax.ShapeDtypeStruct(
                (count, 2 + depth // 128, strands, share, total_res), jnp.bfloat16
            ),
            jax.ShapeDtypeStruct(coupling.shape, jnp.float32),
        ),
        in_specs=[pl.BlockSpec(memory_space=pltpu.SMEM)] + whole(7),
        out_specs=tuple(whole(3)),
        scratch_shapes=[pltpu.VMEM((own.shape[0], final.shape[0]), jnp.bfloat16)],
        compiler_params=params(24),
        name="outer_product_entry",
    )(core, flanks, other, own, mixed, coupling, final, entry)


def spread_kernel(final_ref, block_ref, wide_ref):
    width = final_ref.shape[1]
    depth = block_ref.shape[0] // 128
    groups = 128 // depth
    wide_ref[...] = final_ref[...].astype(jnp.float32)
    block_ref[...] = jnp.zeros(block_ref.shape, block_ref.dtype)
    for e in range(depth):
        piece = wide_ref[pl.ds(e, depth, stride=depth), :].astype(jnp.bfloat16)
        for g in range(groups):
            at = e * 128 + g * depth
            block_ref[at : at + depth, g * width : (g + 1) * width] = piece


def spread_call(final):
    depth = math.isqrt(final.shape[0])
    width = final.shape[1]
    return pl.pallas_call(
        spread_kernel,
        out_shape=jax.ShapeDtypeStruct((depth * 128, 128 // depth * width), jnp.bfloat16),
        in_specs=whole(1),
        out_specs=pl.BlockSpec(memory_space=pltpu.VMEM),
        scratch_shapes=[pltpu.VMEM(final.shape, jnp.float32)],
        compiler_params=params(),
        name="spread_weight",
    )(final)


def prepare_kernel(
    entry_ref,
    average_ref,
    project_ref,
    focus_ref,
    sides_ref,
    left_ref,
    right_ref,
    turned_ref,
    near_focus_ref,
):
    near_focus_ref[...] = focus_ref[...]
    turned_ref[...] = project_ref[...].astype(jnp.float32).T.astype(jnp.bfloat16)
    channels = average_ref.shape[1] // 2
    for ref, first, lane_of in (
        (left_ref, 0, lambda ch, g, size: g * channels + ch),
        (right_ref, channels, lambda ch, g, size: ch * size + g),
    ):
        size, _, lanes = ref.shape
        for g in range(size):
            ch = lax.broadcasted_iota(jnp.int32, (2 * channels, lanes), 0) - first
            lane = lax.broadcasted_iota(jnp.int32, (2 * channels, lanes), 1)
            chosen = (lane_of(ch, g, size) == lane) & (ch >= 0) & (ch < channels)
            placed = jnp.dot(
                average_ref[...],
                jnp.where(chosen, 1.0, 0.0).astype(jnp.bfloat16),
                preferred_element_type=jnp.float32,
            )
            ref[g] = placed.astype(jnp.bfloat16)
    for d in range(2):
        sides_ref[d] = entry_ref[d].astype(jnp.float32).T.astype(jnp.bfloat16)


def prepare_call(entries, average, project, focus):
    depth = average.shape[1] // 2
    width = entries.shape[1]
    return pl.pallas_call(
        prepare_kernel,
        out_shape=(
            jax.ShapeDtypeStruct((2, 5 * width, width), jnp.bfloat16),
            jax.ShapeDtypeStruct((128 // depth, average.shape[0], 128), jnp.bfloat16),
            jax.ShapeDtypeStruct((8, average.shape[0], 8 * depth), jnp.bfloat16),
            jax.ShapeDtypeStruct(project.shape[::-1], jnp.bfloat16),
            jax.ShapeDtypeStruct(focus.shape, jnp.bfloat16),
        ),
        in_specs=whole(4),
        out_specs=tuple(whole(5)),
        compiler_params=params(),
        name="prepare_weights",
    )(entries, average, project, focus)


def pack_kernel(
    msa_ref, pair_ref, weight_ref, out_ref, own_ref, rows_ref, logit_ref, term_ref, in_sems, out_sems
):
    count, parts = out_ref.shape[:2]
    loads = [
        pltpu.make_async_copy(pair_ref, rows_ref, in_sems.at[0]),
        pltpu.make_async_copy(weight_ref, logit_ref, in_sems.at[1]),
    ]
    own = pltpu.make_async_copy(msa_ref, own_ref, in_sems.at[2])
    stores = [
        pltpu.make_async_copy(
            own_ref.at[:, :, :, pl.ds(k * 128, 128)], out_ref.at[:, k], out_sems.at[count + k]
        )
        for k in range(parts - 1)
    ]
    for copy in loads + [own]:
        copy.start()
    for copy in loads:
        copy.wait()
    for r in range(rows_ref.shape[0]):
        if r == 1:
            own.wait()
            for copy in stores:
                copy.start()
        normed = lanes_norm(rows_ref[r].astype(jnp.float32)).astype(jnp.bfloat16)
        bias = lax.dot_general(
            logit_ref[...], normed, (((1,), (1,)), ((), ())), preferred_element_type=jnp.float32
        )
        upper = bias.astype(jnp.bfloat16)
        term_ref[0, r] = upper
        term_ref[1, r] = (bias - upper.astype(jnp.float32)).astype(jnp.bfloat16)
    terms = [
        pltpu.make_async_copy(term_ref.at[d % 2], out_ref.at[d, parts - 1], out_sems.at[d])
        for d in range(count)
    ]
    for copy in terms:
        copy.start()
    for copy in stores + terms:
        copy.wait()


def pack_call(msa, pair, weight, count):
    chains, strands, depth = msa.shape
    parts, heads = depth // 128, weight.shape[1]
    anywhere = pl.BlockSpec(memory_space=pltpu.HBM)
    return pl.pallas_call(
        pack_kernel,
        out_shape=jax.ShapeDtypeStruct(
            (count, parts + 1, chains // count, strands, 128), jnp.bfloat16
        ),
        in_specs=[anywhere] * 3,
        out_specs=anywhere,
        scratch_shapes=[
            pltpu.VMEM((count, chains // count, strands, depth), jnp.bfloat16),
            pltpu.VMEM(pair.shape, jnp.bfloat16),
            pltpu.VMEM((heads, pair.shape[2]), jnp.bfloat16),
            pltpu.VMEM((2, strands, heads, pair.shape[1]), jnp.bfloat16),
            pltpu.SemaphoreType.DMA((3,)),
            pltpu.SemaphoreType.DMA((count + parts,)),
        ],
        compiler_params=params(),
        name="pack_rows",
    )(
        *(
            pltpu.with_memory_space_constraint(operand, pltpu.HBM)
            for operand in (msa.reshape(count, chains // count, strands, depth), pair, weight.T)
        )
    )


def arrived_rows(arrived_ref, s):
    count, parts, _, strands, lanes = arrived_ref.shape
    pieces = [
        arrived_ref[:, k, s].astype(jnp.float32).reshape(count * strands, lanes)
        for k in range(parts - 1)
    ]
    return jnp.concatenate(pieces, axis=-1)


def project_kernel(arrived_ref, weight_ref, query_ref, key_ref, value_ref, gate_ref):
    inner = query_ref.shape[1]
    total_res = query_ref.shape[2]
    for s in range(0, query_ref.shape[0], 2):
        rows = jnp.concatenate([arrived_rows(arrived_ref, s + k) for k in range(2)])
        mapped = lax.dot_general(
            weight_ref[...],
            lanes_norm(rows).astype(jnp.bfloat16),
            (((1,), (1,)), ((), ())),
            preferred_element_type=jnp.float32,
        )
        for k in range(2):
            part = mapped[:, k * total_res : (k + 1) * total_res]
            for block, ref in enumerate((query_ref, key_ref, value_ref)):
                ref[s + k] = part[block * inner : (block + 1) * inner].astype(jnp.bfloat16)
            gate_ref[s + k] = jax.nn.sigmoid(part[3 * inner :])


def project_call(arrived, weight):
    count, _, chains, strands, _ = arrived.shape
    turned = (chains, weight.shape[0] // 4, count * strands)
    half = jax.ShapeDtypeStruct(turned, jnp.bfloat16)
    return pl.pallas_call(
        project_kernel,
        out_shape=(half, half, half, jax.ShapeDtypeStruct(turned, jnp.float32)),
        in_specs=whole(2),
        out_specs=tuple(whole(4)),
        compiler_params=params(),
        name="project_rows",
    )(arrived, weight)


def attend_kernel(
    width,
    arrived_ref,
    other_ref,
    query_ref,
    key_ref,
    value_ref,
    gate_ref,
    final_ref,
    left_ref,
    right_ref,
    mixed_ref,
    flanks_ref,
    bias_ref,
    turned_ref,
    scaled_ref,
):
    count, chains, strands, depth = mixed_ref.shape
    inner, total_res = query_ref.shape[1:]
    heads = inner // width
    mine = arrived_ref[:, arrived_ref.shape[1] - 1].astype(jnp.float32)
    bias = mine + other_ref[...].astype(jnp.float32)
    bias_ref[...] = bias.reshape(total_res * heads, total_res)
    for h in range(heads):
        turned_ref[h] = bias_ref[pl.ds(h, total_res, stride=heads), :].T * LOG2E
    scale = width ** (-0.5) * LOG2E

    def score(s, h):
        at = slice(h * width, (h + 1) * width)
        return lax.dot_general(
            key_ref[s, at],
            query_ref[s, at],
            (((0,), (0,)), ((), ())),
            preferred_element_type=jnp.float32,
        )

    def weigh(scores, h):
        scores = scores * scale + turned_ref[h]
        weights = jnp.exp2(scores - jnp.max(scores, axis=0, keepdims=True))
        total = jnp.sum(weights, axis=0, keepdims=True)
        return (weights * (1.0 / total)).astype(jnp.bfloat16)

    def finish(s, attended):
        attended = jnp.concatenate(attended).astype(jnp.bfloat16).astype(jnp.float32)
        gated = (attended * gate_ref[s]).astype(jnp.bfloat16)
        increment = lax.dot_general(
            gated, final_ref[...], (((0,), (0,)), ((), ())), preferred_element_type=jnp.float32
        )
        mixed = (arrived_rows(arrived_ref, s) + increment).astype(jnp.bfloat16)
        mixed = mixed.astype(jnp.float32)
        normed = lanes_norm(mixed)
        for k in range(depth // 128):
            scaled_ref[k, pl.ds(s, total_res, stride=chains), :] = normed[:, k * 128 : (k + 1) * 128]
        mixed_ref[:, s] = mixed.reshape(count, strands, depth).astype(jnp.bfloat16)

    steps = [(s, h) for s in range(chains) for h in range(heads)]
    ahead = 2
    scores = {n: score(*steps[n]) for n in range(ahead)}
    weighed, attended = {}, []
    for n in range(len(steps) + 1):
        if n + ahead < len(steps):
            scores[n + ahead] = score(*steps[n + ahead])
        if n < len(steps):
            weighed[n] = weigh(scores.pop(n), steps[n][1])
        if n:
            s, h = steps[n - 1]
            attended.append(
                jnp.dot(
                    value_ref[s, h * width : (h + 1) * width],
                    weighed.pop(n - 1),
                    preferred_element_type=jnp.float32,
                )
            )
            if h + 1 == heads:
                finish(s, attended)
                attended = []

    scaled = jnp.concatenate([scaled_ref[k] for k in range(depth // 128)], axis=-1)
    scaled = scaled.reshape(total_res, chains, depth)

    def side(weights_ref):
        group, _, lanes = weights_ref.shape
        total = None
        grouped = scaled.reshape(total_res // group, group, chains, depth)
        for g in range(group):
            part = grouped[:, g].reshape(total_res // group * chains, depth).astype(jnp.bfloat16)
            out = jnp.dot(part, weights_ref[g], preferred_element_type=jnp.float32)
            total = out if total is None else total + out
        return total.reshape(total_res // group, chains, lanes).astype(jnp.bfloat16)

    left, right = side(left_ref), side(right_ref)
    lefts, rights = left.shape[0] // count, right.shape[0] // 2
    for d in range(count):
        at = 0
        for k in range(lefts):
            flanks_ref[d, :, at : at + left.shape[2]] = left[d * lefts + k]
            at += left.shape[2]
        for k in range(rights):
            flanks_ref[d, :, at : at + right.shape[2]] = right[(d % 2) * rights + k]
            at += right.shape[2]


def attend_call(arrived, other, projected, width, final, left, right):
    count, parts, chains, strands, _ = arrived.shape
    inner, total_res = projected[0].shape[1:]
    depth, heads = (parts - 1) * 128, inner // width
    lanes = strands // left.shape[0] * left.shape[2] + total_res // 2 // right.shape[0] * right.shape[2]
    return pl.pallas_call(
        lambda *refs: attend_kernel(width, *refs),
        out_shape=(
            jax.ShapeDtypeStruct((count, chains, strands, depth), jnp.bfloat16),
            jax.ShapeDtypeStruct((count, chains, lanes), jnp.bfloat16),
        ),
        in_specs=whole(9),
        out_specs=tuple(whole(2)),
        scratch_shapes=[
            pltpu.VMEM((total_res * heads, total_res), jnp.float32),
            pltpu.VMEM((heads, total_res, total_res), jnp.float32),
            pltpu.VMEM((depth // 128, total_res * chains, 128), jnp.float32),
        ],
        compiler_params=params(),
        name="attend_rows",
    )(arrived, other, *projected, final, left, right)


def pair_track(core, flanks, other, mixed, coupling, final, prepared, exits, flat):
    sides = prepared[0]
    own = own_call(flanks, final, flat, coupling.shape[1] // 2)
    pair, edges, gate = opm_call(core, flanks, other, own, mixed, coupling, final, sides, flat)
    for d in range(2):
        arrived = exchange(edges)
        product = product_call(arrived, d == 1)
        gathered = exchange(product)
        if d == 0:
            pair, edges, gate, returned = exit_entry_call(
                gathered, exits, pair, gate, sides, arrived
            )
        else:
            pair = exit_call(gathered, exits, pair, gate)
    return returned.reshape((-1,) + mixed.shape[2:]), pair


def triangle(pair_prev, weight_in, weight_out, contraction):
    local_strands, total_res, pair_width = pair_prev.shape
    count = lax.axis_size("res")
    share = pair_width // count
    normed = standardise_entries(pair_prev, -1).astype(jnp.bfloat16)
    five = weight_in.reshape(pair_width, 5, pair_width)
    paired = five[:, :4].reshape(pair_width, 2, 2, count, share).transpose(0, 2, 3, 1, 4)
    mapped = jnp.einsum(
        "rnc,ctwsk->twskrn", normed, paired, preferred_element_type=jnp.float32
    )
    edges = (jax.nn.sigmoid(mapped[0]) * mapped[1]).astype(jnp.bfloat16)
    arrived = exchange(edges)
    gate_pair = jax.nn.sigmoid(
        jnp.einsum("rnc,cf->rnf", normed, five[:, 4], preferred_element_type=jnp.float32)
    )
    product = jnp.einsum(
        contraction, arrived[:, 0], arrived[:, 1], preferred_element_type=jnp.float32
    ).astype(jnp.bfloat16)
    product = product.reshape(share, count, local_strands, total_res).transpose(1, 0, 2, 3)
    gathered = exchange(product).reshape(pair_width, local_strands, total_res)
    edge_norm = standardise_entries(gathered, 0).astype(jnp.bfloat16)
    update = jnp.einsum("crn,cf->rnf", edge_norm, weight_out, preferred_element_type=jnp.float32)
    return (pair_prev.astype(jnp.float32) + gate_pair * update).astype(jnp.bfloat16)


def body(
    alignment_embedding,
    coupling_embedding,
    query_key_matrix,
    coupling_logit_matrix,
    focus_final_matrix,
    tensor_average_matrix,
    tensor_average_final,
    trilateral_entry_matrix,
    trilateral_exit_matrix,
):
    chain_tally, local_strands, depth = alignment_embedding.shape
    total_res, pair_width = coupling_embedding.shape[1:]
    count = lax.axis_size("res")
    core = lax.axis_index("res") % 2
    heads = coupling_logit_matrix.shape[1]
    width = query_key_matrix.shape[1] // (4 * heads)
    per_device = chain_tally // count
    tensor_depth = tensor_average_matrix.shape[1] // 2
    half = total_res // 2

    fits = (
        pair_width == 128
        and pair_width % (8 * count) == 0
        and count & (count - 1) == 0
        and total_res == 128
        and local_strands == 8
        and per_device == 8
        and heads == 8
        and heads * width == depth
        and depth % 128 == 0
        and tensor_depth == 32
    )
    if fits:
        prepared = prepare_call(
            trilateral_entry_matrix,
            tensor_average_matrix,
            query_key_matrix,
            focus_final_matrix,
        )
        packed = pack_call(alignment_embedding, coupling_embedding, coupling_logit_matrix, count)
        arrived = exchange(packed)
        other = across(arrived[:, -1], 1)
        projected = project_call(arrived, prepared[3])
        mixed, flanks = attend_call(arrived, other, projected, width, prepared[4], *prepared[1:3])
        flanks = exchange(flanks)
        flanks = flanks.reshape(chain_tally, -1)
        other = across(flanks, 1)
        final = spread_call(tensor_average_final)
        return pair_track(
            core.reshape(1),
            flanks,
            other,
            mixed,
            coupling_embedding,
            final,
            prepared,
            trilateral_exit_matrix,
            local_strands * tensor_depth,
        )

    rows = exchange(alignment_embedding).reshape(count, per_device, local_strands, depth)
    rows = rows.transpose(1, 0, 2, 3).reshape(per_device, total_res, depth)
    pair_norm = standardise_entries(coupling_embedding, -1).astype(jnp.bfloat16)
    bias_rows = jnp.einsum(
        "rnc,ch->hrn", pair_norm, coupling_logit_matrix, preferred_element_type=jnp.float32
    )
    bias = lax.all_gather(bias_rows, "res", axis=1, tiled=True)

    standard = standardise_entries(rows, -1).astype(jnp.bfloat16)
    projection = query_key_matrix.reshape(depth, 4, heads, width)
    mapped = jnp.einsum(
        "snc,cthd->tshnd", standard, projection[:, :3], preferred_element_type=jnp.float32
    ).astype(jnp.bfloat16)
    gate = jax.nn.sigmoid(
        jnp.einsum("snc,chd->shnd", standard, projection[:, 3], preferred_element_type=jnp.float32)
    )
    scores = (
        jnp.einsum("shid,shjd->shij", mapped[0], mapped[1], preferred_element_type=jnp.float32)
        * width ** (-0.5)
        + bias
    )
    weights = jnp.exp(scores - jnp.max(scores, axis=-1, keepdims=True))
    weights = (weights / jnp.sum(weights, axis=-1, keepdims=True)).astype(jnp.bfloat16)
    attended = jnp.einsum(
        "shij,shjd->shid", weights, mapped[2], preferred_element_type=jnp.float32
    ).astype(jnp.bfloat16)
    gated = (attended.astype(jnp.float32) * gate).astype(jnp.bfloat16)
    increment = jnp.einsum(
        "shnd,hdc->snc",
        gated,
        focus_final_matrix.reshape(heads, width, depth),
        preferred_element_type=jnp.float32,
    )
    mixed = (rows.astype(jnp.float32) + increment).astype(jnp.bfloat16)

    tensor_scaled = standardise_entries(mixed, -1).astype(jnp.bfloat16)
    flank = jnp.einsum(
        "snc,ctk->tsnk",
        tensor_scaled,
        tensor_average_matrix.reshape(depth, 2, tensor_depth),
        preferred_element_type=jnp.float32,
    ).astype(jnp.bfloat16)
    left = flank[0].reshape(per_device, count // 2, 2, local_strands * tensor_depth)
    left = left.transpose(1, 2, 0, 3)
    right = flank[1].reshape(per_device, 2, half // 8, 8, tensor_depth).transpose(1, 0, 2, 4, 3)
    right = right.reshape(2, per_device, tensor_depth * half)
    right = jnp.broadcast_to(right, (count // 2,) + right.shape)
    flanks = jnp.concatenate([left, right], axis=-1).reshape(count, per_device, -1)
    flanks = exchange(flanks)
    mixed_out = exchange(
        mixed.reshape(per_device, count, local_strands, depth).transpose(1, 0, 2, 3)
    ).reshape(chain_tally, local_strands, depth)

    flanks = flanks.reshape(chain_tally, -1)
    mine = flanks[:, local_strands * tensor_depth :]
    other = across(mine, 1)
    group = max(1, 128 // tensor_depth)
    final = tensor_average_final.reshape(tensor_depth, tensor_depth, pair_width)
    final = jnp.einsum("ab,cef->eacbf", jnp.eye(group, dtype=final.dtype), final)
    final = final.reshape(tensor_depth * group * tensor_depth, group * pair_width)
    left_all = flanks[:, : local_strands * tensor_depth]
    both = jnp.stack([mine, other])
    both = jnp.where(core == 0, both, both[::-1])
    both = both.reshape(2, chain_tally, half // 8, tensor_depth, 8)
    outer = jnp.einsum(
        "xsaej,sgm->gxajem",
        both,
        left_all.reshape(chain_tally, local_strands // group, group * tensor_depth),
        preferred_element_type=jnp.float32,
    ) * (1.0 / chain_tally)
    outer = outer.astype(jnp.bfloat16).reshape(local_strands // group, total_res, -1)
    opm = jnp.einsum("gjk,kn->gjn", outer, final, preferred_element_type=jnp.float32)
    opm = opm.reshape(local_strands // group, total_res, group, pair_width)
    opm = opm.transpose(0, 2, 1, 3).reshape(local_strands, total_res, pair_width)
    pair_mid = (coupling_embedding.astype(jnp.float32) + opm).astype(jnp.bfloat16)

    pair_tri = triangle(
        pair_mid, trilateral_entry_matrix[0], trilateral_exit_matrix[0], "xcik,ycjk->cxiyj"
    )
    coupling_refreshed = triangle(
        pair_tri, trilateral_entry_matrix[1], trilateral_exit_matrix[1], "xcki,xckj->cij"
    )
    return (mixed_out, coupling_refreshed)


def solution(mesh):
    return jax.shard_map(
        body,
        mesh=mesh,
        in_specs=(P("grp", "res", None), P("res", "grp", None), P(), P(), P(), P(), P(), P(), P()),
        out_specs=(P("grp", "res", None), P("res", "grp", None)),
        check_vma=False,
    )
```

```python
import math

import jax
import jax.numpy as jnp
from jax import lax
from jax.experimental import pallas as pl
from jax.experimental.pallas import tpu as pltpu
from jax.sharding import PartitionSpec as P


LOG2E = math.log2(math.e)


def standardise_entries(values_in, axis_num):
    values_in = values_in.astype(jnp.float32)
    centred = values_in - jnp.mean(values_in, axis=axis_num, keepdims=True)
    spread = jnp.mean(centred * centred, axis=axis_num, keepdims=True)
    return centred * lax.rsqrt(spread + 1e-05)


def exchange(blocks):
    return lax.all_to_all(blocks, "res", split_axis=0, concat_axis=0, tiled=True)


def across(values, bit):
    count = lax.axis_size("res")
    return lax.ppermute(values, "res", [(k, k ^ bit) for k in range(count)])


def params(megabytes=16):
    return pltpu.CompilerParams(vmem_limit_bytes=megabytes << 20)


def whole(count):
    return [pl.BlockSpec(memory_space=pltpu.VMEM)] * count


def lanes_norm(values):
    centred = values - jnp.mean(values, axis=-1, keepdims=True)
    spread = jnp.mean(centred * centred, axis=-1, keepdims=True)
    return centred * lax.rsqrt(spread + 1e-05)


def edges_in_turn(new_row, entry_ref, edges_ref, gate_ref):
    count, _, strands, share, lanes = edges_ref.shape
    width = count * share
    normed, mapped, gates = {}, {}, {}
    pairs = strands // 2
    for n in range(pairs + 2):
        if n < pairs:
            rows = [lanes_norm(new_row(2 * n + k)).astype(jnp.bfloat16) for k in range(2)]
            normed[n] = jnp.concatenate(rows)
        if 0 < n <= pairs:
            rows = normed.pop(n - 1)
            mapped[n - 1] = [
                lax.dot_general(
                    entry_ref[2 * side * width : 2 * (side + 1) * width],
                    rows,
                    (((1,), (1,)), ((), ())),
                    preferred_element_type=jnp.float32,
                )
                for side in range(2)
            ]
            gates[n - 1] = lax.dot_general(
                rows,
                entry_ref[4 * width :],
                (((1,), (1,)), ((), ())),
                preferred_element_type=jnp.float32,
            )
        if n > 1:
            gate = jax.nn.sigmoid(gates.pop(n - 2))
            for k in range(2):
                gate_ref[2 * n - 4 + k] = gate[k * lanes : (k + 1) * lanes]
            for side, both in enumerate(mapped.pop(n - 2)):
                edge = jax.nn.sigmoid(both[:width]) * both[width:]
                for k in range(2):
                    part = edge[:, k * lanes : (k + 1) * lanes].reshape(count, share, lanes)
                    edges_ref[:, side, 2 * n - 4 + k] = part.astype(jnp.bfloat16)


def product_kernel(incoming, arrived_ref, product_ref, left_ref, right_ref):
    count, _, strands, share, lanes = arrived_ref.shape
    rows = count * strands
    for side, ref in enumerate((left_ref, right_ref)):
        ref[...] = arrived_ref[:, side].astype(jnp.float32).reshape(rows * share, lanes)
    dims = (((0,), (0,)), ((), ())) if incoming else (((1,), (1,)), ((), ()))
    for ch in range(share):
        left = left_ref[pl.ds(ch, rows, stride=share), :].astype(jnp.bfloat16)
        right = right_ref[pl.ds(ch, rows, stride=share), :].astype(jnp.bfloat16)
        out = lax.dot_general(left, right, dims, preferred_element_type=jnp.float32)
        product_ref[:, ch] = out.reshape(count, strands, lanes).astype(jnp.bfloat16)


def product_call(arrived, incoming):
    count, _, strands, share, lanes = arrived.shape
    scratch = pltpu.VMEM((count * strands * share, lanes), jnp.float32)
    return pl.pallas_call(
        lambda *refs: product_kernel(incoming, *refs),
        out_shape=jax.ShapeDtypeStruct((count, share, strands, lanes), jnp.bfloat16),
        in_specs=whole(1),
        out_specs=pl.BlockSpec(memory_space=pltpu.VMEM),
        scratch_shapes=[scratch, scratch],
        compiler_params=params(),
        name="edge_product",
    )(arrived)


def exit_rows(which, gathered_ref, exit_ref, pair_ref, gate_ref, out_ref, spread_ref):
    count, share, strands, lanes = gathered_ref.shape
    width = count * share
    spread_ref[...] = gathered_ref[...].astype(jnp.float32).reshape(width * strands, lanes)

    def update(r):
        edges = spread_ref[pl.ds(r, width, stride=strands), :]
        centred = edges - jnp.mean(edges, axis=0, keepdims=True)
        spread = jnp.mean(centred * centred, axis=0, keepdims=True)
        normed = (centred * lax.rsqrt(spread + 1e-05)).astype(jnp.bfloat16)
        return lax.dot_general(
            normed, exit_ref[which], (((0,), (0,)), ((), ())), preferred_element_type=jnp.float32
        )

    ahead = 2
    updates = {r: update(r) for r in range(ahead)}

    def new_row(r):
        if r + ahead < strands:
            updates[r + ahead] = update(r + ahead)
        new = pair_ref[r].astype(jnp.float32) + gate_ref[r] * updates.pop(r)
        new = new.astype(jnp.bfloat16)
        out_ref[r] = new
        return new.astype(jnp.float32)

    return new_row


def exit_entry_kernel(
    gathered_ref,
    exit_ref,
    pair_ref,
    gate_ref,
    entry_ref,
    arrived_ref,
    out_ref,
    edges_ref,
    next_gate_ref,
    mixed_ref,
    spread_ref,
    sems,
):
    copies = [
        pltpu.make_async_copy(
            arrived_ref.at[:, 2 + k], mixed_ref.at[:, :, :, pl.ds(k * 128, 128)], sems.at[k]
        )
        for k in range(arrived_ref.shape[1] - 2)
    ]
    for copy in copies:
        copy.start()
    new_row = exit_rows(0, gathered_ref, exit_ref, pair_ref, gate_ref, out_ref, spread_ref)
    edges_in_turn(new_row, entry_ref.at[1], edges_ref, next_gate_ref)
    for copy in copies:
        copy.wait()


def exit_entry_call(gathered, weight, pair_prev, gate, entry, arrived):
    count, share, strands, lanes = gathered.shape
    parts = arrived.shape[1] - 2
    anywhere = pl.BlockSpec(memory_space=pl.ANY)
    return pl.pallas_call(
        exit_entry_kernel,
        out_shape=(
            jax.ShapeDtypeStruct(pair_prev.shape, jnp.bfloat16),
            jax.ShapeDtypeStruct((count, 2, strands, share, lanes), jnp.bfloat16),
            jax.ShapeDtypeStruct(pair_prev.shape, jnp.float32),
            jax.ShapeDtypeStruct((count, strands, share, parts * 128), jnp.bfloat16),
        ),
        in_specs=whole(5) + [anywhere],
        out_specs=tuple(whole(3)) + (pl.BlockSpec(memory_space=pltpu.HBM),),
        scratch_shapes=[
            pltpu.VMEM((count * share * strands, lanes), jnp.float32),
            pltpu.SemaphoreType.DMA((parts,)),
        ],
        compiler_params=params(),
        name="triangle_exit_entry",
    )(gathered, weight, pair_prev, gate, entry, arrived)


def exit_kernel(gathered_ref, exit_ref, pair_ref, gate_ref, out_ref, spread_ref):
    new_row = exit_rows(1, gathered_ref, exit_ref, pair_ref, gate_ref, out_ref, spread_ref)
    for r in range(pair_ref.shape[0]):
        new_row(r)


def exit_call(gathered, weight, pair_prev, gate):
    count, share, strands, lanes = gathered.shape
    return pl.pallas_call(
        exit_kernel,
        out_shape=jax.ShapeDtypeStruct(pair_prev.shape, jnp.bfloat16),
        in_specs=whole(4),
        out_specs=pl.BlockSpec(memory_space=pltpu.VMEM),
        scratch_shapes=[pltpu.VMEM((count * share * strands, lanes), jnp.float32)],
        compiler_params=params(),
        name="triangle_exit",
    )(gathered, weight, pair_prev, gate)


def half_product(flanks_ref, left, final_ref, outer_ref):
    chains, flat = left.shape
    depth = final_ref.shape[0] // 128
    span, blocks = 8 * depth, flat // 128
    half = (flanks_ref.shape[1] - flat) // depth
    for pair in range(half // 16):
        parts = []
        for jg in (2 * pair, 2 * pair + 1):
            part = lax.dot_general(
                flanks_ref[:, flat + jg * span : flat + (jg + 1) * span],
                left,
                (((0,), (0,)), ((), ())),
                preferred_element_type=jnp.float32,
            ) * (1.0 / chains)
            parts.append(part.reshape(depth, 8, flat))
        both = jnp.concatenate(parts, axis=1).astype(jnp.bfloat16)
        for ig in range(blocks):
            at = ig * half + pair * 16
            for e in range(depth):
                outer_ref[at : at + 16, e * 128 : (e + 1) * 128] = both[e, :, ig * 128 : (ig + 1) * 128]
    return jnp.dot(outer_ref[...], final_ref[...], preferred_element_type=jnp.float32)


def own_kernel(flat, flanks_ref, final_ref, product_ref, outer_ref):
    product_ref[...] = half_product(flanks_ref, flanks_ref[:, :flat], final_ref, outer_ref)


def own_call(flanks, final, flat, half):
    rows = flat // 128 * half
    return pl.pallas_call(
        lambda *refs: own_kernel(flat, *refs),
        out_shape=jax.ShapeDtypeStruct((rows, final.shape[1]), jnp.float32),
        in_specs=whole(2),
        out_specs=pl.BlockSpec(memory_space=pltpu.VMEM),
        scratch_shapes=[pltpu.VMEM((rows, final.shape[0]), jnp.bfloat16)],
        compiler_params=params(24),
        name="outer_product_own",
    )(flanks, final)


def opm_kernel(
    flat,
    core_ref,
    flanks_ref,
    other_ref,
    own_ref,
    mixed_ref,
    coupling_ref,
    final_ref,
    entry_ref,
    pair_ref,
    edges_ref,
    gate_ref,
    outer_ref,
):
    _, total_res, width = coupling_ref.shape
    groups = final_ref.shape[1] // width
    half = total_res // 2
    for k in range(edges_ref.shape[1] - 2):
        edges_ref[:, 2 + k] = mixed_ref[:, :, :, k * 128 : (k + 1) * 128]
    first = core_ref[0] == 0
    product = half_product(other_ref, flanks_ref[:, :flat], final_ref, outer_ref)

    def new_row(r):
        ig, i4 = divmod(r, groups)
        rows, lanes = slice(ig * half, (ig + 1) * half), slice(i4 * width, (i4 + 1) * width)
        mine, theirs = own_ref[rows, lanes], product[rows, lanes]
        piece = jnp.concatenate([jnp.where(first, mine, theirs), jnp.where(first, theirs, mine)])
        new = (coupling_ref[r].astype(jnp.float32) + piece).astype(jnp.bfloat16)
        pair_ref[r] = new
        return new.astype(jnp.float32)

    edges_in_turn(new_row, entry_ref.at[0], edges_ref, gate_ref)


def opm_call(core, flanks, other, own, mixed, coupling, final, entry, flat):
    count, _, _, depth = mixed.shape
    strands, total_res, width = coupling.shape
    share = width // count
    return pl.pallas_call(
        lambda *refs: opm_kernel(flat, *refs),
        out_shape=(
            jax.ShapeDtypeStruct(coupling.shape, jnp.bfloat16),
            jax.ShapeDtypeStruct(
                (count, 2 + depth // 128, strands, share, total_res), jnp.bfloat16
            ),
            jax.ShapeDtypeStruct(coupling.shape, jnp.float32),
        ),
        in_specs=[pl.BlockSpec(memory_space=pltpu.SMEM)] + whole(7),
        out_specs=tuple(whole(3)),
        scratch_shapes=[pltpu.VMEM((own.shape[0], final.shape[0]), jnp.bfloat16)],
        compiler_params=params(24),
        name="outer_product_entry",
    )(core, flanks, other, own, mixed, coupling, final, entry)


def spread_kernel(final_ref, block_ref, wide_ref):
    width = final_ref.shape[1]
    depth = block_ref.shape[0] // 128
    groups = 128 // depth
    wide_ref[...] = final_ref[...].astype(jnp.float32)
    block_ref[...] = jnp.zeros(block_ref.shape, block_ref.dtype)
    for e in range(depth):
        piece = wide_ref[pl.ds(e, depth, stride=depth), :].astype(jnp.bfloat16)
        for g in range(groups):
            at = e * 128 + g * depth
            block_ref[at : at + depth, g * width : (g + 1) * width] = piece


def spread_call(final):
    depth = math.isqrt(final.shape[0])
    width = final.shape[1]
    return pl.pallas_call(
        spread_kernel,
        out_shape=jax.ShapeDtypeStruct((depth * 128, 128 // depth * width), jnp.bfloat16),
        in_specs=whole(1),
        out_specs=pl.BlockSpec(memory_space=pltpu.VMEM),
        scratch_shapes=[pltpu.VMEM(final.shape, jnp.float32)],
        compiler_params=params(),
        name="spread_weight",
    )(final)


def prepare_kernel(
    entry_ref,
    average_ref,
    project_ref,
    focus_ref,
    sides_ref,
    left_ref,
    right_ref,
    turned_ref,
    near_focus_ref,
):
    near_focus_ref[...] = focus_ref[...]
    turned_ref[...] = project_ref[...].astype(jnp.float32).T.astype(jnp.bfloat16)
    channels = average_ref.shape[1] // 2
    for ref, first, lane_of in (
        (left_ref, 0, lambda ch, g, size: g * channels + ch),
        (right_ref, channels, lambda ch, g, size: ch * size + g),
    ):
        size, _, lanes = ref.shape
        for g in range(size):
            ch = lax.broadcasted_iota(jnp.int32, (2 * channels, lanes), 0) - first
            lane = lax.broadcasted_iota(jnp.int32, (2 * channels, lanes), 1)
            chosen = (lane_of(ch, g, size) == lane) & (ch >= 0) & (ch < channels)
            placed = jnp.dot(
                average_ref[...],
                jnp.where(chosen, 1.0, 0.0).astype(jnp.bfloat16),
                preferred_element_type=jnp.float32,
            )
            ref[g] = placed.astype(jnp.bfloat16)
    for d in range(2):
        sides_ref[d] = entry_ref[d].astype(jnp.float32).T.astype(jnp.bfloat16)


def prepare_call(entries, average, project, focus):
    depth = average.shape[1] // 2
    width = entries.shape[1]
    return pl.pallas_call(
        prepare_kernel,
        out_shape=(
            jax.ShapeDtypeStruct((2, 5 * width, width), jnp.bfloat16),
            jax.ShapeDtypeStruct((128 // depth, average.shape[0], 128), jnp.bfloat16),
            jax.ShapeDtypeStruct((8, average.shape[0], 8 * depth), jnp.bfloat16),
            jax.ShapeDtypeStruct(project.shape[::-1], jnp.bfloat16),
            jax.ShapeDtypeStruct(focus.shape, jnp.bfloat16),
        ),
        in_specs=whole(4),
        out_specs=tuple(whole(5)),
        compiler_params=params(),
        name="prepare_weights",
    )(entries, average, project, focus)


def pack_kernel(
    msa_ref, pair_ref, weight_ref, out_ref, own_ref, rows_ref, logit_ref, term_ref, in_sems, out_sems
):
    count, parts = out_ref.shape[:2]
    loads = [
        pltpu.make_async_copy(pair_ref, rows_ref, in_sems.at[0]),
        pltpu.make_async_copy(weight_ref, logit_ref, in_sems.at[1]),
    ]
    own = pltpu.make_async_copy(msa_ref, own_ref, in_sems.at[2])
    stores = [
        pltpu.make_async_copy(
            own_ref.at[:, :, :, pl.ds(k * 128, 128)], out_ref.at[:, k], out_sems.at[count + k]
        )
        for k in range(parts - 1)
    ]
    for copy in loads + [own]:
        copy.start()
    for copy in loads:
        copy.wait()
    for r in range(rows_ref.shape[0]):
        if r == 1:
            own.wait()
            for copy in stores:
                copy.start()
        normed = lanes_norm(rows_ref[r].astype(jnp.float32)).astype(jnp.bfloat16)
        bias = lax.dot_general(
            logit_ref[...], normed, (((1,), (1,)), ((), ())), preferred_element_type=jnp.float32
        )
        upper = bias.astype(jnp.bfloat16)
        term_ref[0, r] = upper
        term_ref[1, r] = (bias - upper.astype(jnp.float32)).astype(jnp.bfloat16)
    terms = [
        pltpu.make_async_copy(term_ref.at[d % 2], out_ref.at[d, parts - 1], out_sems.at[d])
        for d in range(count)
    ]
    for copy in terms:
        copy.start()
    for copy in stores + terms:
        copy.wait()


def pack_call(msa, pair, weight, count):
    chains, strands, depth = msa.shape
    parts, heads = depth // 128, weight.shape[1]
    anywhere = pl.BlockSpec(memory_space=pltpu.HBM)
    return pl.pallas_call(
        pack_kernel,
        out_shape=jax.ShapeDtypeStruct(
            (count, parts + 1, chains // count, strands, 128), jnp.bfloat16
        ),
        in_specs=[anywhere] * 3,
        out_specs=anywhere,
        scratch_shapes=[
            pltpu.VMEM((count, chains // count, strands, depth), jnp.bfloat16),
            pltpu.VMEM(pair.shape, jnp.bfloat16),
            pltpu.VMEM((heads, pair.shape[2]), jnp.bfloat16),
            pltpu.VMEM((2, strands, heads, pair.shape[1]), jnp.bfloat16),
            pltpu.SemaphoreType.DMA((3,)),
            pltpu.SemaphoreType.DMA((count + parts,)),
        ],
        compiler_params=params(),
        name="pack_rows",
    )(
        *(
            pltpu.with_memory_space_constraint(operand, pltpu.HBM)
            for operand in (msa.reshape(count, chains // count, strands, depth), pair, weight.T)
        )
    )


def arrived_rows(arrived_ref, s):
    count, parts, _, strands, lanes = arrived_ref.shape
    pieces = [
        arrived_ref[:, k, s].astype(jnp.float32).reshape(count * strands, lanes)
        for k in range(parts - 1)
    ]
    return jnp.concatenate(pieces, axis=-1)


def project_kernel(arrived_ref, weight_ref, query_ref, key_ref, value_ref, gate_ref):
    inner = query_ref.shape[1]
    total_res = query_ref.shape[2]
    for s in range(0, query_ref.shape[0], 2):
        rows = jnp.concatenate([arrived_rows(arrived_ref, s + k) for k in range(2)])
        mapped = lax.dot_general(
            weight_ref[...],
            lanes_norm(rows).astype(jnp.bfloat16),
            (((1,), (1,)), ((), ())),
            preferred_element_type=jnp.float32,
        )
        for k in range(2):
            part = mapped[:, k * total_res : (k + 1) * total_res]
            for block, ref in enumerate((query_ref, key_ref, value_ref)):
                ref[s + k] = part[block * inner : (block + 1) * inner].astype(jnp.bfloat16)
            gate_ref[s + k] = jax.nn.sigmoid(part[3 * inner :])


def project_call(arrived, weight):
    count, _, chains, strands, _ = arrived.shape
    turned = (chains, weight.shape[0] // 4, count * strands)
    half = jax.ShapeDtypeStruct(turned, jnp.bfloat16)
    return pl.pallas_call(
        project_kernel,
        out_shape=(half, half, half, jax.ShapeDtypeStruct(turned, jnp.float32)),
        in_specs=whole(2),
        out_specs=tuple(whole(4)),
        compiler_params=params(),
        name="project_rows",
    )(arrived, weight)


def attend_kernel(
    width,
    arrived_ref,
    other_ref,
    query_ref,
    key_ref,
    value_ref,
    gate_ref,
    final_ref,
    left_ref,
    right_ref,
    mixed_ref,
    flanks_ref,
    bias_ref,
    turned_ref,
    scaled_ref,
):
    count, chains, strands, depth = mixed_ref.shape
    inner, total_res = query_ref.shape[1:]
    heads = inner // width
    mine = arrived_ref[:, arrived_ref.shape[1] - 1].astype(jnp.float32)
    bias = mine + other_ref[...].astype(jnp.float32)
    bias_ref[...] = bias.reshape(total_res * heads, total_res)
    for h in range(heads):
        turned_ref[h] = bias_ref[pl.ds(h, total_res, stride=heads), :].T * LOG2E
    scale = width ** (-0.5) * LOG2E

    def score(s, h):
        at = slice(h * width, (h + 1) * width)
        return lax.dot_general(
            key_ref[s, at],
            query_ref[s, at],
            (((0,), (0,)), ((), ())),
            preferred_element_type=jnp.float32,
        )

    def weigh(scores, h):
        scores = scores * scale + turned_ref[h]
        weights = jnp.exp2(scores - jnp.max(scores, axis=0, keepdims=True))
        total = jnp.sum(weights, axis=0, keepdims=True)
        return (weights * (1.0 / total)).astype(jnp.bfloat16)

    def finish(s, attended):
        attended = jnp.concatenate(attended).astype(jnp.bfloat16).astype(jnp.float32)
        gated = (attended * gate_ref[s]).astype(jnp.bfloat16)
        increment = lax.dot_general(
            gated, final_ref[...], (((0,), (0,)), ((), ())), preferred_element_type=jnp.float32
        )
        mixed = (arrived_rows(arrived_ref, s) + increment).astype(jnp.bfloat16)
        mixed = mixed.astype(jnp.float32)
        normed = lanes_norm(mixed)
        for k in range(depth // 128):
            scaled_ref[k, pl.ds(s, total_res, stride=chains), :] = normed[:, k * 128 : (k + 1) * 128]
        mixed_ref[:, s] = mixed.reshape(count, strands, depth).astype(jnp.bfloat16)

    steps = [(s, h) for s in range(chains) for h in range(heads)]
    ahead, lag = 4, 3
    scores = {n: score(*steps[n]) for n in range(ahead)}
    weighed, attended = {}, []
    for n in range(len(steps) + lag):
        if n + ahead < len(steps):
            scores[n + ahead] = score(*steps[n + ahead])
        if n < len(steps):
            weighed[n] = weigh(scores.pop(n), steps[n][1])
        if n >= lag:
            s, h = steps[n - lag]
            attended.append(
                jnp.dot(
                    value_ref[s, h * width : (h + 1) * width],
                    weighed.pop(n - lag),
                    preferred_element_type=jnp.float32,
                )
            )
            if h + 1 == heads:
                finish(s, attended)
                attended = []

    scaled = jnp.concatenate([scaled_ref[k] for k in range(depth // 128)], axis=-1)
    scaled = scaled.reshape(total_res, chains, depth)

    def side(weights_ref):
        group, _, lanes = weights_ref.shape
        total = None
        grouped = scaled.reshape(total_res // group, group, chains, depth)
        for g in range(group):
            part = grouped[:, g].reshape(total_res // group * chains, depth).astype(jnp.bfloat16)
            out = jnp.dot(part, weights_ref[g], preferred_element_type=jnp.float32)
            total = out if total is None else total + out
        return total.reshape(total_res // group, chains, lanes).astype(jnp.bfloat16)

    left, right = side(left_ref), side(right_ref)
    lefts, rights = left.shape[0] // count, right.shape[0] // 2
    for d in range(count):
        at = 0
        for k in range(lefts):
            flanks_ref[d, :, at : at + left.shape[2]] = left[d * lefts + k]
            at += left.shape[2]
        for k in range(rights):
            flanks_ref[d, :, at : at + right.shape[2]] = right[(d % 2) * rights + k]
            at += right.shape[2]


def attend_call(arrived, other, projected, width, final, left, right):
    count, parts, chains, strands, _ = arrived.shape
    inner, total_res = projected[0].shape[1:]
    depth, heads = (parts - 1) * 128, inner // width
    lanes = strands // left.shape[0] * left.shape[2] + total_res // 2 // right.shape[0] * right.shape[2]
    return pl.pallas_call(
        lambda *refs: attend_kernel(width, *refs),
        out_shape=(
            jax.ShapeDtypeStruct((count, chains, strands, depth), jnp.bfloat16),
            jax.ShapeDtypeStruct((count, chains, lanes), jnp.bfloat16),
        ),
        in_specs=whole(9),
        out_specs=tuple(whole(2)),
        scratch_shapes=[
            pltpu.VMEM((total_res * heads, total_res), jnp.float32),
            pltpu.VMEM((heads, total_res, total_res), jnp.float32),
            pltpu.VMEM((depth // 128, total_res * chains, 128), jnp.float32),
        ],
        compiler_params=params(),
        name="attend_rows",
    )(arrived, other, *projected, final, left, right)


def pair_track(core, flanks, other, mixed, coupling, final, prepared, exits, flat):
    sides = prepared[0]
    own = own_call(flanks, final, flat, coupling.shape[1] // 2)
    pair, edges, gate = opm_call(core, flanks, other, own, mixed, coupling, final, sides, flat)
    for d in range(2):
        arrived = exchange(edges)
        product = product_call(arrived, d == 1)
        gathered = exchange(product)
        if d == 0:
            pair, edges, gate, returned = exit_entry_call(
                gathered, exits, pair, gate, sides, arrived
            )
        else:
            pair = exit_call(gathered, exits, pair, gate)
    return returned.reshape((-1,) + mixed.shape[2:]), pair


def triangle(pair_prev, weight_in, weight_out, contraction):
    local_strands, total_res, pair_width = pair_prev.shape
    count = lax.axis_size("res")
    share = pair_width // count
    normed = standardise_entries(pair_prev, -1).astype(jnp.bfloat16)
    five = weight_in.reshape(pair_width, 5, pair_width)
    paired = five[:, :4].reshape(pair_width, 2, 2, count, share).transpose(0, 2, 3, 1, 4)
    mapped = jnp.einsum(
        "rnc,ctwsk->twskrn", normed, paired, preferred_element_type=jnp.float32
    )
    edges = (jax.nn.sigmoid(mapped[0]) * mapped[1]).astype(jnp.bfloat16)
    arrived = exchange(edges)
    gate_pair = jax.nn.sigmoid(
        jnp.einsum("rnc,cf->rnf", normed, five[:, 4], preferred_element_type=jnp.float32)
    )
    product = jnp.einsum(
        contraction, arrived[:, 0], arrived[:, 1], preferred_element_type=jnp.float32
    ).astype(jnp.bfloat16)
    product = product.reshape(share, count, local_strands, total_res).transpose(1, 0, 2, 3)
    gathered = exchange(product).reshape(pair_width, local_strands, total_res)
    edge_norm = standardise_entries(gathered, 0).astype(jnp.bfloat16)
    update = jnp.einsum("crn,cf->rnf", edge_norm, weight_out, preferred_element_type=jnp.float32)
    return (pair_prev.astype(jnp.float32) + gate_pair * update).astype(jnp.bfloat16)


def body(
    alignment_embedding,
    coupling_embedding,
    query_key_matrix,
    coupling_logit_matrix,
    focus_final_matrix,
    tensor_average_matrix,
    tensor_average_final,
    trilateral_entry_matrix,
    trilateral_exit_matrix,
):
    chain_tally, local_strands, depth = alignment_embedding.shape
    total_res, pair_width = coupling_embedding.shape[1:]
    count = lax.axis_size("res")
    core = lax.axis_index("res") % 2
    heads = coupling_logit_matrix.shape[1]
    width = query_key_matrix.shape[1] // (4 * heads)
    per_device = chain_tally // count
    tensor_depth = tensor_average_matrix.shape[1] // 2
    half = total_res // 2

    fits = (
        pair_width == 128
        and pair_width % (8 * count) == 0
        and count & (count - 1) == 0
        and total_res == 128
        and local_strands == 8
        and per_device == 8
        and heads == 8
        and heads * width == depth
        and depth % 128 == 0
        and tensor_depth == 32
    )
    if fits:
        prepared = prepare_call(
            trilateral_entry_matrix,
            tensor_average_matrix,
            query_key_matrix,
            focus_final_matrix,
        )
        packed = pack_call(alignment_embedding, coupling_embedding, coupling_logit_matrix, count)
        arrived = exchange(packed)
        other = across(arrived[:, -1], 1)
        projected = project_call(arrived, prepared[3])
        mixed, flanks = attend_call(arrived, other, projected, width, prepared[4], *prepared[1:3])
        flanks = exchange(flanks)
        flanks = flanks.reshape(chain_tally, -1)
        other = across(flanks, 1)
        final = spread_call(tensor_average_final)
        return pair_track(
            core.reshape(1),
            flanks,
            other,
            mixed,
            coupling_embedding,
            final,
            prepared,
            trilateral_exit_matrix,
            local_strands * tensor_depth,
        )

    rows = exchange(alignment_embedding).reshape(count, per_device, local_strands, depth)
    rows = rows.transpose(1, 0, 2, 3).reshape(per_device, total_res, depth)
    pair_norm = standardise_entries(coupling_embedding, -1).astype(jnp.bfloat16)
    bias_rows = jnp.einsum(
        "rnc,ch->hrn", pair_norm, coupling_logit_matrix, preferred_element_type=jnp.float32
    )
    bias = lax.all_gather(bias_rows, "res", axis=1, tiled=True)

    standard = standardise_entries(rows, -1).astype(jnp.bfloat16)
    projection = query_key_matrix.reshape(depth, 4, heads, width)
    mapped = jnp.einsum(
        "snc,cthd->tshnd", standard, projection[:, :3], preferred_element_type=jnp.float32
    ).astype(jnp.bfloat16)
    gate = jax.nn.sigmoid(
        jnp.einsum("snc,chd->shnd", standard, projection[:, 3], preferred_element_type=jnp.float32)
    )
    scores = (
        jnp.einsum("shid,shjd->shij", mapped[0], mapped[1], preferred_element_type=jnp.float32)
        * width ** (-0.5)
        + bias
    )
    weights = jnp.exp(scores - jnp.max(scores, axis=-1, keepdims=True))
    weights = (weights / jnp.sum(weights, axis=-1, keepdims=True)).astype(jnp.bfloat16)
    attended = jnp.einsum(
        "shij,shjd->shid", weights, mapped[2], preferred_element_type=jnp.float32
    ).astype(jnp.bfloat16)
    gated = (attended.astype(jnp.float32) * gate).astype(jnp.bfloat16)
    increment = jnp.einsum(
        "shnd,hdc->snc",
        gated,
        focus_final_matrix.reshape(heads, width, depth),
        preferred_element_type=jnp.float32,
    )
    mixed = (rows.astype(jnp.float32) + increment).astype(jnp.bfloat16)

    tensor_scaled = standardise_entries(mixed, -1).astype(jnp.bfloat16)
    flank = jnp.einsum(
        "snc,ctk->tsnk",
        tensor_scaled,
        tensor_average_matrix.reshape(depth, 2, tensor_depth),
        preferred_element_type=jnp.float32,
    ).astype(jnp.bfloat16)
    left = flank[0].reshape(per_device, count // 2, 2, local_strands * tensor_depth)
    left = left.transpose(1, 2, 0, 3)
    right = flank[1].reshape(per_device, 2, half // 8, 8, tensor_depth).transpose(1, 0, 2, 4, 3)
    right = right.reshape(2, per_device, tensor_depth * half)
    right = jnp.broadcast_to(right, (count // 2,) + right.shape)
    flanks = jnp.concatenate([left, right], axis=-1).reshape(count, per_device, -1)
    flanks = exchange(flanks)
    mixed_out = exchange(
        mixed.reshape(per_device, count, local_strands, depth).transpose(1, 0, 2, 3)
    ).reshape(chain_tally, local_strands, depth)

    flanks = flanks.reshape(chain_tally, -1)
    mine = flanks[:, local_strands * tensor_depth :]
    other = across(mine, 1)
    group = max(1, 128 // tensor_depth)
    final = tensor_average_final.reshape(tensor_depth, tensor_depth, pair_width)
    final = jnp.einsum("ab,cef->eacbf", jnp.eye(group, dtype=final.dtype), final)
    final = final.reshape(tensor_depth * group * tensor_depth, group * pair_width)
    left_all = flanks[:, : local_strands * tensor_depth]
    both = jnp.stack([mine, other])
    both = jnp.where(core == 0, both, both[::-1])
    both = both.reshape(2, chain_tally, half // 8, tensor_depth, 8)
    outer = jnp.einsum(
        "xsaej,sgm->gxajem",
        both,
        left_all.reshape(chain_tally, local_strands // group, group * tensor_depth),
        preferred_element_type=jnp.float32,
    ) * (1.0 / chain_tally)
    outer = outer.astype(jnp.bfloat16).reshape(local_strands // group, total_res, -1)
    opm = jnp.einsum("gjk,kn->gjn", outer, final, preferred_element_type=jnp.float32)
    opm = opm.reshape(local_strands // group, total_res, group, pair_width)
    opm = opm.transpose(0, 2, 1, 3).reshape(local_strands, total_res, pair_width)
    pair_mid = (coupling_embedding.astype(jnp.float32) + opm).astype(jnp.bfloat16)

    pair_tri = triangle(
        pair_mid, trilateral_entry_matrix[0], trilateral_exit_matrix[0], "xcik,ycjk->cxiyj"
    )
    coupling_refreshed = triangle(
        pair_tri, trilateral_entry_matrix[1], trilateral_exit_matrix[1], "xcki,xckj->cij"
    )
    return (mixed_out, coupling_refreshed)


def solution(mesh):
    return jax.shard_map(
        body,
        mesh=mesh,
        in_specs=(P("grp", "res", None), P("res", "grp", None), P(), P(), P(), P(), P(), P(), P()),
        out_specs=(P("grp", "res", None), P("res", "grp", None)),
        check_vma=False,
    )
```

```python
import math

import jax
import jax.numpy as jnp
from jax import lax
from jax.experimental import pallas as pl
from jax.experimental.pallas import tpu as pltpu
from jax.sharding import PartitionSpec as P


LOG2E = math.log2(math.e)


def standardise_entries(values_in, axis_num):
    values_in = values_in.astype(jnp.float32)
    centred = values_in - jnp.mean(values_in, axis=axis_num, keepdims=True)
    spread = jnp.mean(centred * centred, axis=axis_num, keepdims=True)
    return centred * lax.rsqrt(spread + 1e-05)


def exchange(blocks):
    return lax.all_to_all(blocks, "res", split_axis=0, concat_axis=0, tiled=True)


def across(values, bit):
    count = lax.axis_size("res")
    return lax.ppermute(values, "res", [(k, k ^ bit) for k in range(count)])


def params(megabytes=16):
    return pltpu.CompilerParams(vmem_limit_bytes=megabytes << 20)


def whole(count):
    return [pl.BlockSpec(memory_space=pltpu.VMEM)] * count


def lanes_norm(values):
    centred = values - jnp.mean(values, axis=-1, keepdims=True)
    spread = jnp.mean(centred * centred, axis=-1, keepdims=True)
    return centred * lax.rsqrt(spread + 1e-05)


def edges_in_turn(new_row, entry_ref, edges_ref, gate_ref):
    count, _, strands, share, lanes = edges_ref.shape
    width = count * share
    normed, mapped, gates = {}, {}, {}
    pairs = strands // 2
    for n in range(pairs + 2):
        if n < pairs:
            rows = [lanes_norm(new_row(2 * n + k)).astype(jnp.bfloat16) for k in range(2)]
            normed[n] = jnp.concatenate(rows)
        if 0 < n <= pairs:
            rows = normed.pop(n - 1)
            mapped[n - 1] = [
                lax.dot_general(
                    entry_ref[2 * side * width : 2 * (side + 1) * width],
                    rows,
                    (((1,), (1,)), ((), ())),
                    preferred_element_type=jnp.float32,
                )
                for side in range(2)
            ]
            gates[n - 1] = lax.dot_general(
                rows,
                entry_ref[4 * width :],
                (((1,), (1,)), ((), ())),
                preferred_element_type=jnp.float32,
            )
        if n > 1:
            gate = jax.nn.sigmoid(gates.pop(n - 2))
            for k in range(2):
                gate_ref[2 * n - 4 + k] = gate[k * lanes : (k + 1) * lanes]
            for side, both in enumerate(mapped.pop(n - 2)):
                edge = jax.nn.sigmoid(both[:width]) * both[width:]
                for k in range(2):
                    part = edge[:, k * lanes : (k + 1) * lanes].reshape(count, share, lanes)
                    edges_ref[:, side, 2 * n - 4 + k] = part.astype(jnp.bfloat16)


def product_kernel(incoming, arrived_ref, product_ref, left_ref, right_ref):
    count, _, strands, share, lanes = arrived_ref.shape
    rows = count * strands
    for side, ref in enumerate((left_ref, right_ref)):
        ref[...] = arrived_ref[:, side].astype(jnp.float32).reshape(rows * share, lanes)
    dims = (((0,), (0,)), ((), ())) if incoming else (((1,), (1,)), ((), ()))
    for ch in range(share):
        left = left_ref[pl.ds(ch, rows, stride=share), :].astype(jnp.bfloat16)
        right = right_ref[pl.ds(ch, rows, stride=share), :].astype(jnp.bfloat16)
        out = lax.dot_general(left, right, dims, preferred_element_type=jnp.float32)
        product_ref[:, ch] = out.reshape(count, strands, lanes).astype(jnp.bfloat16)


def product_call(arrived, incoming):
    count, _, strands, share, lanes = arrived.shape
    scratch = pltpu.VMEM((count * strands * share, lanes), jnp.float32)
    return pl.pallas_call(
        lambda *refs: product_kernel(incoming, *refs),
        out_shape=jax.ShapeDtypeStruct((count, share, strands, lanes), jnp.bfloat16),
        in_specs=whole(1),
        out_specs=pl.BlockSpec(memory_space=pltpu.VMEM),
        scratch_shapes=[scratch, scratch],
        compiler_params=params(),
        name="edge_product",
    )(arrived)


def exit_rows(which, gathered_ref, exit_ref, pair_ref, gate_ref, out_ref, spread_ref):
    count, share, strands, lanes = gathered_ref.shape
    width = count * share
    spread_ref[...] = gathered_ref[...].astype(jnp.float32).reshape(width * strands, lanes)

    def update(r):
        edges = spread_ref[pl.ds(r, width, stride=strands), :]
        centred = edges - jnp.mean(edges, axis=0, keepdims=True)
        spread = jnp.mean(centred * centred, axis=0, keepdims=True)
        normed = (centred * lax.rsqrt(spread + 1e-05)).astype(jnp.bfloat16)
        return lax.dot_general(
            normed, exit_ref[which], (((0,), (0,)), ((), ())), preferred_element_type=jnp.float32
        )

    ahead = 2
    updates = {r: update(r) for r in range(ahead)}

    def new_row(r):
        if r + ahead < strands:
            updates[r + ahead] = update(r + ahead)
        new = pair_ref[r].astype(jnp.float32) + gate_ref[r] * updates.pop(r)
        new = new.astype(jnp.bfloat16)
        out_ref[r] = new
        return new.astype(jnp.float32)

    return new_row


def exit_entry_kernel(
    gathered_ref,
    exit_ref,
    pair_ref,
    gate_ref,
    entry_ref,
    arrived_ref,
    out_ref,
    edges_ref,
    next_gate_ref,
    mixed_ref,
    spread_ref,
    sems,
):
    copies = [
        pltpu.make_async_copy(
            arrived_ref.at[:, 2 + k], mixed_ref.at[:, :, :, pl.ds(k * 128, 128)], sems.at[k]
        )
        for k in range(arrived_ref.shape[1] - 2)
    ]
    for copy in copies:
        copy.start()
    new_row = exit_rows(0, gathered_ref, exit_ref, pair_ref, gate_ref, out_ref, spread_ref)
    edges_in_turn(new_row, entry_ref.at[1], edges_ref, next_gate_ref)
    for copy in copies:
        copy.wait()


def exit_entry_call(gathered, weight, pair_prev, gate, entry, arrived):
    count, share, strands, lanes = gathered.shape
    parts = arrived.shape[1] - 2
    anywhere = pl.BlockSpec(memory_space=pl.ANY)
    return pl.pallas_call(
        exit_entry_kernel,
        out_shape=(
            jax.ShapeDtypeStruct(pair_prev.shape, jnp.bfloat16),
            jax.ShapeDtypeStruct((count, 2, strands, share, lanes), jnp.bfloat16),
            jax.ShapeDtypeStruct(pair_prev.shape, jnp.float32),
            jax.ShapeDtypeStruct((count, strands, share, parts * 128), jnp.bfloat16),
        ),
        in_specs=whole(5) + [anywhere],
        out_specs=tuple(whole(3)) + (pl.BlockSpec(memory_space=pltpu.HBM),),
        scratch_shapes=[
            pltpu.VMEM((count * share * strands, lanes), jnp.float32),
            pltpu.SemaphoreType.DMA((parts,)),
        ],
        compiler_params=params(),
        name="triangle_exit_entry",
    )(gathered, weight, pair_prev, gate, entry, arrived)


def exit_kernel(gathered_ref, exit_ref, pair_ref, gate_ref, out_ref, near_ref, spread_ref, sems):
    new_row = exit_rows(1, gathered_ref, exit_ref, pair_ref, gate_ref, near_ref, spread_ref)
    copies = []
    for r in range(pair_ref.shape[0]):
        new_row(r)
        if r % 2:
            at = pl.ds(r - 1, 2)
            copies.append(pltpu.make_async_copy(near_ref.at[at], out_ref.at[at], sems.at[r // 2]))
            copies[-1].start()
    for copy in copies:
        copy.wait()


def exit_call(gathered, weight, pair_prev, gate):
    count, share, strands, lanes = gathered.shape
    return pl.pallas_call(
        exit_kernel,
        out_shape=jax.ShapeDtypeStruct(pair_prev.shape, jnp.bfloat16),
        in_specs=whole(4),
        out_specs=pl.BlockSpec(memory_space=pltpu.HBM),
        scratch_shapes=[
            pltpu.VMEM(pair_prev.shape, jnp.bfloat16),
            pltpu.VMEM((count * share * strands, lanes), jnp.float32),
            pltpu.SemaphoreType.DMA((strands // 2,)),
        ],
        compiler_params=params(),
        name="triangle_exit",
    )(gathered, weight, pair_prev, gate)


def half_product(flanks_ref, left, final_ref, outer_ref):
    chains, flat = left.shape
    depth = final_ref.shape[0] // 128
    span, blocks = 8 * depth, flat // 128
    half = (flanks_ref.shape[1] - flat) // depth
    for pair in range(half // 16):
        parts = []
        for jg in (2 * pair, 2 * pair + 1):
            part = lax.dot_general(
                flanks_ref[:, flat + jg * span : flat + (jg + 1) * span],
                left,
                (((0,), (0,)), ((), ())),
                preferred_element_type=jnp.float32,
            ) * (1.0 / chains)
            parts.append(part.reshape(depth, 8, flat))
        both = jnp.concatenate(parts, axis=1).astype(jnp.bfloat16)
        for ig in range(blocks):
            at = ig * half + pair * 16
            for e in range(depth):
                outer_ref[at : at + 16, e * 128 : (e + 1) * 128] = both[e, :, ig * 128 : (ig + 1) * 128]
    return jnp.dot(outer_ref[...], final_ref[...], preferred_element_type=jnp.float32)


def own_kernel(flat, flanks_ref, final_ref, product_ref, outer_ref):
    product_ref[...] = half_product(flanks_ref, flanks_ref[:, :flat], final_ref, outer_ref)


def own_call(flanks, final, flat, half):
    rows = flat // 128 * half
    return pl.pallas_call(
        lambda *refs: own_kernel(flat, *refs),
        out_shape=jax.ShapeDtypeStruct((rows, final.shape[1]), jnp.float32),
        in_specs=whole(2),
        out_specs=pl.BlockSpec(memory_space=pltpu.VMEM),
        scratch_shapes=[pltpu.VMEM((rows, final.shape[0]), jnp.bfloat16)],
        compiler_params=params(24),
        name="outer_product_own",
    )(flanks, final)


def opm_kernel(
    flat,
    core_ref,
    flanks_ref,
    other_ref,
    own_ref,
    mixed_ref,
    coupling_ref,
    final_ref,
    entry_ref,
    pair_ref,
    edges_ref,
    gate_ref,
    outer_ref,
    sems,
):
    _, total_res, width = coupling_ref.shape
    groups = final_ref.shape[1] // width
    half = total_res // 2
    copies = [
        pltpu.make_async_copy(
            mixed_ref.at[:, :, :, pl.ds(k * 128, 128)], edges_ref.at[:, 2 + k], sems.at[k]
        )
        for k in range(edges_ref.shape[1] - 2)
    ]
    for copy in copies:
        copy.start()
    first = core_ref[0] == 0
    product = half_product(other_ref, flanks_ref[:, :flat], final_ref, outer_ref)

    def new_row(r):
        ig, i4 = divmod(r, groups)
        rows, lanes = slice(ig * half, (ig + 1) * half), slice(i4 * width, (i4 + 1) * width)
        mine, theirs = own_ref[rows, lanes], product[rows, lanes]
        piece = jnp.concatenate([jnp.where(first, mine, theirs), jnp.where(first, theirs, mine)])
        new = (coupling_ref[r].astype(jnp.float32) + piece).astype(jnp.bfloat16)
        pair_ref[r] = new
        return new.astype(jnp.float32)

    edges_in_turn(new_row, entry_ref.at[0], edges_ref, gate_ref)
    for copy in copies:
        copy.wait()


def opm_call(core, flanks, other, own, mixed, coupling, final, entry, flat):
    count, _, _, depth = mixed.shape
    strands, total_res, width = coupling.shape
    share = width // count
    return pl.pallas_call(
        lambda *refs: opm_kernel(flat, *refs),
        out_shape=(
            jax.ShapeDtypeStruct(coupling.shape, jnp.bfloat16),
            jax.ShapeDtypeStruct(
                (count, 2 + depth // 128, strands, share, total_res), jnp.bfloat16
            ),
            jax.ShapeDtypeStruct(coupling.shape, jnp.float32),
        ),
        in_specs=[pl.BlockSpec(memory_space=pltpu.SMEM)] + whole(7),
        out_specs=tuple(whole(3)),
        scratch_shapes=[
            pltpu.VMEM((own.shape[0], final.shape[0]), jnp.bfloat16),
            pltpu.SemaphoreType.DMA((depth // 128,)),
        ],
        compiler_params=params(24),
        name="outer_product_entry",
    )(core, flanks, other, own, mixed, coupling, final, entry)


def spread_kernel(final_ref, block_ref, wide_ref):
    width = final_ref.shape[1]
    depth = block_ref.shape[0] // 128
    groups = 128 // depth
    wide_ref[...] = final_ref[...].astype(jnp.float32)
    block_ref[...] = jnp.zeros(block_ref.shape, block_ref.dtype)
    for e in range(depth):
        piece = wide_ref[pl.ds(e, depth, stride=depth), :].astype(jnp.bfloat16)
        for g in range(groups):
            at = e * 128 + g * depth
            block_ref[at : at + depth, g * width : (g + 1) * width] = piece


def spread_call(final):
    depth = math.isqrt(final.shape[0])
    width = final.shape[1]
    return pl.pallas_call(
        spread_kernel,
        out_shape=jax.ShapeDtypeStruct((depth * 128, 128 // depth * width), jnp.bfloat16),
        in_specs=whole(1),
        out_specs=pl.BlockSpec(memory_space=pltpu.VMEM),
        scratch_shapes=[pltpu.VMEM(final.shape, jnp.float32)],
        compiler_params=params(),
        name="spread_weight",
    )(final)


def prepare_kernel(
    entry_ref,
    average_ref,
    project_ref,
    focus_ref,
    sides_ref,
    left_ref,
    right_ref,
    turned_ref,
    near_focus_ref,
):
    near_focus_ref[...] = focus_ref[...]
    turned_ref[...] = project_ref[...].astype(jnp.float32).T.astype(jnp.bfloat16)
    channels = average_ref.shape[1] // 2
    for ref, first, lane_of in (
        (left_ref, 0, lambda ch, g, size: g * channels + ch),
        (right_ref, channels, lambda ch, g, size: ch * size + g),
    ):
        size, _, lanes = ref.shape
        for g in range(size):
            ch = lax.broadcasted_iota(jnp.int32, (2 * channels, lanes), 0) - first
            lane = lax.broadcasted_iota(jnp.int32, (2 * channels, lanes), 1)
            chosen = (lane_of(ch, g, size) == lane) & (ch >= 0) & (ch < channels)
            placed = jnp.dot(
                average_ref[...],
                jnp.where(chosen, 1.0, 0.0).astype(jnp.bfloat16),
                preferred_element_type=jnp.float32,
            )
            ref[g] = placed.astype(jnp.bfloat16)
    for d in range(2):
        sides_ref[d] = entry_ref[d].astype(jnp.float32).T.astype(jnp.bfloat16)


def prepare_call(entries, average, project, focus):
    depth = average.shape[1] // 2
    width = entries.shape[1]
    return pl.pallas_call(
        prepare_kernel,
        out_shape=(
            jax.ShapeDtypeStruct((2, 5 * width, width), jnp.bfloat16),
            jax.ShapeDtypeStruct((128 // depth, average.shape[0], 128), jnp.bfloat16),
            jax.ShapeDtypeStruct((8, average.shape[0], 8 * depth), jnp.bfloat16),
            jax.ShapeDtypeStruct(project.shape[::-1], jnp.bfloat16),
            jax.ShapeDtypeStruct(focus.shape, jnp.bfloat16),
        ),
        in_specs=whole(4),
        out_specs=tuple(whole(5)),
        compiler_params=params(),
        name="prepare_weights",
    )(entries, average, project, focus)


def pack_kernel(
    msa_ref, pair_ref, weight_ref, out_ref, own_ref, rows_ref, logit_ref, term_ref, in_sems, out_sems
):
    count, parts = out_ref.shape[:2]
    loads = [
        pltpu.make_async_copy(pair_ref, rows_ref, in_sems.at[0]),
        pltpu.make_async_copy(weight_ref, logit_ref, in_sems.at[1]),
    ]
    own = pltpu.make_async_copy(msa_ref, own_ref, in_sems.at[2])
    stores = [
        pltpu.make_async_copy(
            own_ref.at[:, :, :, pl.ds(k * 128, 128)], out_ref.at[:, k], out_sems.at[count + k]
        )
        for k in range(parts - 1)
    ]
    for copy in loads + [own]:
        copy.start()
    for copy in loads:
        copy.wait()
    for r in range(rows_ref.shape[0]):
        if r == 1:
            own.wait()
            for copy in stores:
                copy.start()
        normed = lanes_norm(rows_ref[r].astype(jnp.float32)).astype(jnp.bfloat16)
        bias = lax.dot_general(
            logit_ref[...], normed, (((1,), (1,)), ((), ())), preferred_element_type=jnp.float32
        )
        upper = bias.astype(jnp.bfloat16)
        term_ref[0, r] = upper
        term_ref[1, r] = (bias - upper.astype(jnp.float32)).astype(jnp.bfloat16)
    terms = [
        pltpu.make_async_copy(term_ref.at[d % 2], out_ref.at[d, parts - 1], out_sems.at[d])
        for d in range(count)
    ]
    for copy in terms:
        copy.start()
    for copy in stores + terms:
        copy.wait()


def pack_call(msa, pair, weight, count):
    chains, strands, depth = msa.shape
    parts, heads = depth // 128, weight.shape[1]
    anywhere = pl.BlockSpec(memory_space=pltpu.HBM)
    return pl.pallas_call(
        pack_kernel,
        out_shape=jax.ShapeDtypeStruct(
            (count, parts + 1, chains // count, strands, 128), jnp.bfloat16
        ),
        in_specs=[anywhere] * 3,
        out_specs=anywhere,
        scratch_shapes=[
            pltpu.VMEM((count, chains // count, strands, depth), jnp.bfloat16),
            pltpu.VMEM(pair.shape, jnp.bfloat16),
            pltpu.VMEM((heads, pair.shape[2]), jnp.bfloat16),
            pltpu.VMEM((2, strands, heads, pair.shape[1]), jnp.bfloat16),
            pltpu.SemaphoreType.DMA((3,)),
            pltpu.SemaphoreType.DMA((count + parts,)),
        ],
        compiler_params=params(),
        name="pack_rows",
    )(
        *(
            pltpu.with_memory_space_constraint(operand, pltpu.HBM)
            for operand in (msa.reshape(count, chains // count, strands, depth), pair, weight.T)
        )
    )


def arrived_rows(arrived_ref, s):
    count, parts, _, strands, lanes = arrived_ref.shape
    pieces = [
        arrived_ref[:, k, s].astype(jnp.float32).reshape(count * strands, lanes)
        for k in range(parts - 1)
    ]
    return jnp.concatenate(pieces, axis=-1)


def project_kernel(arrived_ref, weight_ref, query_ref, key_ref, value_ref, gate_ref):
    inner = query_ref.shape[1]
    total_res = query_ref.shape[2]
    for s in range(0, query_ref.shape[0], 2):
        rows = jnp.concatenate([arrived_rows(arrived_ref, s + k) for k in range(2)])
        mapped = lax.dot_general(
            weight_ref[...],
            lanes_norm(rows).astype(jnp.bfloat16),
            (((1,), (1,)), ((), ())),
            preferred_element_type=jnp.float32,
        )
        for k in range(2):
            part = mapped[:, k * total_res : (k + 1) * total_res]
            for block, ref in enumerate((query_ref, key_ref, value_ref)):
                ref[s + k] = part[block * inner : (block + 1) * inner].astype(jnp.bfloat16)
            gate_ref[s + k] = jax.nn.sigmoid(part[3 * inner :])


def project_call(arrived, weight):
    count, _, chains, strands, _ = arrived.shape
    turned = (chains, weight.shape[0] // 4, count * strands)
    half = jax.ShapeDtypeStruct(turned, jnp.bfloat16)
    return pl.pallas_call(
        project_kernel,
        out_shape=(half, half, half, jax.ShapeDtypeStruct(turned, jnp.float32)),
        in_specs=whole(2),
        out_specs=tuple(whole(4)),
        compiler_params=params(),
        name="project_rows",
    )(arrived, weight)


def attend_kernel(
    width,
    arrived_ref,
    other_ref,
    query_ref,
    key_ref,
    value_ref,
    gate_ref,
    final_ref,
    left_ref,
    right_ref,
    mixed_ref,
    flanks_ref,
    bias_ref,
    turned_ref,
    scaled_ref,
):
    count, chains, strands, depth = mixed_ref.shape
    inner, total_res = query_ref.shape[1:]
    heads = inner // width
    mine = arrived_ref[:, arrived_ref.shape[1] - 1].astype(jnp.float32)
    bias = mine + other_ref[...].astype(jnp.float32)
    bias_ref[...] = bias.reshape(total_res * heads, total_res)
    for h in range(heads):
        turned_ref[h] = bias_ref[pl.ds(h, total_res, stride=heads), :].T * LOG2E
    scale = width ** (-0.5) * LOG2E

    def score(s, h):
        at = slice(h * width, (h + 1) * width)
        return lax.dot_general(
            key_ref[s, at],
            query_ref[s, at],
            (((0,), (0,)), ((), ())),
            preferred_element_type=jnp.float32,
        )

    def weigh(scores, h):
        scores = scores * scale + turned_ref[h]
        weights = jnp.exp2(scores - jnp.max(scores, axis=0, keepdims=True))
        total = jnp.sum(weights, axis=0, keepdims=True)
        return (weights * (1.0 / total)).astype(jnp.bfloat16)

    def finish(s, attended):
        attended = jnp.concatenate(attended).astype(jnp.bfloat16).astype(jnp.float32)
        gated = (attended * gate_ref[s]).astype(jnp.bfloat16)
        increment = lax.dot_general(
            gated, final_ref[...], (((0,), (0,)), ((), ())), preferred_element_type=jnp.float32
        )
        mixed = (arrived_rows(arrived_ref, s) + increment).astype(jnp.bfloat16)
        mixed = mixed.astype(jnp.float32)
        normed = lanes_norm(mixed)
        for k in range(depth // 128):
            scaled_ref[k, pl.ds(s, total_res, stride=chains), :] = normed[:, k * 128 : (k + 1) * 128]
        mixed_ref[:, s] = mixed.reshape(count, strands, depth).astype(jnp.bfloat16)

    steps = [(s, h) for s in range(chains) for h in range(heads)]
    ahead, lag = 6, 4
    scores = {n: score(*steps[n]) for n in range(ahead)}
    weighed, attended = {}, []
    for n in range(len(steps) + lag):
        if n + ahead < len(steps):
            scores[n + ahead] = score(*steps[n + ahead])
        if n < len(steps):
            weighed[n] = weigh(scores.pop(n), steps[n][1])
        if n >= lag:
            s, h = steps[n - lag]
            attended.append(
                jnp.dot(
                    value_ref[s, h * width : (h + 1) * width],
                    weighed.pop(n - lag),
                    preferred_element_type=jnp.float32,
                )
            )
            if h + 1 == heads:
                finish(s, attended)
                attended = []

    scaled = jnp.concatenate([scaled_ref[k] for k in range(depth // 128)], axis=-1)
    scaled = scaled.reshape(total_res, chains, depth)

    def side(weights_ref):
        group, _, lanes = weights_ref.shape
        total = None
        grouped = scaled.reshape(total_res // group, group, chains, depth)
        for g in range(group):
            part = grouped[:, g].reshape(total_res // group * chains, depth).astype(jnp.bfloat16)
            out = jnp.dot(part, weights_ref[g], preferred_element_type=jnp.float32)
            total = out if total is None else total + out
        return total.reshape(total_res // group, chains, lanes).astype(jnp.bfloat16)

    left, right = side(left_ref), side(right_ref)
    lefts, rights = left.shape[0] // count, right.shape[0] // 2
    for d in range(count):
        at = 0
        for k in range(lefts):
            flanks_ref[d, :, at : at + left.shape[2]] = left[d * lefts + k]
            at += left.shape[2]
        for k in range(rights):
            flanks_ref[d, :, at : at + right.shape[2]] = right[(d % 2) * rights + k]
            at += right.shape[2]


def attend_call(arrived, other, projected, width, final, left, right):
    count, parts, chains, strands, _ = arrived.shape
    inner, total_res = projected[0].shape[1:]
    depth, heads = (parts - 1) * 128, inner // width
    lanes = strands // left.shape[0] * left.shape[2] + total_res // 2 // right.shape[0] * right.shape[2]
    return pl.pallas_call(
        lambda *refs: attend_kernel(width, *refs),
        out_shape=(
            jax.ShapeDtypeStruct((count, chains, strands, depth), jnp.bfloat16),
            jax.ShapeDtypeStruct((count, chains, lanes), jnp.bfloat16),
        ),
        in_specs=whole(9),
        out_specs=tuple(whole(2)),
        scratch_shapes=[
            pltpu.VMEM((total_res * heads, total_res), jnp.float32),
            pltpu.VMEM((heads, total_res, total_res), jnp.float32),
            pltpu.VMEM((depth // 128, total_res * chains, 128), jnp.float32),
        ],
        compiler_params=params(),
        name="attend_rows",
    )(arrived, other, *projected, final, left, right)


def pair_track(core, flanks, other, mixed, coupling, final, prepared, exits, flat):
    sides = prepared[0]
    own = own_call(flanks, final, flat, coupling.shape[1] // 2)
    pair, edges, gate = opm_call(core, flanks, other, own, mixed, coupling, final, sides, flat)
    for d in range(2):
        arrived = exchange(edges)
        product = product_call(arrived, d == 1)
        gathered = exchange(product)
        if d == 0:
            pair, edges, gate, returned = exit_entry_call(
                gathered, exits, pair, gate, sides, arrived
            )
        else:
            pair = exit_call(gathered, exits, pair, gate)
    return returned.reshape((-1,) + mixed.shape[2:]), pair


def triangle(pair_prev, weight_in, weight_out, contraction):
    local_strands, total_res, pair_width = pair_prev.shape
    count = lax.axis_size("res")
    share = pair_width // count
    normed = standardise_entries(pair_prev, -1).astype(jnp.bfloat16)
    five = weight_in.reshape(pair_width, 5, pair_width)
    paired = five[:, :4].reshape(pair_width, 2, 2, count, share).transpose(0, 2, 3, 1, 4)
    mapped = jnp.einsum(
        "rnc,ctwsk->twskrn", normed, paired, preferred_element_type=jnp.float32
    )
    edges = (jax.nn.sigmoid(mapped[0]) * mapped[1]).astype(jnp.bfloat16)
    arrived = exchange(edges)
    gate_pair = jax.nn.sigmoid(
        jnp.einsum("rnc,cf->rnf", normed, five[:, 4], preferred_element_type=jnp.float32)
    )
    product = jnp.einsum(
        contraction, arrived[:, 0], arrived[:, 1], preferred_element_type=jnp.float32
    ).astype(jnp.bfloat16)
    product = product.reshape(share, count, local_strands, total_res).transpose(1, 0, 2, 3)
    gathered = exchange(product).reshape(pair_width, local_strands, total_res)
    edge_norm = standardise_entries(gathered, 0).astype(jnp.bfloat16)
    update = jnp.einsum("crn,cf->rnf", edge_norm, weight_out, preferred_element_type=jnp.float32)
    return (pair_prev.astype(jnp.float32) + gate_pair * update).astype(jnp.bfloat16)


def body(
    alignment_embedding,
    coupling_embedding,
    query_key_matrix,
    coupling_logit_matrix,
    focus_final_matrix,
    tensor_average_matrix,
    tensor_average_final,
    trilateral_entry_matrix,
    trilateral_exit_matrix,
):
    chain_tally, local_strands, depth = alignment_embedding.shape
    total_res, pair_width = coupling_embedding.shape[1:]
    count = lax.axis_size("res")
    core = lax.axis_index("res") % 2
    heads = coupling_logit_matrix.shape[1]
    width = query_key_matrix.shape[1] // (4 * heads)
    per_device = chain_tally // count
    tensor_depth = tensor_average_matrix.shape[1] // 2
    half = total_res // 2

    fits = (
        pair_width == 128
        and pair_width % (8 * count) == 0
        and count & (count - 1) == 0
        and total_res == 128
        and local_strands == 8
        and per_device == 8
        and heads == 8
        and heads * width == depth
        and depth % 128 == 0
        and tensor_depth == 32
    )
    if fits:
        prepared = prepare_call(
            trilateral_entry_matrix,
            tensor_average_matrix,
            query_key_matrix,
            focus_final_matrix,
        )
        packed = pack_call(alignment_embedding, coupling_embedding, coupling_logit_matrix, count)
        arrived = exchange(packed)
        other = across(arrived[:, -1], 1)
        projected = project_call(arrived, prepared[3])
        mixed, flanks = attend_call(arrived, other, projected, width, prepared[4], *prepared[1:3])
        flanks = exchange(flanks)
        flanks = flanks.reshape(chain_tally, -1)
        other = across(flanks, 1)
        final = spread_call(tensor_average_final)
        return pair_track(
            core.reshape(1),
            flanks,
            other,
            mixed,
            coupling_embedding,
            final,
            prepared,
            trilateral_exit_matrix,
            local_strands * tensor_depth,
        )

    rows = exchange(alignment_embedding).reshape(count, per_device, local_strands, depth)
    rows = rows.transpose(1, 0, 2, 3).reshape(per_device, total_res, depth)
    pair_norm = standardise_entries(coupling_embedding, -1).astype(jnp.bfloat16)
    bias_rows = jnp.einsum(
        "rnc,ch->hrn", pair_norm, coupling_logit_matrix, preferred_element_type=jnp.float32
    )
    bias = lax.all_gather(bias_rows, "res", axis=1, tiled=True)

    standard = standardise_entries(rows, -1).astype(jnp.bfloat16)
    projection = query_key_matrix.reshape(depth, 4, heads, width)
    mapped = jnp.einsum(
        "snc,cthd->tshnd", standard, projection[:, :3], preferred_element_type=jnp.float32
    ).astype(jnp.bfloat16)
    gate = jax.nn.sigmoid(
        jnp.einsum("snc,chd->shnd", standard, projection[:, 3], preferred_element_type=jnp.float32)
    )
    scores = (
        jnp.einsum("shid,shjd->shij", mapped[0], mapped[1], preferred_element_type=jnp.float32)
        * width ** (-0.5)
        + bias
    )
    weights = jnp.exp(scores - jnp.max(scores, axis=-1, keepdims=True))
    weights = (weights / jnp.sum(weights, axis=-1, keepdims=True)).astype(jnp.bfloat16)
    attended = jnp.einsum(
        "shij,shjd->shid", weights, mapped[2], preferred_element_type=jnp.float32
    ).astype(jnp.bfloat16)
    gated = (attended.astype(jnp.float32) * gate).astype(jnp.bfloat16)
    increment = jnp.einsum(
        "shnd,hdc->snc",
        gated,
        focus_final_matrix.reshape(heads, width, depth),
        preferred_element_type=jnp.float32,
    )
    mixed = (rows.astype(jnp.float32) + increment).astype(jnp.bfloat16)

    tensor_scaled = standardise_entries(mixed, -1).astype(jnp.bfloat16)
    flank = jnp.einsum(
        "snc,ctk->tsnk",
        tensor_scaled,
        tensor_average_matrix.reshape(depth, 2, tensor_depth),
        preferred_element_type=jnp.float32,
    ).astype(jnp.bfloat16)
    left = flank[0].reshape(per_device, count // 2, 2, local_strands * tensor_depth)
    left = left.transpose(1, 2, 0, 3)
    right = flank[1].reshape(per_device, 2, half // 8, 8, tensor_depth).transpose(1, 0, 2, 4, 3)
    right = right.reshape(2, per_device, tensor_depth * half)
    right = jnp.broadcast_to(right, (count // 2,) + right.shape)
    flanks = jnp.concatenate([left, right], axis=-1).reshape(count, per_device, -1)
    flanks = exchange(flanks)
    mixed_out = exchange(
        mixed.reshape(per_device, count, local_strands, depth).transpose(1, 0, 2, 3)
    ).reshape(chain_tally, local_strands, depth)

    flanks = flanks.reshape(chain_tally, -1)
    mine = flanks[:, local_strands * tensor_depth :]
    other = across(mine, 1)
    group = max(1, 128 // tensor_depth)
    final = tensor_average_final.reshape(tensor_depth, tensor_depth, pair_width)
    final = jnp.einsum("ab,cef->eacbf", jnp.eye(group, dtype=final.dtype), final)
    final = final.reshape(tensor_depth * group * tensor_depth, group * pair_width)
    left_all = flanks[:, : local_strands * tensor_depth]
    both = jnp.stack([mine, other])
    both = jnp.where(core == 0, both, both[::-1])
    both = both.reshape(2, chain_tally, half // 8, tensor_depth, 8)
    outer = jnp.einsum(
        "xsaej,sgm->gxajem",
        both,
        left_all.reshape(chain_tally, local_strands // group, group * tensor_depth),
        preferred_element_type=jnp.float32,
    ) * (1.0 / chain_tally)
    outer = outer.astype(jnp.bfloat16).reshape(local_strands // group, total_res, -1)
    opm = jnp.einsum("gjk,kn->gjn", outer, final, preferred_element_type=jnp.float32)
    opm = opm.reshape(local_strands // group, total_res, group, pair_width)
    opm = opm.transpose(0, 2, 1, 3).reshape(local_strands, total_res, pair_width)
    pair_mid = (coupling_embedding.astype(jnp.float32) + opm).astype(jnp.bfloat16)

    pair_tri = triangle(
        pair_mid, trilateral_entry_matrix[0], trilateral_exit_matrix[0], "xcik,ycjk->cxiyj"
    )
    coupling_refreshed = triangle(
        pair_tri, trilateral_entry_matrix[1], trilateral_exit_matrix[1], "xcki,xckj->cij"
    )
    return (mixed_out, coupling_refreshed)


def solution(mesh):
    return jax.shard_map(
        body,
        mesh=mesh,
        in_specs=(P("grp", "res", None), P("res", "grp", None), P(), P(), P(), P(), P(), P(), P()),
        out_specs=(P("grp", "res", None), P("res", "grp", None)),
        check_vma=False,
    )
```

```python
import math

import jax
import jax.numpy as jnp
from jax import lax
from jax.experimental import pallas as pl
from jax.experimental.pallas import tpu as pltpu
from jax.sharding import PartitionSpec as P


LOG2E = math.log2(math.e)


def standardise_entries(values_in, axis_num):
    values_in = values_in.astype(jnp.float32)
    centred = values_in - jnp.mean(values_in, axis=axis_num, keepdims=True)
    spread = jnp.mean(centred * centred, axis=axis_num, keepdims=True)
    return centred * lax.rsqrt(spread + 1e-05)


def exchange(blocks):
    return lax.all_to_all(blocks, "res", split_axis=0, concat_axis=0, tiled=True)


def across(values, bit):
    count = lax.axis_size("res")
    return lax.ppermute(values, "res", [(k, k ^ bit) for k in range(count)])


def params(megabytes=16):
    return pltpu.CompilerParams(vmem_limit_bytes=megabytes << 20)


def whole(count):
    return [pl.BlockSpec(memory_space=pltpu.VMEM)] * count


def lanes_norm(values):
    centred = values - jnp.mean(values, axis=-1, keepdims=True)
    spread = jnp.mean(centred * centred, axis=-1, keepdims=True)
    return centred * lax.rsqrt(spread + 1e-05)


def edges_in_turn(new_row, entry_ref, edges_ref, gate_ref):
    count, _, strands, share, lanes = edges_ref.shape
    width = count * share
    normed, mapped, gates = {}, {}, {}
    pairs = strands // 2
    for n in range(pairs + 2):
        if n < pairs:
            rows = [lanes_norm(new_row(2 * n + k)).astype(jnp.bfloat16) for k in range(2)]
            normed[n] = jnp.concatenate(rows)
        if 0 < n <= pairs:
            rows = normed.pop(n - 1)
            mapped[n - 1] = [
                lax.dot_general(
                    entry_ref[2 * side * width : 2 * (side + 1) * width],
                    rows,
                    (((1,), (1,)), ((), ())),
                    preferred_element_type=jnp.float32,
                )
                for side in range(2)
            ]
            gates[n - 1] = lax.dot_general(
                rows,
                entry_ref[4 * width :],
                (((1,), (1,)), ((), ())),
                preferred_element_type=jnp.float32,
            )
        if n > 1:
            gate = jax.nn.sigmoid(gates.pop(n - 2))
            for k in range(2):
                gate_ref[2 * n - 4 + k] = gate[k * lanes : (k + 1) * lanes]
            for side, both in enumerate(mapped.pop(n - 2)):
                edge = jax.nn.sigmoid(both[:width]) * both[width:]
                for k in range(2):
                    part = edge[:, k * lanes : (k + 1) * lanes].reshape(count, share, lanes)
                    edges_ref[:, side, 2 * n - 4 + k] = part.astype(jnp.bfloat16)


def product_kernel(incoming, arrived_ref, product_ref, left_ref, right_ref):
    count, _, strands, share, lanes = arrived_ref.shape
    rows = count * strands
    for side, ref in enumerate((left_ref, right_ref)):
        ref[...] = arrived_ref[:, side].astype(jnp.float32).reshape(rows * share, lanes)
    dims = (((0,), (0,)), ((), ())) if incoming else (((1,), (1,)), ((), ()))
    for ch in range(share):
        left = left_ref[pl.ds(ch, rows, stride=share), :].astype(jnp.bfloat16)
        right = right_ref[pl.ds(ch, rows, stride=share), :].astype(jnp.bfloat16)
        out = lax.dot_general(left, right, dims, preferred_element_type=jnp.float32)
        product_ref[:, ch] = out.reshape(count, strands, lanes).astype(jnp.bfloat16)


def product_call(arrived, incoming):
    count, _, strands, share, lanes = arrived.shape
    scratch = pltpu.VMEM((count * strands * share, lanes), jnp.float32)
    return pl.pallas_call(
        lambda *refs: product_kernel(incoming, *refs),
        out_shape=jax.ShapeDtypeStruct((count, share, strands, lanes), jnp.bfloat16),
        in_specs=whole(1),
        out_specs=pl.BlockSpec(memory_space=pltpu.VMEM),
        scratch_shapes=[scratch, scratch],
        compiler_params=params(),
        name="edge_product",
    )(arrived)


def exit_rows(which, gathered_ref, exit_ref, pair_ref, gate_ref, out_ref, spread_ref):
    count, share, strands, lanes = gathered_ref.shape
    width = count * share
    spread_ref[...] = gathered_ref[...].astype(jnp.float32).reshape(width * strands, lanes)

    def update(r):
        edges = spread_ref[pl.ds(r, width, stride=strands), :]
        centred = edges - jnp.mean(edges, axis=0, keepdims=True)
        spread = jnp.mean(centred * centred, axis=0, keepdims=True)
        normed = (centred * lax.rsqrt(spread + 1e-05)).astype(jnp.bfloat16)
        return lax.dot_general(
            normed, exit_ref[which], (((0,), (0,)), ((), ())), preferred_element_type=jnp.float32
        )

    ahead = 2
    updates = {r: update(r) for r in range(ahead)}

    def new_row(r):
        if r + ahead < strands:
            updates[r + ahead] = update(r + ahead)
        new = pair_ref[r].astype(jnp.float32) + gate_ref[r] * updates.pop(r)
        new = new.astype(jnp.bfloat16)
        out_ref[r] = new
        return new.astype(jnp.float32)

    return new_row


def exit_entry_kernel(
    gathered_ref,
    exit_ref,
    pair_ref,
    gate_ref,
    entry_ref,
    arrived_ref,
    out_ref,
    edges_ref,
    next_gate_ref,
    mixed_ref,
    spread_ref,
    sems,
):
    copies = [
        pltpu.make_async_copy(
            arrived_ref.at[:, 2 + k], mixed_ref.at[:, :, :, pl.ds(k * 128, 128)], sems.at[k]
        )
        for k in range(arrived_ref.shape[1] - 2)
    ]
    for copy in copies:
        copy.start()
    new_row = exit_rows(0, gathered_ref, exit_ref, pair_ref, gate_ref, out_ref, spread_ref)
    edges_in_turn(new_row, entry_ref.at[1], edges_ref, next_gate_ref)
    for copy in copies:
        copy.wait()


def exit_entry_call(gathered, weight, pair_prev, gate, entry, arrived):
    count, share, strands, lanes = gathered.shape
    parts = arrived.shape[1] - 2
    anywhere = pl.BlockSpec(memory_space=pl.ANY)
    return pl.pallas_call(
        exit_entry_kernel,
        out_shape=(
            jax.ShapeDtypeStruct(pair_prev.shape, jnp.bfloat16),
            jax.ShapeDtypeStruct((count, 2, strands, share, lanes), jnp.bfloat16),
            jax.ShapeDtypeStruct(pair_prev.shape, jnp.float32),
            jax.ShapeDtypeStruct((count, strands, share, parts * 128), jnp.bfloat16),
        ),
        in_specs=whole(5) + [anywhere],
        out_specs=tuple(whole(3)) + (pl.BlockSpec(memory_space=pltpu.HBM),),
        scratch_shapes=[
            pltpu.VMEM((count * share * strands, lanes), jnp.float32),
            pltpu.SemaphoreType.DMA((parts,)),
        ],
        compiler_params=params(),
        name="triangle_exit_entry",
    )(gathered, weight, pair_prev, gate, entry, arrived)


def exit_kernel(gathered_ref, exit_ref, pair_ref, gate_ref, out_ref, near_ref, spread_ref, sems):
    new_row = exit_rows(1, gathered_ref, exit_ref, pair_ref, gate_ref, near_ref, spread_ref)
    copies = []
    for r in range(pair_ref.shape[0]):
        new_row(r)
        if r % 2:
            at = pl.ds(r - 1, 2)
            copies.append(pltpu.make_async_copy(near_ref.at[at], out_ref.at[at], sems.at[r // 2]))
            copies[-1].start()
    for copy in copies:
        copy.wait()


def exit_call(gathered, weight, pair_prev, gate):
    count, share, strands, lanes = gathered.shape
    return pl.pallas_call(
        exit_kernel,
        out_shape=jax.ShapeDtypeStruct(pair_prev.shape, jnp.bfloat16),
        in_specs=whole(4),
        out_specs=pl.BlockSpec(memory_space=pltpu.HBM),
        scratch_shapes=[
            pltpu.VMEM(pair_prev.shape, jnp.bfloat16),
            pltpu.VMEM((count * share * strands, lanes), jnp.float32),
            pltpu.SemaphoreType.DMA((strands // 2,)),
        ],
        compiler_params=params(),
        name="triangle_exit",
    )(gathered, weight, pair_prev, gate)


def half_product(flanks_ref, left, final_ref, outer_ref):
    chains, flat = left.shape
    depth = final_ref.shape[0] // 128
    span, blocks = 8 * depth, flat // 128
    half = (flanks_ref.shape[1] - flat) // depth
    for pair in range(half // 16):
        parts = []
        for jg in (2 * pair, 2 * pair + 1):
            part = lax.dot_general(
                flanks_ref[:, flat + jg * span : flat + (jg + 1) * span],
                left,
                (((0,), (0,)), ((), ())),
                preferred_element_type=jnp.float32,
            ) * (1.0 / chains)
            parts.append(part.reshape(depth, 8, flat))
        both = jnp.concatenate(parts, axis=1).astype(jnp.bfloat16)
        for ig in range(blocks):
            at = ig * half + pair * 16
            for e in range(depth):
                outer_ref[at : at + 16, e * 128 : (e + 1) * 128] = both[e, :, ig * 128 : (ig + 1) * 128]
    return jnp.dot(outer_ref[...], final_ref[...], preferred_element_type=jnp.float32)


def own_kernel(flat, flanks_ref, final_ref, product_ref, outer_ref):
    product_ref[...] = half_product(flanks_ref, flanks_ref[:, :flat], final_ref, outer_ref)


def own_call(flanks, final, flat, half):
    rows = flat // 128 * half
    return pl.pallas_call(
        lambda *refs: own_kernel(flat, *refs),
        out_shape=jax.ShapeDtypeStruct((rows, final.shape[1]), jnp.float32),
        in_specs=whole(2),
        out_specs=pl.BlockSpec(memory_space=pltpu.VMEM),
        scratch_shapes=[pltpu.VMEM((rows, final.shape[0]), jnp.bfloat16)],
        compiler_params=params(24),
        name="outer_product_own",
    )(flanks, final)


def opm_kernel(
    flat,
    core_ref,
    flanks_ref,
    other_ref,
    own_ref,
    mixed_ref,
    coupling_ref,
    final_ref,
    entry_ref,
    pair_ref,
    edges_ref,
    gate_ref,
    outer_ref,
    sems,
):
    _, total_res, width = coupling_ref.shape
    groups = final_ref.shape[1] // width
    half = total_res // 2
    copies = [
        pltpu.make_async_copy(
            mixed_ref.at[:, :, :, pl.ds(k * 128, 128)], edges_ref.at[:, 2 + k], sems.at[k]
        )
        for k in range(edges_ref.shape[1] - 2)
    ]
    for copy in copies:
        copy.start()
    first = core_ref[0] == 0
    product = half_product(other_ref, flanks_ref[:, :flat], final_ref, outer_ref)

    def new_row(r):
        ig, i4 = divmod(r, groups)
        rows, lanes = slice(ig * half, (ig + 1) * half), slice(i4 * width, (i4 + 1) * width)
        mine, theirs = own_ref[rows, lanes], product[rows, lanes]
        piece = jnp.concatenate([jnp.where(first, mine, theirs), jnp.where(first, theirs, mine)])
        new = (coupling_ref[r].astype(jnp.float32) + piece).astype(jnp.bfloat16)
        pair_ref[r] = new
        return new.astype(jnp.float32)

    edges_in_turn(new_row, entry_ref.at[0], edges_ref, gate_ref)
    for copy in copies:
        copy.wait()


def opm_call(core, flanks, other, own, mixed, coupling, final, entry, flat):
    count, _, _, depth = mixed.shape
    strands, total_res, width = coupling.shape
    share = width // count
    return pl.pallas_call(
        lambda *refs: opm_kernel(flat, *refs),
        out_shape=(
            jax.ShapeDtypeStruct(coupling.shape, jnp.bfloat16),
            jax.ShapeDtypeStruct(
                (count, 2 + depth // 128, strands, share, total_res), jnp.bfloat16
            ),
            jax.ShapeDtypeStruct(coupling.shape, jnp.float32),
        ),
        in_specs=[pl.BlockSpec(memory_space=pltpu.SMEM)] + whole(7),
        out_specs=tuple(whole(3)),
        scratch_shapes=[
            pltpu.VMEM((own.shape[0], final.shape[0]), jnp.bfloat16),
            pltpu.SemaphoreType.DMA((depth // 128,)),
        ],
        compiler_params=params(24),
        name="outer_product_entry",
    )(core, flanks, other, own, mixed, coupling, final, entry)


def spread_kernel(final_ref, block_ref, wide_ref):
    width = final_ref.shape[1]
    depth = block_ref.shape[0] // 128
    groups = 128 // depth
    wide_ref[...] = final_ref[...].astype(jnp.float32)
    block_ref[...] = jnp.zeros(block_ref.shape, block_ref.dtype)
    for e in range(depth):
        piece = wide_ref[pl.ds(e, depth, stride=depth), :].astype(jnp.bfloat16)
        for g in range(groups):
            at = e * 128 + g * depth
            block_ref[at : at + depth, g * width : (g + 1) * width] = piece


def spread_call(final):
    depth = math.isqrt(final.shape[0])
    width = final.shape[1]
    return pl.pallas_call(
        spread_kernel,
        out_shape=jax.ShapeDtypeStruct((depth * 128, 128 // depth * width), jnp.bfloat16),
        in_specs=whole(1),
        out_specs=pl.BlockSpec(memory_space=pltpu.VMEM),
        scratch_shapes=[pltpu.VMEM(final.shape, jnp.float32)],
        compiler_params=params(),
        name="spread_weight",
    )(final)


def prepare_kernel(
    entry_ref,
    average_ref,
    project_ref,
    focus_ref,
    sides_ref,
    left_ref,
    right_ref,
    turned_ref,
    near_focus_ref,
):
    near_focus_ref[...] = focus_ref[...]
    turned_ref[...] = project_ref[...].astype(jnp.float32).T.astype(jnp.bfloat16)
    channels = average_ref.shape[1] // 2
    for ref, first, lane_of in (
        (left_ref, 0, lambda ch, g, size: g * channels + ch),
        (right_ref, channels, lambda ch, g, size: ch * size + g),
    ):
        size, _, lanes = ref.shape
        for g in range(size):
            ch = lax.broadcasted_iota(jnp.int32, (2 * channels, lanes), 0) - first
            lane = lax.broadcasted_iota(jnp.int32, (2 * channels, lanes), 1)
            chosen = (lane_of(ch, g, size) == lane) & (ch >= 0) & (ch < channels)
            placed = jnp.dot(
                average_ref[...],
                jnp.where(chosen, 1.0, 0.0).astype(jnp.bfloat16),
                preferred_element_type=jnp.float32,
            )
            ref[g] = placed.astype(jnp.bfloat16)
    for d in range(2):
        sides_ref[d] = entry_ref[d].astype(jnp.float32).T.astype(jnp.bfloat16)


def prepare_call(entries, average, project, focus):
    depth = average.shape[1] // 2
    width = entries.shape[1]
    return pl.pallas_call(
        prepare_kernel,
        out_shape=(
            jax.ShapeDtypeStruct((2, 5 * width, width), jnp.bfloat16),
            jax.ShapeDtypeStruct((128 // depth, average.shape[0], 128), jnp.bfloat16),
            jax.ShapeDtypeStruct((8, average.shape[0], 8 * depth), jnp.bfloat16),
            jax.ShapeDtypeStruct(project.shape[::-1], jnp.bfloat16),
            jax.ShapeDtypeStruct(focus.shape, jnp.bfloat16),
        ),
        in_specs=whole(4),
        out_specs=tuple(whole(5)),
        compiler_params=params(),
        name="prepare_weights",
    )(entries, average, project, focus)


def pack_kernel(
    msa_ref, pair_ref, weight_ref, out_ref, own_ref, rows_ref, logit_ref, term_ref, in_sems, out_sems
):
    count, parts = out_ref.shape[:2]
    loads = [
        pltpu.make_async_copy(pair_ref, rows_ref, in_sems.at[0]),
        pltpu.make_async_copy(weight_ref, logit_ref, in_sems.at[1]),
    ]
    own = pltpu.make_async_copy(msa_ref, own_ref, in_sems.at[2])
    stores = [
        pltpu.make_async_copy(
            own_ref.at[:, :, :, pl.ds(k * 128, 128)], out_ref.at[:, k], out_sems.at[count + k]
        )
        for k in range(parts - 1)
    ]
    for copy in loads + [own]:
        copy.start()
    for copy in loads:
        copy.wait()
    for r in range(rows_ref.shape[0]):
        if r == 1:
            own.wait()
            for copy in stores:
                copy.start()
        normed = lanes_norm(rows_ref[r].astype(jnp.float32)).astype(jnp.bfloat16)
        bias = lax.dot_general(
            logit_ref[...], normed, (((1,), (1,)), ((), ())), preferred_element_type=jnp.float32
        )
        upper = bias.astype(jnp.bfloat16)
        term_ref[0, r] = upper
        term_ref[1, r] = (bias - upper.astype(jnp.float32)).astype(jnp.bfloat16)
    terms = [
        pltpu.make_async_copy(term_ref.at[d % 2], out_ref.at[d, parts - 1], out_sems.at[d])
        for d in range(count)
    ]
    for copy in terms:
        copy.start()
    for copy in stores + terms:
        copy.wait()


def pack_call(msa, pair, weight, count):
    chains, strands, depth = msa.shape
    parts, heads = depth // 128, weight.shape[1]
    anywhere = pl.BlockSpec(memory_space=pltpu.HBM)
    return pl.pallas_call(
        pack_kernel,
        out_shape=jax.ShapeDtypeStruct(
            (count, parts + 1, chains // count, strands, 128), jnp.bfloat16
        ),
        in_specs=[anywhere] * 3,
        out_specs=anywhere,
        scratch_shapes=[
            pltpu.VMEM((count, chains // count, strands, depth), jnp.bfloat16),
            pltpu.VMEM(pair.shape, jnp.bfloat16),
            pltpu.VMEM((heads, pair.shape[2]), jnp.bfloat16),
            pltpu.VMEM((2, strands, heads, pair.shape[1]), jnp.bfloat16),
            pltpu.SemaphoreType.DMA((3,)),
            pltpu.SemaphoreType.DMA((count + parts,)),
        ],
        compiler_params=params(),
        name="pack_rows",
    )(
        *(
            pltpu.with_memory_space_constraint(operand, pltpu.HBM)
            for operand in (msa.reshape(count, chains // count, strands, depth), pair, weight.T)
        )
    )


def arrived_rows(arrived_ref, s):
    count, parts, _, strands, lanes = arrived_ref.shape
    pieces = [
        arrived_ref[:, k, s].astype(jnp.float32).reshape(count * strands, lanes)
        for k in range(parts - 1)
    ]
    return jnp.concatenate(pieces, axis=-1)


def project_kernel(arrived_ref, weight_ref, query_ref, key_ref, value_ref, gate_ref):
    inner = query_ref.shape[1]
    total_res = query_ref.shape[2]
    for s in range(0, query_ref.shape[0], 2):
        rows = jnp.concatenate([arrived_rows(arrived_ref, s + k) for k in range(2)])
        mapped = lax.dot_general(
            weight_ref[...],
            lanes_norm(rows).astype(jnp.bfloat16),
            (((1,), (1,)), ((), ())),
            preferred_element_type=jnp.float32,
        )
        for k in range(2):
            part = mapped[:, k * total_res : (k + 1) * total_res]
            for block, ref in enumerate((query_ref, key_ref, value_ref)):
                ref[s + k] = part[block * inner : (block + 1) * inner].astype(jnp.bfloat16)
            gate_ref[s + k] = jax.nn.sigmoid(part[3 * inner :])


def project_call(arrived, weight):
    count, _, chains, strands, _ = arrived.shape
    turned = (chains, weight.shape[0] // 4, count * strands)
    half = jax.ShapeDtypeStruct(turned, jnp.bfloat16)
    return pl.pallas_call(
        project_kernel,
        out_shape=(half, half, half, jax.ShapeDtypeStruct(turned, jnp.float32)),
        in_specs=whole(2),
        out_specs=tuple(whole(4)),
        compiler_params=params(),
        name="project_rows",
    )(arrived, weight)


def attend_kernel(
    width,
    arrived_ref,
    other_ref,
    query_ref,
    key_ref,
    value_ref,
    gate_ref,
    final_ref,
    left_ref,
    right_ref,
    mixed_ref,
    flanks_ref,
    bias_ref,
    turned_ref,
    scaled_ref,
):
    count, chains, strands, depth = mixed_ref.shape
    inner, total_res = query_ref.shape[1:]
    heads = inner // width
    mine = arrived_ref[:, arrived_ref.shape[1] - 1].astype(jnp.float32)
    bias = mine + other_ref[...].astype(jnp.float32)
    bias_ref[...] = bias.reshape(total_res * heads, total_res)
    for h in range(heads):
        turned_ref[h] = bias_ref[pl.ds(h, total_res, stride=heads), :].T * LOG2E
    scale = width ** (-0.5) * LOG2E

    def score(s, h):
        at = slice(h * width, (h + 1) * width)
        return lax.dot_general(
            key_ref[s, at],
            query_ref[s, at],
            (((0,), (0,)), ((), ())),
            preferred_element_type=jnp.float32,
        )

    def weigh(scores, h):
        scores = scores * scale + turned_ref[h]
        weights = jnp.exp2(scores - jnp.max(scores, axis=0, keepdims=True))
        total = jnp.sum(weights, axis=0, keepdims=True)
        return (weights * (1.0 / total)).astype(jnp.bfloat16)

    def finish(s, attended):
        attended = jnp.concatenate(attended).astype(jnp.bfloat16).astype(jnp.float32)
        gated = (attended * gate_ref[s]).astype(jnp.bfloat16)
        increment = lax.dot_general(
            gated, final_ref[...], (((0,), (0,)), ((), ())), preferred_element_type=jnp.float32
        )
        mixed = (arrived_rows(arrived_ref, s) + increment).astype(jnp.bfloat16)
        mixed = mixed.astype(jnp.float32)
        normed = lanes_norm(mixed)
        for k in range(depth // 128):
            scaled_ref[k, pl.ds(s, total_res, stride=chains), :] = normed[:, k * 128 : (k + 1) * 128]
        mixed_ref[:, s] = mixed.reshape(count, strands, depth).astype(jnp.bfloat16)

    steps = [(s, h) for s in range(chains) for h in range(heads)]
    ahead, lag = 6, 4
    scores = {n: score(*steps[n]) for n in range(ahead)}
    weighed, attended = {}, []
    for n in range(len(steps) + lag):
        if n + ahead < len(steps):
            scores[n + ahead] = score(*steps[n + ahead])
        if n < len(steps):
            weighed[n] = weigh(scores.pop(n), steps[n][1])
        if n >= lag:
            s, h = steps[n - lag]
            attended.append(
                jnp.dot(
                    value_ref[s, h * width : (h + 1) * width],
                    weighed.pop(n - lag),
                    preferred_element_type=jnp.float32,
                )
            )
            if h + 1 == heads:
                finish(s, attended)
                attended = []

    scaled = jnp.concatenate([scaled_ref[k] for k in range(depth // 128)], axis=-1)
    scaled = scaled.reshape(total_res, chains, depth)

    def side(weights_ref):
        group, _, lanes = weights_ref.shape
        rows = total_res // group
        grouped = scaled.reshape(rows, group, chains, depth)
        parts = [grouped[:, g].reshape(rows * chains, depth) for g in range(group)]
        total = jnp.dot(
            jnp.concatenate(parts, axis=-1).astype(jnp.bfloat16),
            weights_ref[...].reshape(group * depth, lanes),
            preferred_element_type=jnp.float32,
        )
        return total.reshape(rows, chains, lanes).astype(jnp.bfloat16)

    left, right = side(left_ref), side(right_ref)
    lefts, rights = left.shape[0] // count, right.shape[0] // 2
    for d in range(count):
        at = 0
        for k in range(lefts):
            flanks_ref[d, :, at : at + left.shape[2]] = left[d * lefts + k]
            at += left.shape[2]
        for k in range(rights):
            flanks_ref[d, :, at : at + right.shape[2]] = right[(d % 2) * rights + k]
            at += right.shape[2]


def attend_call(arrived, other, projected, width, final, left, right):
    count, parts, chains, strands, _ = arrived.shape
    inner, total_res = projected[0].shape[1:]
    depth, heads = (parts - 1) * 128, inner // width
    lanes = strands // left.shape[0] * left.shape[2] + total_res // 2 // right.shape[0] * right.shape[2]
    return pl.pallas_call(
        lambda *refs: attend_kernel(width, *refs),
        out_shape=(
            jax.ShapeDtypeStruct((count, chains, strands, depth), jnp.bfloat16),
            jax.ShapeDtypeStruct((count, chains, lanes), jnp.bfloat16),
        ),
        in_specs=whole(9),
        out_specs=tuple(whole(2)),
        scratch_shapes=[
            pltpu.VMEM((total_res * heads, total_res), jnp.float32),
            pltpu.VMEM((heads, total_res, total_res), jnp.float32),
            pltpu.VMEM((depth // 128, total_res * chains, 128), jnp.float32),
        ],
        compiler_params=params(),
        name="attend_rows",
    )(arrived, other, *projected, final, left, right)


def pair_track(core, flanks, other, mixed, coupling, final, prepared, exits, flat):
    sides = prepared[0]
    own = own_call(flanks, final, flat, coupling.shape[1] // 2)
    pair, edges, gate = opm_call(core, flanks, other, own, mixed, coupling, final, sides, flat)
    for d in range(2):
        arrived = exchange(edges)
        product = product_call(arrived, d == 1)
        gathered = exchange(product)
        if d == 0:
            pair, edges, gate, returned = exit_entry_call(
                gathered, exits, pair, gate, sides, arrived
            )
        else:
            pair = exit_call(gathered, exits, pair, gate)
    return returned.reshape((-1,) + mixed.shape[2:]), pair


def triangle(pair_prev, weight_in, weight_out, contraction):
    local_strands, total_res, pair_width = pair_prev.shape
    count = lax.axis_size("res")
    share = pair_width // count
    normed = standardise_entries(pair_prev, -1).astype(jnp.bfloat16)
    five = weight_in.reshape(pair_width, 5, pair_width)
    paired = five[:, :4].reshape(pair_width, 2, 2, count, share).transpose(0, 2, 3, 1, 4)
    mapped = jnp.einsum(
        "rnc,ctwsk->twskrn", normed, paired, preferred_element_type=jnp.float32
    )
    edges = (jax.nn.sigmoid(mapped[0]) * mapped[1]).astype(jnp.bfloat16)
    arrived = exchange(edges)
    gate_pair = jax.nn.sigmoid(
        jnp.einsum("rnc,cf->rnf", normed, five[:, 4], preferred_element_type=jnp.float32)
    )
    product = jnp.einsum(
        contraction, arrived[:, 0], arrived[:, 1], preferred_element_type=jnp.float32
    ).astype(jnp.bfloat16)
    product = product.reshape(share, count, local_strands, total_res).transpose(1, 0, 2, 3)
    gathered = exchange(product).reshape(pair_width, local_strands, total_res)
    edge_norm = standardise_entries(gathered, 0).astype(jnp.bfloat16)
    update = jnp.einsum("crn,cf->rnf", edge_norm, weight_out, preferred_element_type=jnp.float32)
    return (pair_prev.astype(jnp.float32) + gate_pair * update).astype(jnp.bfloat16)


def body(
    alignment_embedding,
    coupling_embedding,
    query_key_matrix,
    coupling_logit_matrix,
    focus_final_matrix,
    tensor_average_matrix,
    tensor_average_final,
    trilateral_entry_matrix,
    trilateral_exit_matrix,
):
    chain_tally, local_strands, depth = alignment_embedding.shape
    total_res, pair_width = coupling_embedding.shape[1:]
    count = lax.axis_size("res")
    core = lax.axis_index("res") % 2
    heads = coupling_logit_matrix.shape[1]
    width = query_key_matrix.shape[1] // (4 * heads)
    per_device = chain_tally // count
    tensor_depth = tensor_average_matrix.shape[1] // 2
    half = total_res // 2

    fits = (
        pair_width == 128
        and pair_width % (8 * count) == 0
        and count & (count - 1) == 0
        and total_res == 128
        and local_strands == 8
        and per_device == 8
        and heads == 8
        and heads * width == depth
        and depth % 128 == 0
        and tensor_depth == 32
    )
    if fits:
        prepared = prepare_call(
            trilateral_entry_matrix,
            tensor_average_matrix,
            query_key_matrix,
            focus_final_matrix,
        )
        packed = pack_call(alignment_embedding, coupling_embedding, coupling_logit_matrix, count)
        arrived = exchange(packed)
        other = across(arrived[:, -1], 1)
        projected = project_call(arrived, prepared[3])
        mixed, flanks = attend_call(arrived, other, projected, width, prepared[4], *prepared[1:3])
        flanks = exchange(flanks)
        flanks = flanks.reshape(chain_tally, -1)
        other = across(flanks, 1)
        final = spread_call(tensor_average_final)
        return pair_track(
            core.reshape(1),
            flanks,
            other,
            mixed,
            coupling_embedding,
            final,
            prepared,
            trilateral_exit_matrix,
            local_strands * tensor_depth,
        )

    rows = exchange(alignment_embedding).reshape(count, per_device, local_strands, depth)
    rows = rows.transpose(1, 0, 2, 3).reshape(per_device, total_res, depth)
    pair_norm = standardise_entries(coupling_embedding, -1).astype(jnp.bfloat16)
    bias_rows = jnp.einsum(
        "rnc,ch->hrn", pair_norm, coupling_logit_matrix, preferred_element_type=jnp.float32
    )
    bias = lax.all_gather(bias_rows, "res", axis=1, tiled=True)

    standard = standardise_entries(rows, -1).astype(jnp.bfloat16)
    projection = query_key_matrix.reshape(depth, 4, heads, width)
    mapped = jnp.einsum(
        "snc,cthd->tshnd", standard, projection[:, :3], preferred_element_type=jnp.float32
    ).astype(jnp.bfloat16)
    gate = jax.nn.sigmoid(
        jnp.einsum("snc,chd->shnd", standard, projection[:, 3], preferred_element_type=jnp.float32)
    )
    scores = (
        jnp.einsum("shid,shjd->shij", mapped[0], mapped[1], preferred_element_type=jnp.float32)
        * width ** (-0.5)
        + bias
    )
    weights = jnp.exp(scores - jnp.max(scores, axis=-1, keepdims=True))
    weights = (weights / jnp.sum(weights, axis=-1, keepdims=True)).astype(jnp.bfloat16)
    attended = jnp.einsum(
        "shij,shjd->shid", weights, mapped[2], preferred_element_type=jnp.float32
    ).astype(jnp.bfloat16)
    gated = (attended.astype(jnp.float32) * gate).astype(jnp.bfloat16)
    increment = jnp.einsum(
        "shnd,hdc->snc",
        gated,
        focus_final_matrix.reshape(heads, width, depth),
        preferred_element_type=jnp.float32,
    )
    mixed = (rows.astype(jnp.float32) + increment).astype(jnp.bfloat16)

    tensor_scaled = standardise_entries(mixed, -1).astype(jnp.bfloat16)
    flank = jnp.einsum(
        "snc,ctk->tsnk",
        tensor_scaled,
        tensor_average_matrix.reshape(depth, 2, tensor_depth),
        preferred_element_type=jnp.float32,
    ).astype(jnp.bfloat16)
    left = flank[0].reshape(per_device, count // 2, 2, local_strands * tensor_depth)
    left = left.transpose(1, 2, 0, 3)
    right = flank[1].reshape(per_device, 2, half // 8, 8, tensor_depth).transpose(1, 0, 2, 4, 3)
    right = right.reshape(2, per_device, tensor_depth * half)
    right = jnp.broadcast_to(right, (count // 2,) + right.shape)
    flanks = jnp.concatenate([left, right], axis=-1).reshape(count, per_device, -1)
    flanks = exchange(flanks)
    mixed_out = exchange(
        mixed.reshape(per_device, count, local_strands, depth).transpose(1, 0, 2, 3)
    ).reshape(chain_tally, local_strands, depth)

    flanks = flanks.reshape(chain_tally, -1)
    mine = flanks[:, local_strands * tensor_depth :]
    other = across(mine, 1)
    group = max(1, 128 // tensor_depth)
    final = tensor_average_final.reshape(tensor_depth, tensor_depth, pair_width)
    final = jnp.einsum("ab,cef->eacbf", jnp.eye(group, dtype=final.dtype), final)
    final = final.reshape(tensor_depth * group * tensor_depth, group * pair_width)
    left_all = flanks[:, : local_strands * tensor_depth]
    both = jnp.stack([mine, other])
    both = jnp.where(core == 0, both, both[::-1])
    both = both.reshape(2, chain_tally, half // 8, tensor_depth, 8)
    outer = jnp.einsum(
        "xsaej,sgm->gxajem",
        both,
        left_all.reshape(chain_tally, local_strands // group, group * tensor_depth),
        preferred_element_type=jnp.float32,
    ) * (1.0 / chain_tally)
    outer = outer.astype(jnp.bfloat16).reshape(local_strands // group, total_res, -1)
    opm = jnp.einsum("gjk,kn->gjn", outer, final, preferred_element_type=jnp.float32)
    opm = opm.reshape(local_strands // group, total_res, group, pair_width)
    opm = opm.transpose(0, 2, 1, 3).reshape(local_strands, total_res, pair_width)
    pair_mid = (coupling_embedding.astype(jnp.float32) + opm).astype(jnp.bfloat16)

    pair_tri = triangle(
        pair_mid, trilateral_entry_matrix[0], trilateral_exit_matrix[0], "xcik,ycjk->cxiyj"
    )
    coupling_refreshed = triangle(
        pair_tri, trilateral_entry_matrix[1], trilateral_exit_matrix[1], "xcki,xckj->cij"
    )
    return (mixed_out, coupling_refreshed)


def solution(mesh):
    return jax.shard_map(
        body,
        mesh=mesh,
        in_specs=(P("grp", "res", None), P("res", "grp", None), P(), P(), P(), P(), P(), P(), P()),
        out_specs=(P("grp", "res", None), P("res", "grp", None)),
        check_vma=False,
    )
```
